512 devices in a mesh: grp: 32 (over z, x), sub: 16 (over y, core).
Axes of the slice: x: 4, y: 8, z: 8, core: 2. Of those that a mesh axis runs over, the one named last changes fastest.
Arguments:
- field: float32 [2048, 2, 16, 256], P(('grp', 'sub')), may hold values from -6 to 6
- source: float32 [2048, 2, 16, 256], P(('grp', 'sub')), may hold values from -6 to 6
- patch_of_slot: int32 [2048], P(('grp', 'sub')), may hold values from -1 to 47, as said below
- neighbour: int32 [2048, 6], P(('grp', 'sub')), may hold values from -1 to 63, as said below
- wave_index: int32 [2048], P(('grp', 'sub')), may hold values from 0 to 15
- wave_table: float32 [16], replicated, may hold values from 0.02 to 0.2
Outputs:
- corrected: float32 [2048, 2, 16, 256], P(('grp', 'sub'))
The draws below stay inside these ranges and needn't reach their ends.
Inputs may be any that keep to these rules, and one draw needn't show every extreme that they name: `patch_of_slot`: in each slab every patch 0 to 47 is held by exactly one slot; each device holds 2 to 4 patches in its first slots, the rest -1; in every slab some device holds 4 and some 2. `neighbour`: consistent with patch_of_slot and the slab grid: -1 exactly for empty slots, for faces on the grid's boundary.
All inputs are finite; a program needn't handle non-finite values.
Results may differ from the reference program's by a relative error of at most 0.0003.
Values sent between devices are 32-bit elements; how exact they have to be, the bound alone decides.
No kernel may reach another device: no remote copies, remote signals or barrier semaphores. Data moves between devices by JAX's collectives and lax.ppermute only.
A program may use at most 64 MiB of HBM per device.

```python
import math
import jax
import jax.numpy as jnp
from jax import lax

C = 16
P_DEV = 4
PZ = 4
NK = 16
CITER = 3
PY = 12
PPS = 48
GS = 64
SLOTS = 2048
N_GRP = 32
N_SUB = 16


def group_layout(group_key):
    key_delta, key_pick, key_sign, key_order = jax.random.split(group_key, 4)
    pair_count = N_SUB // 2
    shift_delta = jax.random.randint(key_delta, (pair_count,), -1, 2)
    picked_pair = jax.random.randint(key_pick, (), 0, pair_count)
    signed_step = jax.random.randint(key_sign, (), 0, 2) * 2 - 1
    shift_delta = jnp.where(jnp.arange(pair_count) == picked_pair, signed_step, shift_delta)
    slot_counts = jnp.stack([3 + shift_delta, 3 - shift_delta], 1).reshape(N_SUB)
    slot_starts = jnp.cumsum(slot_counts) - slot_counts
    patch_order = jax.random.permutation(key_order, PPS)
    slot_position = jnp.arange(P_DEV)
    slot_index = slot_starts[:, None] + slot_position[None, :]
    live_slots = slot_position[None, :] < slot_counts[:, None]
    chosen_patch = patch_order[jnp.clip(slot_index, 0, PPS - 1)]
    return jnp.where(live_slots, chosen_patch, -1).reshape(GS).astype(jnp.int32)


def arrangement(key):
    base_key = jax.random.fold_in(key, 11)
    group_keys = jax.random.split(base_key, N_GRP)
    return jax.vmap(group_layout)(group_keys)


def draw_patch_of_slot(key, part):
    return arrangement(key).reshape(SLOTS)


def draw_neighbour(key, part):
    patches = arrangement(key)
    live_slots = patches >= 0
    target = jnp.where(live_slots, patches, PPS)
    slot_numbers = jnp.broadcast_to(jnp.arange(GS, dtype=jnp.int32), patches.shape)
    group_rows = jnp.arange(N_GRP)[:, None]
    inverse = jnp.zeros((N_GRP, PPS + 1), jnp.int32).at[group_rows, target].set(slot_numbers)[:, :PPS]
    safe_patch = jnp.where(live_slots, patches, 0)
    row_y = safe_patch // PZ
    col_z = safe_patch % PZ

    def lookup(group_index, patch_index, allowed):
        group_safe = jnp.clip(group_index, 0, N_GRP - 1)
        found = inverse[group_safe, jnp.clip(patch_index, 0, PPS - 1)]
        return jnp.where(allowed & live_slots, found, -1)
    group_full = jnp.broadcast_to(group_rows, patches.shape)
    lower_x = lookup(group_full - 1, safe_patch, group_full > 0)
    upper_x = lookup(group_full + 1, safe_patch, group_full < N_GRP - 1)
    lower_y = lookup(group_full, safe_patch - PZ, row_y > 0)
    upper_y = lookup(group_full, safe_patch + PZ, row_y < PY - 1)
    lower_z = lookup(group_full, safe_patch - 1, col_z > 0)
    upper_z = lookup(group_full, safe_patch + 1, col_z < PZ - 1)
    links = jnp.stack([lower_x, upper_x, lower_y, upper_y, lower_z, upper_z], -1)
    return links.reshape(SLOTS, 6).astype(jnp.int32)


def with_ends(values, own_key, smallest, high):
    index_at = [jax.random.randint(jax.random.fold_in(own_key, axis), (), 0, length) for axis, length in enumerate(values.shape)]
    main_axis = values.shape.index(max(values.shape))
    beside = index_at[:main_axis] + [(index_at[main_axis] + 1) % values.shape[main_axis]] + index_at[main_axis + 1:]
    return values.at[tuple(index_at)].set(smallest).at[tuple(beside)].set(high)


def block_scale(stream_key, shape, cuts, least, high):
    gain, own = 1.0, jax.random.fold_in(stream_key, 6)
    for position, parts in cuts:
        steps = jnp.exp(jax.random.uniform(jax.random.fold_in(own, position), (parts,), jnp.float32, least / len(cuts), high / len(cuts)))
        gain = gain * jnp.repeat(steps, shape[position] // parts).reshape([-1 if axis == position else 1 for axis in range(len(shape))])
    return gain


def gaussian(stream_key, extent, scale, bound, cuts=(), kind=jnp.bfloat16):
    loudness = block_scale(stream_key, extent, cuts, -0.22, 0.18) if cuts else 1.0
    drawn = jax.random.normal(stream_key, extent, jnp.float32) * scale * loudness
    return jnp.minimum(jnp.maximum(drawn, -bound), bound).astype(kind)


def setup_inputs(seed: int = 0) -> dict:
    key_of = jax.random.split(jax.random.key(seed), 7)
    return {
        "field": gaussian(key_of[0], (SLOTS, 2, C, C * C), 1.0, 6.0, ((0, 512),), jnp.float32),
        "source": gaussian(key_of[1], (SLOTS, 2, C, C * C), 1.0, 6.0, ((0, 512),), jnp.float32),
        "patch_of_slot": draw_patch_of_slot(jax.random.fold_in(key_of[6], 71), 0),
        "neighbour": draw_neighbour(jax.random.fold_in(key_of[6], 71), 0),
        "wave_index": with_ends(jax.random.randint(key_of[4], (SLOTS,), 0, NK), jax.random.fold_in(key_of[4], 1), 0, NK - 1).astype(jnp.int32),
        "wave_table": jnp.clip(jnp.exp(jax.random.uniform(key_of[5], (NK,), jnp.float32, math.log(0.02), math.log(0.2))), 0.02, 0.2),
    }


omega_fine = 0.7
omega_coarse = 0.6
shift_imag = 0.5


def faces_of(cubes):
    slot_count = cubes.shape[0]
    edge = cubes.shape[2]
    layers = [cubes[:, :, 0], cubes[:, :, -1], cubes[:, :, :, 0], cubes[:, :, :, -1], cubes[:, :, :, :, 0], cubes[:, :, :, :, -1]]
    return jnp.stack([layer.reshape(slot_count, 2, edge * edge) for layer in layers], 1)


def neighbour_sum(cubes, ghosts):
    slot_count = cubes.shape[0]
    edge = cubes.shape[2]
    ghost_sheets = ghosts.reshape(slot_count, 6, 2, edge, edge)
    total = jnp.concatenate([ghost_sheets[:, 0][:, :, None], cubes[:, :, :-1]], 2)
    total = total + jnp.concatenate([cubes[:, :, 1:], ghost_sheets[:, 1][:, :, None]], 2)
    total = total + jnp.concatenate([ghost_sheets[:, 2][:, :, :, None], cubes[:, :, :, :-1]], 3)
    total = total + jnp.concatenate([cubes[:, :, :, 1:], ghost_sheets[:, 3][:, :, :, None]], 3)
    total = total + jnp.concatenate([ghost_sheets[:, 4][..., None], cubes[..., :-1]], 4)
    total = total + jnp.concatenate([cubes[..., 1:], ghost_sheets[:, 5][..., None]], 4)
    return total


def residual_of(cubes, rights, ghosts, wave_sq):
    beside_all = neighbour_sum(cubes, ghosts)
    scale = wave_sq[:, None, None, None]
    real_part = cubes[:, 0]
    imag_part = cubes[:, 1]
    apply_real = 6.0 * real_part - beside_all[:, 0] - scale * (real_part - shift_imag * imag_part)
    apply_imag = 6.0 * imag_part - beside_all[:, 1] - scale * (imag_part + shift_imag * real_part)
    return jnp.stack([rights[:, 0] - apply_real, rights[:, 1] - apply_imag], 1)


def divide_diag(values, real_diag, imag_diag, channel_axis):
    denom = real_diag * real_diag + imag_diag * imag_diag
    first = jnp.take(values, 0, axis=channel_axis)
    second = jnp.take(values, 1, axis=channel_axis)
    out_real = (first * real_diag - second * imag_diag) / denom
    out_imag = (first * imag_diag + second * real_diag) / denom
    return jnp.stack([out_real, out_imag], channel_axis)


def smooth_step(cubes, resid, wave_sq):
    scale = wave_sq[:, None, None, None]
    step_value = divide_diag(resid, 6.0 - scale, shift_imag * scale, 1)
    return cubes + omega_fine * step_value


def restrict(resid):
    slot_count = resid.shape[0]
    edge = resid.shape[2]
    small = edge // 4
    blocks = resid.reshape(slot_count, 2, small, 4, small, 4, small, 4)
    return jnp.mean(blocks, axis=(3, 5, 7)).reshape(slot_count, 2 * small * small * small)


def coarse_residual(padded_x, coarse_rhs, coarse_wave):
    current = padded_x[:, 1:-1]
    beside_all = padded_x[:, :-2] + padded_x[:, 2:]
    ypad = jnp.pad(current, ((0, 0), (0, 0), (1, 1), (0, 0)))
    beside_all = beside_all + ypad[:, :, :-2] + ypad[:, :, 2:]
    zpad = jnp.pad(current, ((0, 0), (0, 0), (0, 0), (1, 1)))
    beside_all = beside_all + zpad[..., :-2] + zpad[..., 2:]
    real_part = current[0]
    imag_part = current[1]
    apply_real = (6.0 * real_part - beside_all[0]) / 16.0 - coarse_wave * (real_part - shift_imag * imag_part)
    apply_imag = (6.0 * imag_part - beside_all[1]) / 16.0 - coarse_wave * (imag_part + shift_imag * real_part)
    return jnp.stack([coarse_rhs[0] - apply_real, coarse_rhs[1] - apply_imag], 0)


def coarse_divide(values, coarse_wave):
    return divide_diag(values, 6.0 / 16.0 - coarse_wave, shift_imag * coarse_wave, 0)


def all_ghosts(cubes_all, links):
    groups = cubes_all.shape[0]
    per_group = cubes_all.shape[1]
    edge = cubes_all.shape[3]
    faces = faces_of(cubes_all.reshape((groups * per_group,) + cubes_all.shape[2:])).reshape(groups, per_group, 6, 2, edge * edge)
    blank = jnp.zeros_like(faces[:1, :, 0])
    lower = jnp.concatenate([blank, faces[:-1, :, 1]], 0)
    upper = jnp.concatenate([faces[1:, :, 0], blank], 0)
    candidate = jnp.concatenate([lower[:, :, None], upper[:, :, None], faces[:, :, 3:4], faces[:, :, 2:3], faces[:, :, 5:6], faces[:, :, 4:5]], 2)
    safe_links = jnp.maximum(links, 0)
    picked = candidate[jnp.arange(groups)[:, None, None], safe_links, jnp.arange(6)[None, None, :]]
    return jnp.where((links >= 0)[..., None, None], picked, 0.0)


def reference(field, source, patch_of_slot, neighbour, wave_index, wave_table):
    groups = N_GRP
    per_group = N_SUB * P_DEV
    edge = C
    small = edge // 4
    rows_y = PY
    patch_total = PPS
    cubes = field.reshape(groups, per_group, 2, edge, edge, edge)
    rights = source.reshape(groups, per_group, 2, edge, edge, edge)
    links = neighbour.reshape(groups, per_group, 6)
    wave_sq = wave_table[wave_index].reshape(groups, per_group)
    patch_ids = patch_of_slot.reshape(groups, per_group)

    def sweep_group(items):
        cube_g, right_g, ghost_g, wave_g = items
        return smooth_step(cube_g, residual_of(cube_g, right_g, ghost_g, wave_g), wave_g)

    for sweep_index in range(2):
        ghosts = all_ghosts(cubes, links)
        cubes = lax.map(sweep_group, (cubes, rights, ghosts, wave_sq))
    ghosts = all_ghosts(cubes, links)

    def restrict_group(items):
        cube_g, right_g, ghost_g, wave_g = items
        return restrict(residual_of(cube_g, right_g, ghost_g, wave_g))

    coarse_rows = lax.map(restrict_group, (cubes, rights, ghosts, wave_sq))

    def slab_group(items):
        rows_g, wave_g, ids_g = items
        selector = (ids_g[None, :] == jnp.arange(patch_total)[:, None]).astype(jnp.float32)
        placed = jnp.dot(selector, rows_g, precision=lax.Precision.HIGHEST)
        placed_wave = jnp.dot(selector, wave_g[:, None], precision=lax.Precision.HIGHEST)[:, 0]
        slab = placed.reshape(rows_y, PZ, 2, small, small, small).transpose(2, 3, 0, 4, 1, 5).reshape(2, small, rows_y * small, PZ * small)
        wave_grid = jnp.repeat(jnp.repeat(placed_wave.reshape(rows_y, PZ), small, 0), small, 1)
        return slab, wave_grid

    slabs, wave_grids = lax.map(slab_group, (coarse_rows, wave_sq, patch_ids))
    coarse_rhs = slabs.transpose(1, 0, 2, 3, 4).reshape(2, groups * small, rows_y * small, PZ * small)
    coarse_wave = jnp.repeat(wave_grids, small, 0)
    correction = omega_coarse * coarse_divide(coarse_rhs, coarse_wave)
    for sweep_index in range(CITER - 1):
        padded = jnp.pad(correction, ((0, 0), (1, 1), (0, 0), (0, 0)))
        correction = correction + omega_coarse * coarse_divide(coarse_residual(padded, coarse_rhs, coarse_wave), coarse_wave)
    patch_blocks = correction.reshape(2, groups, small, rows_y, small, PZ, small).transpose(1, 3, 5, 0, 2, 4, 6).reshape(groups, patch_total, 2, small, small, small)

    def prolong_group(items):
        cube_g, blocks_g, ids_g = items
        mine = blocks_g[jnp.maximum(ids_g, 0)]
        count = cube_g.shape[0]
        grown = jnp.broadcast_to(mine[:, :, :, None, :, None, :, None], (count, 2, small, 4, small, 4, small, 4)).reshape(count, 2, edge, edge, edge)
        return jnp.where((ids_g >= 0)[:, None, None, None, None], cube_g + grown, 0.0)

    result = lax.map(prolong_group, (cubes, patch_blocks, patch_ids))
    return result.reshape(groups * per_group, 2, edge, edge * edge)
```

```python
import jax
import jax.numpy as jnp
from jax import lax
from jax.experimental import pallas as pl
from jax.experimental.pallas import tpu as pltpu
from jax.sharding import PartitionSpec as P

PZ = 4
PY = 12
PATCHES = PY * PZ
EDGE = 16
CELLS = EDGE * EDGE
SLOTS = 4
NS = 16
LIVE = NS * SLOTS
LANES = 128

omega_fine = 0.7
omega_coarse = 0.6
shift_imag = 0.5

HI = lax.Precision.HIGHEST
F32 = jnp.float32
VM = pl.BlockSpec(memory_space=pltpu.VMEM)
SM = pl.BlockSpec(memory_space=pltpu.SMEM)


def call(body, outs, ins, scratch=()):
    return pl.pallas_call(
        body,
        out_shape=[jax.ShapeDtypeStruct(shape, F32) for shape in outs],
        in_specs=[SM if a.dtype == jnp.int32 or a.ndim == 1 else VM for a in ins],
        out_specs=[VM] * len(outs),
        scratch_shapes=[pltpu.VMEM(shape, F32) for shape in scratch],
    )(*ins)


def iota(shape, dim):
    return lax.broadcasted_iota(jnp.int32, shape, dim)


def lane_roll(x, shift):
    return pltpu.roll(x, shift % x.shape[1], 1)


def row_roll(x, shift):
    return pltpu.roll(x, shift % x.shape[0], 0)


def in_plane(u):
    shape = u[0].shape
    lane = iota(shape, 1)
    patch = iota(shape, 0)
    k = lane % EDGE
    col = patch % PZ
    not_last, not_first = k < EDGE - 1, k > 0
    has_next, has_prev = col < PZ - 1, col > 0
    out = []
    ahead = [lane_roll(t, -EDGE) for t in u]
    behind = [lane_roll(t, EDGE) for t in u]
    low, high = lane >= EDGE, lane < LANES - EDGE
    y_next = [
        jnp.where(high, ahead[0], ahead[1]),
        jnp.where(high, ahead[1], jnp.where(patch < PATCHES - PZ, row_roll(ahead[0], -PZ), 0.0)),
    ]
    y_prev = [
        jnp.where(low, behind[0], jnp.where(patch >= PZ, row_roll(behind[1], PZ), 0.0)),
        jnp.where(low, behind[1], behind[0]),
    ]
    for h in range(2):
        t = u[h]
        z_next = jnp.where(
            not_last,
            lane_roll(t, -1),
            jnp.where(has_next, row_roll(lane_roll(t, EDGE - 1), -1), 0.0),
        )
        z_prev = jnp.where(
            not_first,
            lane_roll(t, 1),
            jnp.where(has_prev, row_roll(lane_roll(t, 1 - EDGE), 1), 0.0),
        )
        out.append((z_next + z_prev) + (y_next[h] + y_prev[h]))
    return out


def halves(ref, index):
    return [ref[index, :, :LANES], ref[index, :, LANES:]]


def put(ref, index, pair):
    ref[index, :, :LANES] = pair[0]
    ref[index, :, LANES:] = pair[1]


def field_of(ref, first):
    return [halves(ref, first), halves(ref, first + 1)]


def choose(flag, a, b):
    return [[jnp.where(flag, x, y) for x, y in zip(p, q)] for p, q in zip(a, b)]


def around(u, before, after):
    return [
        [n + (x + y) for n, x, y in zip(in_plane(u[part]), before[part], after[part])]
        for part in range(2)
    ]


def diagonal(wave):
    real, imag = 6.0 - wave, shift_imag * wave
    return real, imag


def smooth(u, total, rights, wave):
    real, imag = diagonal(wave)
    scale = omega_fine / (real * real + imag * imag)
    real, imag = real * scale, imag * scale
    keep = 1.0 - omega_fine
    out_re, out_im = [], []
    for h in range(2):
        a = rights[0][h] + total[0][h]
        b = rights[1][h] + total[1][h]
        out_re.append(keep * u[0][h] + (a * real - b * imag))
        out_im.append(keep * u[1][h] + (a * imag + b * real))
    return [out_re, out_im]


def residual(u, total, rights, wave):
    real, imag = diagonal(wave)
    out_re, out_im = [], []
    for h in range(2):
        out_re.append(rights[0][h] + total[0][h] - (real * u[0][h] + imag * u[1][h]))
        out_im.append(rights[1][h] + total[1][h] - (real * u[1][h] - imag * u[0][h]))
    return [out_re, out_im]


def position():
    return lax.axis_index("grp"), lax.axis_index("sub")


def low_side_open(g):
    last = lax.axis_size("grp") - 1
    beyond = jnp.where(g % 2 == 0, g - 1, g + 1)
    return (beyond >= 0) & (beyond <= last)


def pack_body(field_ref, source_ref, patch_ref, index_ref, table_ref, out_ref):
    g, _ = position()
    odd = g % 2 == 1
    for q in range(SLOTS):
        patch = jnp.full((1, LANES), patch_ref[q].astype(F32), F32)
        wave = jnp.full((1, LANES), table_ref[index_ref[q]], F32)
        for s in range(NS):
            out_ref[s, 10 * q + 8 : 10 * q + 9, :] = patch
            out_ref[s, 10 * q + 9 : 10 * q + 10, :] = wave
    for s in range(NS):
        layer = jnp.where(odd, EDGE - 1 - s, s)
        for q in range(SLOTS):
            for a, ref in enumerate((field_ref, source_ref)):
                for part in range(2):
                    row = 10 * q + 4 * a + 2 * part
                    cells = ref[q, part, pl.ds(layer, 1), :]
                    out_ref[s, row : row + 1, :] = cells[:, :LANES]
                    out_ref[s, row + 1 : row + 2, :] = cells[:, LANES:]


def place_body(raw_ref, plane_ref, field_ref, slot_ref):
    patches = raw_ref[pl.ds(8, LIVE, stride=10), :]
    held = (patches == iota((LIVE, LANES), 1).astype(F32)).astype(F32)
    slot_ref[...] = held
    pick = held.T[:PATCHES]
    order = (0, 1, 2, 3, 4, 5, 6, 7, 9)
    rows = jnp.concatenate([raw_ref[pl.ds(c, LIVE, stride=10), :] for c in order], 1)
    placed = jnp.dot(pick, rows, precision=HI, preferred_element_type=F32)
    for c in range(4):
        put(plane_ref, c, [placed[:, 256 * c : 256 * c + 128], placed[:, 256 * c + 128 : 256 * c + 256]])
    for c in range(2):
        put(field_ref, c, [placed[:, 256 * c : 256 * c + 128], placed[:, 256 * c + 128 : 256 * c + 256]])
    put(plane_ref, 4, [placed[:, 1024:], placed[:, 1024:]])


def first_body(own_ref, before_ref, after_ref, far_ref, out_ref):
    _, s = position()
    u = field_of(own_ref, 0)
    v = field_of(far_ref, 0)
    before = choose(s == 0, v, field_of(before_ref, 0))
    after = choose(s == NS - 1, v, field_of(after_ref, 0))
    new = smooth(u, around(u, before, after), field_of(own_ref, 2), own_ref[4, :, :LANES])
    for part in range(2):
        put(out_ref, part, new[part])
        put(out_ref, 2 + part, v[part])


def open_factor():
    g, s = position()
    return jnp.where((s >= NS // 2) | low_side_open(g), 1.0, 0.0)


def second_body(own_ref, far_ref, before_ref, after_ref, mine_ref, slot_ref, out_ref, sent_ref):
    _, s = position()
    first, last = s == 0, s == NS - 1
    u = field_of(own_ref, 0)
    v = field_of(far_ref, 0)
    one = field_of(mine_ref, 0)
    v_before = choose(first, u, field_of(before_ref, 2))
    v_after = choose(last, u, field_of(after_ref, 2))
    v_one = smooth(v, around(v, v_before, v_after), field_of(far_ref, 2), far_ref[4, :, :LANES])
    factor = open_factor()
    v_one = [[x * factor for x in pair] for pair in v_one]
    before = choose(first, v_one, field_of(before_ref, 0))
    after = choose(last, v_one, field_of(after_ref, 0))
    two = smooth(one, around(one, before, after), field_of(own_ref, 2), own_ref[4, :, :LANES])
    for part in range(2):
        put(out_ref, part, two[part])
        put(out_ref, 2 + part, v_one[part])
    rows = jnp.concatenate(two[0] + two[1], 1)
    slots = jnp.dot(slot_ref[:, :PATCHES], rows, precision=HI, preferred_element_type=F32)
    for c in range(4):
        sent_ref[pl.ds(c, LIVE, stride=4), :] = slots[:, LANES * c : LANES * (c + 1)]


def coarse_lane(shape, dim):
    cell = iota(shape, dim)
    part, inside = cell // CELLS, cell % CELLS
    return part * 64 + (inside // (4 * EDGE)) * EDGE + (inside % EDGE) // 4


def restrict_body(own_ref, far_ref, before_ref, after_ref, two_ref, one_ref, out_ref):
    _, s = position()
    first, last = s == 0, s == NS - 1
    one = field_of(one_ref, 0)
    two = field_of(two_ref, 0)
    v_one = field_of(two_ref, 2)
    wave = own_ref[4, :, :LANES]
    v_before = choose(first, one, field_of(before_ref, 2))
    v_after = choose(last, one, field_of(after_ref, 2))
    v_two = smooth(v_one, around(v_one, v_before, v_after), field_of(far_ref, 2), far_ref[4, :, :LANES])
    factor = open_factor()
    v_two = [[x * factor for x in pair] for pair in v_two]
    before = choose(first, v_two, field_of(before_ref, 0))
    after = choose(last, v_two, field_of(after_ref, 0))
    r = residual(two, around(two, before, after), field_of(own_ref, 2), wave)
    rows = jnp.concatenate(r[0] + r[1], 1)
    shape = (2 * CELLS, LANES)
    gather = (coarse_lane(shape, 0) == iota(shape, 1)).astype(F32)
    sums = jnp.dot(rows, gather, precision=HI, preferred_element_type=F32)
    col = iota(sums.shape, 0) % PZ
    spread = jnp.where(col == 0, sums, 0.0)
    for c in range(1, PZ):
        spread = jnp.where(col == c, lane_roll(sums, 4 * c), spread)
    group = (iota((16, PATCHES), 1) // PZ == iota((16, PATCHES), 0)).astype(F32)
    block = jnp.dot(group, spread, precision=HI, preferred_element_type=F32)
    diag = jnp.where(iota(wave.shape, 0) == iota(wave.shape, 1), wave, 0.0)
    wave_row = jnp.sum(diag, 0, keepdims=True)
    out_ref[...] = jnp.where(iota(block.shape, 0) == PY, wave_row, block)


def bundle_body(sent_ref, block_ref, far_ref, out_ref):
    out_ref[:, 0:16, :] = sent_ref[...]
    for d in range(NS):
        out_ref[d, 16:32, :] = block_ref[...]
        out_ref[d, 32:48, :] = far_ref[...]


def coarse_sum(e):
    lane = iota(e.shape, 1)
    z = lane % EDGE
    j = (lane // EDGE) % 4
    z_next = jnp.where(z < EDGE - 1, lane_roll(e, -1), 0.0)
    z_prev = jnp.where(z > 0, lane_roll(e, 1), 0.0)
    y_next = jnp.where(j < 3, lane_roll(e, -EDGE), row_roll(lane_roll(e, 3 * EDGE), -1))
    y_prev = jnp.where(j > 0, lane_roll(e, EDGE), row_roll(lane_roll(e, -3 * EDGE), 1))
    return (z_next + z_prev) + (y_next + y_prev)


def correct_body(raw_ref, patch_ref, out_ref, coarse_ref, smooth_ref):
    g, _ = position()
    odd = g % 2 == 1
    shape = (16, LANES)
    row, lane = iota(shape, 0), iota(shape, 1)
    live = row < PY
    spread = (iota((LANES, LANES), 0) % PZ == (iota((LANES, LANES), 1) % EDGE) // 4).astype(F32)
    sign = jnp.where(lane < 64, -1.0, 1.0)

    def inverse(wave_row):
        own = jnp.where((lane // PZ == row) & live, jnp.broadcast_to(wave_row, shape), 0.0)
        wave = jnp.dot(own, spread, precision=HI, preferred_element_type=F32)
        real, imag = 6.0 / 16.0 - wave, shift_imag * wave
        scale = omega_coarse / (real * real + imag * imag)
        return jnp.where(live, real * scale, 0.0), jnp.where(live, sign * imag * scale, 0.0)

    def divide(x, inv):
        return x * inv[0] + lane_roll(x, 64) * inv[1]

    def total(start, tile):
        parts = [raw_ref[start + i, tile : tile + 16, :] for i in range(4)]
        return ((parts[0] + parts[1]) + (parts[2] + parts[3])) * (1.0 / 64.0)

    inv_own = inverse(raw_ref[0, 16 + PY : 17 + PY, :])
    inv_low = inverse(raw_ref[0, 32 + PY : 33 + PY, :])
    inv_high = inverse(raw_ref[NS - 1, 32 + PY : 33 + PY, :])
    inv = [inv_low, inv_low] + [inv_own] * 4 + [inv_high, inv_high]
    rhs = [total(4, 32), total(0, 32)] + [total(4 * i, 16) for i in range(4)] + [total(12, 32), total(8, 32)]
    e = [divide(x, i) for x, i in zip(rhs, inv)]
    low = jnp.where(low_side_open(g), 1.0, 0.0)
    for margin in (1, 2):
        new = list(e)
        for i in range(margin, 8 - margin):
            beside = coarse_sum(e[i]) + (e[i - 1] + e[i + 1])
            new[i] = (1.0 - omega_coarse) * e[i] + divide(rhs[i] + beside * (1.0 / 16.0), inv[i])
        new[1] = new[1] * low
        e = new
    for i in range(4):
        coarse_ref[i] = e[2 + i]
    grown = []
    for q in range(SLOTS):
        patch = jnp.maximum(patch_ref[q], 0)
        rows = []
        for i in range(4):
            plane = jnp.where(odd, 3 - i, i)
            one = coarse_ref[plane, pl.ds(patch // PZ, 1), :]
            rows.append(jnp.broadcast_to(one, (4, LANES)))
        grown.append(pltpu.roll(jnp.concatenate(rows, 0), LANES - 4 * (patch % PZ), 1))
    grown = jnp.concatenate(grown, 0)
    wide = (LANES, 2 * CELLS)
    widen = (coarse_lane(wide, 1) == iota(wide, 0)).astype(F32)
    grown = jnp.dot(grown, widen, precision=HI, preferred_element_type=F32)
    for i in range(EDGE):
        s = jnp.where(odd, EDGE - 1 - i, i)
        for q in range(SLOTS):
            for part in range(2):
                for h in range(2):
                    c = 4 * q + 2 * part + h
                    smooth_ref[2 * q + part, i : i + 1, LANES * h : LANES * (h + 1)] = raw_ref[s, c : c + 1, :]
    for q in range(SLOTS):
        held = patch_ref[q] >= 0
        for part in range(2):
            extra = grown[EDGE * q : EDGE * (q + 1), CELLS * part : CELLS * (part + 1)]
            out_ref[q, part] = jnp.where(held, smooth_ref[2 * q + part] + extra, 0.0)


def swap_pairs(groups, subs):
    pairs = []
    for s in subs:
        for g in range(0 if s >= NS // 2 else 1, groups - 1, 2):
            a, b = g * NS + s, (g + 1) * NS + s
            pairs += [(a, b), (b, a)]
    return pairs


def body(field, source, patch_of_slot, neighbour, wave_index, wave_table):
    groups = lax.axis_size("grp")
    both = ("grp", "sub")
    up = [(i, (i + 1) % NS) for i in range(NS)]
    down = [((i + 1) % NS, i) for i in range(NS)]
    ring = lambda x: (lax.ppermute(x, "sub", up), lax.ppermute(x, "sub", down))
    plane = (PATCHES, CELLS)

    (packed,) = call(pack_body, [(NS, 40, LANES)], [field, source, patch_of_slot, wave_index, wave_table])
    raw = lax.all_to_all(packed, "sub", 0, 0, tiled=True).reshape(NS * 40, LANES)
    own, start, slot = call(place_body, [(5,) + plane, (2,) + plane, (LIVE, LANES)], [raw])
    far = lax.ppermute(own, both, swap_pairs(groups, (0, 1, 2, 13, 14, 15)))
    before, after = ring(start)
    (one,) = call(first_body, [(4,) + plane], [own, before, after, far])
    before, after = ring(one)
    two, sent = call(
        second_body, [(4,) + plane, (4 * LIVE, LANES)], [own, far, before, after, one, slot]
    )
    before, after = ring(two)
    (block,) = call(restrict_body, [(16, LANES)], [own, far, before, after, two, one])
    far_block = lax.ppermute(block, both, swap_pairs(groups, range(NS)))
    (bundle,) = call(bundle_body, [(NS, 48, LANES)], [sent.reshape(NS, 16, LANES), block, far_block])
    back = lax.all_to_all(bundle, "sub", 0, 0, tiled=True)
    (out,) = call(
        correct_body,
        [(SLOTS, 2, EDGE, CELLS)],
        [back, patch_of_slot],
        [(4, 16, LANES), (2 * SLOTS, EDGE, CELLS)],
    )
    return out


def solution(mesh):
    return jax.shard_map(
        body,
        mesh=mesh,
        in_specs=(
            P(("grp", "sub"), None, None, None),
            P(("grp", "sub"), None, None, None),
            P(("grp", "sub")),
            P(("grp", "sub"), None),
            P(("grp", "sub")),
            P(),
        ),
        out_specs=P(("grp", "sub"), None, None, None),
        check_vma=False,
    )
```

```python
import jax
import jax.numpy as jnp
from jax import lax
from jax.experimental import pallas as pl
from jax.experimental.pallas import tpu as pltpu
from jax.sharding import PartitionSpec as P

PZ = 4
PY = 12
PATCHES = PY * PZ
EDGE = 16
CELLS = EDGE * EDGE
SLOTS = 4
NS = 16
LIVE = NS * SLOTS
LANES = 128

omega_fine = 0.7
omega_coarse = 0.6
shift_imag = 0.5

HI = lax.Precision.HIGHEST
F32 = jnp.float32
VM = pl.BlockSpec(memory_space=pltpu.VMEM)
SM = pl.BlockSpec(memory_space=pltpu.SMEM)


def call(body, outs, ins, scratch=()):
    return pl.pallas_call(
        body,
        out_shape=[jax.ShapeDtypeStruct(shape, F32) for shape in outs],
        in_specs=[SM if a.dtype == jnp.int32 or a.ndim == 1 else VM for a in ins],
        out_specs=[VM] * len(outs),
        scratch_shapes=[pltpu.VMEM(shape, F32) for shape in scratch],
        compiler_params=pltpu.CompilerParams(vmem_limit_bytes=16 << 20),
    )(*ins)


def iota(shape, dim):
    return lax.broadcasted_iota(jnp.int32, shape, dim)


def lane_roll(x, shift):
    return pltpu.roll(x, shift % x.shape[1], 1)


def row_roll(x, shift):
    return pltpu.roll(x, shift % x.shape[0], 0)


def in_plane(u):
    shape = u[0].shape
    lane = iota(shape, 1)
    patch = iota(shape, 0)
    k = lane % EDGE
    col = patch % PZ
    not_last, not_first = k < EDGE - 1, k > 0
    has_next, has_prev = col < PZ - 1, col > 0
    out = []
    ahead = [lane_roll(t, -EDGE) for t in u]
    behind = [lane_roll(t, EDGE) for t in u]
    low, high = lane >= EDGE, lane < LANES - EDGE
    y_next = [
        jnp.where(high, ahead[0], ahead[1]),
        jnp.where(high, ahead[1], jnp.where(patch < PATCHES - PZ, row_roll(ahead[0], -PZ), 0.0)),
    ]
    y_prev = [
        jnp.where(low, behind[0], jnp.where(patch >= PZ, row_roll(behind[1], PZ), 0.0)),
        jnp.where(low, behind[1], behind[0]),
    ]
    for h in range(2):
        t = u[h]
        z_next = jnp.where(
            not_last,
            lane_roll(t, -1),
            jnp.where(has_next, row_roll(lane_roll(t, EDGE - 1), -1), 0.0),
        )
        z_prev = jnp.where(
            not_first,
            lane_roll(t, 1),
            jnp.where(has_prev, row_roll(lane_roll(t, 1 - EDGE), 1), 0.0),
        )
        out.append((z_next + z_prev) + (y_next[h] + y_prev[h]))
    return out


def halves(ref, index):
    return [ref[index, :, :LANES], ref[index, :, LANES:]]


def put(ref, index, pair):
    ref[index, :, :LANES] = pair[0]
    ref[index, :, LANES:] = pair[1]


def field_of(ref, first):
    return [halves(ref, first), halves(ref, first + 1)]


def choose(flag, a, b):
    return [[jnp.where(flag, x, y) for x, y in zip(p, q)] for p, q in zip(a, b)]


def around(u, before, after):
    return [
        [n + (x + y) for n, x, y in zip(in_plane(u[part]), before[part], after[part])]
        for part in range(2)
    ]


def diagonal(wave):
    real, imag = 6.0 - wave, shift_imag * wave
    return real, imag


def smooth(u, total, rights, wave):
    real, imag = diagonal(wave)
    scale = omega_fine / (real * real + imag * imag)
    real, imag = real * scale, imag * scale
    keep = 1.0 - omega_fine
    out_re, out_im = [], []
    for h in range(2):
        a = rights[0][h] + total[0][h]
        b = rights[1][h] + total[1][h]
        out_re.append(keep * u[0][h] + (a * real - b * imag))
        out_im.append(keep * u[1][h] + (a * imag + b * real))
    return [out_re, out_im]


def residual(u, total, rights, wave):
    real, imag = diagonal(wave)
    out_re, out_im = [], []
    for h in range(2):
        out_re.append(rights[0][h] + total[0][h] - (real * u[0][h] + imag * u[1][h]))
        out_im.append(rights[1][h] + total[1][h] - (real * u[1][h] - imag * u[0][h]))
    return [out_re, out_im]


def position():
    return lax.axis_index("grp"), lax.axis_index("sub")


def low_side_open(g):
    last = lax.axis_size("grp") - 1
    beyond = jnp.where(g % 2 == 0, g - 1, g + 1)
    return (beyond >= 0) & (beyond <= last)


def pack_body(field_ref, source_ref, patch_ref, index_ref, table_ref, out_ref):
    g, _ = position()
    odd = g % 2 == 1
    for q in range(SLOTS):
        patch = jnp.full((1, LANES), patch_ref[q].astype(F32), F32)
        wave = jnp.full((1, LANES), table_ref[index_ref[q]], F32)
        for s in range(NS):
            out_ref[s, 10 * q + 8 : 10 * q + 9, :] = patch
            out_ref[s, 10 * q + 9 : 10 * q + 10, :] = wave
    for s in range(NS):
        layer = jnp.where(odd, EDGE - 1 - s, s)
        for q in range(SLOTS):
            for a, ref in enumerate((field_ref, source_ref)):
                for part in range(2):
                    row = 10 * q + 4 * a + 2 * part
                    cells = ref[q, part, pl.ds(layer, 1), :]
                    out_ref[s, row : row + 1, :] = cells[:, :LANES]
                    out_ref[s, row + 1 : row + 2, :] = cells[:, LANES:]


def place_body(raw_ref, plane_ref, field_ref, slot_ref):
    patches = raw_ref[pl.ds(8, LIVE, stride=10), :]
    held = (patches == iota((LIVE, LANES), 1).astype(F32)).astype(F32)
    slot_ref[...] = held
    pick = held.T[:PATCHES]
    order = (0, 1, 2, 3, 4, 5, 6, 7, 9)
    rows = jnp.concatenate([raw_ref[pl.ds(c, LIVE, stride=10), :] for c in order], 1)
    placed = jnp.dot(pick, rows, precision=HI, preferred_element_type=F32)
    for c in range(4):
        put(plane_ref, c, [placed[:, 256 * c : 256 * c + 128], placed[:, 256 * c + 128 : 256 * c + 256]])
    for c in range(2):
        put(field_ref, c, [placed[:, 256 * c : 256 * c + 128], placed[:, 256 * c + 128 : 256 * c + 256]])
    put(plane_ref, 4, [placed[:, 1024:], placed[:, 1024:]])


def first_body(own_ref, before_ref, after_ref, far_ref, out_ref):
    _, s = position()
    u = field_of(own_ref, 0)
    v = field_of(far_ref, 0)
    before = choose(s == 0, v, field_of(before_ref, 0))
    after = choose(s == NS - 1, v, field_of(after_ref, 0))
    new = smooth(u, around(u, before, after), field_of(own_ref, 2), own_ref[4, :, :LANES])
    for part in range(2):
        put(out_ref, part, new[part])
        put(out_ref, 2 + part, v[part])


def open_factor():
    g, s = position()
    return jnp.where((s >= NS // 2) | low_side_open(g), 1.0, 0.0)


def second_body(own_ref, far_ref, before_ref, after_ref, mine_ref, slot_ref, out_ref, sent_ref):
    _, s = position()
    first, last = s == 0, s == NS - 1
    u = field_of(own_ref, 0)
    v = field_of(far_ref, 0)
    one = field_of(mine_ref, 0)
    v_before = choose(first, u, field_of(before_ref, 2))
    v_after = choose(last, u, field_of(after_ref, 2))
    v_one = smooth(v, around(v, v_before, v_after), field_of(far_ref, 2), far_ref[4, :, :LANES])
    factor = open_factor()
    v_one = [[x * factor for x in pair] for pair in v_one]
    before = choose(first, v_one, field_of(before_ref, 0))
    after = choose(last, v_one, field_of(after_ref, 0))
    two = smooth(one, around(one, before, after), field_of(own_ref, 2), own_ref[4, :, :LANES])
    for part in range(2):
        put(out_ref, part, two[part])
        put(out_ref, 2 + part, v_one[part])
    rows = jnp.concatenate(two[0] + two[1], 1)
    slots = jnp.dot(slot_ref[:, :PATCHES], rows, precision=HI, preferred_element_type=F32)
    for c in range(4):
        sent_ref[pl.ds(c, LIVE, stride=4), :] = slots[:, LANES * c : LANES * (c + 1)]


def coarse_lane(shape, dim):
    cell = iota(shape, dim)
    part, inside = cell // CELLS, cell % CELLS
    return part * 64 + (inside // (4 * EDGE)) * EDGE + (inside % EDGE) // 4


def restrict_body(own_ref, far_ref, before_ref, after_ref, two_ref, one_ref, out_ref):
    _, s = position()
    first, last = s == 0, s == NS - 1
    one = field_of(one_ref, 0)
    two = field_of(two_ref, 0)
    v_one = field_of(two_ref, 2)
    wave = own_ref[4, :, :LANES]
    v_before = choose(first, one, field_of(before_ref, 2))
    v_after = choose(last, one, field_of(after_ref, 2))
    v_two = smooth(v_one, around(v_one, v_before, v_after), field_of(far_ref, 2), far_ref[4, :, :LANES])
    factor = open_factor()
    v_two = [[x * factor for x in pair] for pair in v_two]
    before = choose(first, v_two, field_of(before_ref, 0))
    after = choose(last, v_two, field_of(after_ref, 0))
    r = residual(two, around(two, before, after), field_of(own_ref, 2), wave)
    rows = jnp.concatenate(r[0] + r[1], 1)
    shape = (2 * CELLS, LANES)
    gather = (coarse_lane(shape, 0) == iota(shape, 1)).astype(F32)
    sums = jnp.dot(rows, gather, precision=HI, preferred_element_type=F32)
    col = iota(sums.shape, 0) % PZ
    spread = jnp.where(col == 0, sums, 0.0)
    for c in range(1, PZ):
        spread = jnp.where(col == c, lane_roll(sums, 4 * c), spread)
    group = (iota((16, PATCHES), 1) // PZ == iota((16, PATCHES), 0)).astype(F32)
    block = jnp.dot(group, spread, precision=HI, preferred_element_type=F32)
    diag = jnp.where(iota(wave.shape, 0) == iota(wave.shape, 1), wave, 0.0)
    wave_row = jnp.sum(diag, 0, keepdims=True)
    out_ref[...] = jnp.where(iota(block.shape, 0) == PY, wave_row, block)


def bundle_body(sent_ref, block_ref, far_ref, out_ref):
    out_ref[:, 0:16, :] = sent_ref[...]
    for d in range(NS):
        out_ref[d, 16:32, :] = block_ref[...]
        out_ref[d, 32:48, :] = far_ref[...]


def coarse_sum(e):
    lane = iota(e.shape, 1)
    z = lane % EDGE
    j = (lane // EDGE) % 4
    z_next = jnp.where(z < EDGE - 1, lane_roll(e, -1), 0.0)
    z_prev = jnp.where(z > 0, lane_roll(e, 1), 0.0)
    y_next = jnp.where(j < 3, lane_roll(e, -EDGE), row_roll(lane_roll(e, 3 * EDGE), -1))
    y_prev = jnp.where(j > 0, lane_roll(e, EDGE), row_roll(lane_roll(e, -3 * EDGE), 1))
    return (z_next + z_prev) + (y_next + y_prev)


def correct_body(raw_ref, patch_ref, out_ref, coarse_ref, smooth_ref):
    g, _ = position()
    odd = g % 2 == 1
    shape = (16, LANES)
    row, lane = iota(shape, 0), iota(shape, 1)
    live = row < PY
    spread = (iota((LANES, LANES), 0) % PZ == (iota((LANES, LANES), 1) % EDGE) // 4).astype(F32)
    sign = jnp.where(lane < 64, -1.0, 1.0)

    def inverse(wave_row):
        own = jnp.where((lane // PZ == row) & live, jnp.broadcast_to(wave_row, shape), 0.0)
        wave = jnp.dot(own, spread, precision=HI, preferred_element_type=F32)
        real, imag = 6.0 / 16.0 - wave, shift_imag * wave
        scale = omega_coarse / (real * real + imag * imag)
        return jnp.where(live, real * scale, 0.0), jnp.where(live, sign * imag * scale, 0.0)

    def divide(x, inv):
        return x * inv[0] + lane_roll(x, 64) * inv[1]

    def total(start, tile):
        parts = [raw_ref[start + i, tile : tile + 16, :] for i in range(4)]
        return ((parts[0] + parts[1]) + (parts[2] + parts[3])) * (1.0 / 64.0)

    inv_own = inverse(raw_ref[0, 16 + PY : 17 + PY, :])
    inv_low = inverse(raw_ref[0, 32 + PY : 33 + PY, :])
    inv_high = inverse(raw_ref[NS - 1, 32 + PY : 33 + PY, :])
    inv = [inv_low, inv_low] + [inv_own] * 4 + [inv_high, inv_high]
    rhs = [total(4, 32), total(0, 32)] + [total(4 * i, 16) for i in range(4)] + [total(12, 32), total(8, 32)]
    e = [divide(x, i) for x, i in zip(rhs, inv)]
    low = jnp.where(low_side_open(g), 1.0, 0.0)
    for margin in (1, 2):
        new = list(e)
        for i in range(margin, 8 - margin):
            beside = coarse_sum(e[i]) + (e[i - 1] + e[i + 1])
            new[i] = (1.0 - omega_coarse) * e[i] + divide(rhs[i] + beside * (1.0 / 16.0), inv[i])
        new[1] = new[1] * low
        e = new
    for i in range(4):
        coarse_ref[i] = e[2 + i]
    grown = []
    for q in range(SLOTS):
        patch = jnp.maximum(patch_ref[q], 0)
        rows = []
        for i in range(4):
            plane = jnp.where(odd, 3 - i, i)
            one = coarse_ref[plane, pl.ds(patch // PZ, 1), :]
            rows.append(jnp.broadcast_to(one, (4, LANES)))
        grown.append(pltpu.roll(jnp.concatenate(rows, 0), LANES - 4 * (patch % PZ), 1))
    grown = jnp.concatenate(grown, 0)
    wide = (LANES, 2 * CELLS)
    widen = (coarse_lane(wide, 1) == iota(wide, 0)).astype(F32)
    grown = jnp.dot(grown, widen, precision=HI, preferred_element_type=F32)
    for i in range(EDGE):
        s = jnp.where(odd, EDGE - 1 - i, i)
        for q in range(SLOTS):
            for part in range(2):
                for h in range(2):
                    c = 4 * q + 2 * part + h
                    smooth_ref[2 * q + part, i : i + 1, LANES * h : LANES * (h + 1)] = raw_ref[s, c : c + 1, :]
    for q in range(SLOTS):
        held = patch_ref[q] >= 0
        for part in range(2):
            extra = grown[EDGE * q : EDGE * (q + 1), CELLS * part : CELLS * (part + 1)]
            out_ref[q, part] = jnp.where(held, smooth_ref[2 * q + part] + extra, 0.0)


def swap_pairs(groups, subs):
    pairs = []
    for s in subs:
        for g in range(0 if s >= NS // 2 else 1, groups - 1, 2):
            a, b = g * NS + s, (g + 1) * NS + s
            pairs += [(a, b), (b, a)]
    return pairs


def body(field, source, patch_of_slot, neighbour, wave_index, wave_table):
    groups = lax.axis_size("grp")
    both = ("grp", "sub")
    up = [(i, (i + 1) % NS) for i in range(NS)]
    down = [((i + 1) % NS, i) for i in range(NS)]
    ring = lambda x: (lax.ppermute(x, "sub", up), lax.ppermute(x, "sub", down))
    plane = (PATCHES, CELLS)

    (packed,) = call(pack_body, [(NS, 40, LANES)], [field, source, patch_of_slot, wave_index, wave_table])
    raw = lax.all_to_all(packed, "sub", 0, 0, tiled=True).reshape(NS * 40, LANES)
    own, start, slot = call(place_body, [(5,) + plane, (2,) + plane, (LIVE, LANES)], [raw])
    far = lax.ppermute(own, both, swap_pairs(groups, (0, 1, 2, 13, 14, 15)))
    before, after = ring(start)
    (one,) = call(first_body, [(4,) + plane], [own, before, after, far])
    before, after = ring(one)
    two, sent = call(
        second_body, [(4,) + plane, (4 * LIVE, LANES)], [own, far, before, after, one, slot]
    )
    before, after = ring(two)
    (block,) = call(restrict_body, [(16, LANES)], [own, far, before, after, two, one])
    far_block = lax.ppermute(block, both, swap_pairs(groups, range(NS)))
    (bundle,) = call(bundle_body, [(NS, 48, LANES)], [sent.reshape(NS, 16, LANES), block, far_block])
    back = lax.all_to_all(bundle, "sub", 0, 0, tiled=True)
    (out,) = call(
        correct_body,
        [(SLOTS, 2, EDGE, CELLS)],
        [back, patch_of_slot],
        [(4, 16, LANES), (2 * SLOTS, EDGE, CELLS)],
    )
    return out


def solution(mesh):
    return jax.shard_map(
        body,
        mesh=mesh,
        in_specs=(
            P(("grp", "sub"), None, None, None),
            P(("grp", "sub"), None, None, None),
            P(("grp", "sub")),
            P(("grp", "sub"), None),
            P(("grp", "sub")),
            P(),
        ),
        out_specs=P(("grp", "sub"), None, None, None),
        check_vma=False,
    )
```

```python
import jax
import jax.numpy as jnp
from jax import lax
from jax.experimental import pallas as pl
from jax.experimental.pallas import tpu as pltpu
from jax.sharding import PartitionSpec as P

PZ = 4
PY = 12
PATCHES = PY * PZ
EDGE = 16
CELLS = EDGE * EDGE
SLOTS = 4
NS = 16
LIVE = NS * SLOTS
LANES = 128

omega_fine = 0.7
omega_coarse = 0.6
shift_imag = 0.5

F32 = jnp.float32
VM = pl.BlockSpec(memory_space=pltpu.VMEM)
SM = pl.BlockSpec(memory_space=pltpu.SMEM)


def call(body, outs, ins, scratch=(), specs=None, limit=16):
    return pl.pallas_call(
        body,
        out_shape=[jax.ShapeDtypeStruct(shape, F32) for shape in outs],
        in_specs=specs or [SM if a.dtype == jnp.int32 else VM for a in ins],
        out_specs=[VM] * len(outs),
        scratch_shapes=[pltpu.VMEM(s, F32) if isinstance(s, tuple) else s for s in scratch],
        compiler_params=pltpu.CompilerParams(vmem_limit_bytes=limit << 20),
    )(*ins)


def select(picks, x):
    picks = picks.astype(jnp.bfloat16)
    out = None
    for _ in range(3):
        piece = x.astype(jnp.bfloat16)
        x = x - piece.astype(F32)
        term = jnp.dot(picks, piece, preferred_element_type=F32)
        out = term if out is None else out + term
    return out


def select_lanes(x, picks):
    picks = picks.astype(jnp.bfloat16)
    out = None
    for _ in range(3):
        piece = x.astype(jnp.bfloat16)
        x = x - piece.astype(F32)
        term = jnp.dot(piece, picks, preferred_element_type=F32)
        out = term if out is None else out + term
    return out


def iota(shape, dim):
    return lax.broadcasted_iota(jnp.int32, shape, dim)


def lane_roll(x, shift):
    return pltpu.roll(x, shift % x.shape[1], 1)


def row_roll(x, shift):
    return pltpu.roll(x, shift % x.shape[0], 0)


def in_plane(u):
    shape = u[0].shape
    lane = iota(shape, 1)
    patch = iota(shape, 0)
    k = lane % EDGE
    col = patch % PZ
    not_last, not_first = k < EDGE - 1, k > 0
    has_next, has_prev = col < PZ - 1, col > 0
    out = []
    ahead = [lane_roll(t, -EDGE) for t in u]
    behind = [lane_roll(t, EDGE) for t in u]
    low, high = lane >= EDGE, lane < LANES - EDGE
    y_next = [
        jnp.where(high, ahead[0], ahead[1]),
        jnp.where(high, ahead[1], jnp.where(patch < PATCHES - PZ, row_roll(ahead[0], -PZ), 0.0)),
    ]
    y_prev = [
        jnp.where(low, behind[0], jnp.where(patch >= PZ, row_roll(behind[1], PZ), 0.0)),
        jnp.where(low, behind[1], behind[0]),
    ]
    for h in range(2):
        t = u[h]
        z_next = jnp.where(
            not_last,
            lane_roll(t, -1),
            jnp.where(has_next, row_roll(lane_roll(t, EDGE - 1), -1), 0.0),
        )
        z_prev = jnp.where(
            not_first,
            lane_roll(t, 1),
            jnp.where(has_prev, row_roll(lane_roll(t, 1 - EDGE), 1), 0.0),
        )
        out.append((z_next + z_prev) + (y_next[h] + y_prev[h]))
    return out


def halves(ref, index):
    return [ref[index, :, :LANES], ref[index, :, LANES:]]


def put(ref, index, pair):
    ref[index, :, :LANES] = pair[0]
    ref[index, :, LANES:] = pair[1]


def field_of(ref, first):
    return [halves(ref, first), halves(ref, first + 1)]


def choose(flag, a, b):
    return [[jnp.where(flag, x, y) for x, y in zip(p, q)] for p, q in zip(a, b)]


def around(u, before, after):
    return [
        [n + (x + y) for n, x, y in zip(in_plane(u[part]), before[part], after[part])]
        for part in range(2)
    ]


def diagonal(wave):
    real, imag = 6.0 - wave, shift_imag * wave
    return real, imag


def smooth(u, total, rights, wave):
    real, imag = diagonal(wave)
    scale = omega_fine / (real * real + imag * imag)
    real, imag = real * scale, imag * scale
    keep = 1.0 - omega_fine
    out_re, out_im = [], []
    for h in range(2):
        a = rights[0][h] + total[0][h]
        b = rights[1][h] + total[1][h]
        out_re.append(keep * u[0][h] + (a * real - b * imag))
        out_im.append(keep * u[1][h] + (a * imag + b * real))
    return [out_re, out_im]


def residual(u, total, rights, wave):
    real, imag = diagonal(wave)
    out_re, out_im = [], []
    for h in range(2):
        out_re.append(rights[0][h] + total[0][h] - (real * u[0][h] + imag * u[1][h]))
        out_im.append(rights[1][h] + total[1][h] - (real * u[1][h] - imag * u[0][h]))
    return [out_re, out_im]


def position():
    return lax.axis_index("grp"), lax.axis_index("sub")


def low_side_open(g):
    last = lax.axis_size("grp") - 1
    beyond = jnp.where(g % 2 == 0, g - 1, g + 1)
    return (beyond >= 0) & (beyond <= last)


def pack_body(
    field_hbm, source_hbm, patch_hbm, index_hbm, table_hbm, out_ref,
    field_ref, source_ref, patch_ref, index_ref, table_ref, sems,
):
    pairs = (
        (field_hbm, field_ref),
        (source_hbm, source_ref),
        (patch_hbm, patch_ref),
        (index_hbm, index_ref),
        (table_hbm, table_ref),
    )
    copies = [pltpu.make_async_copy(a, b, sems.at[i]) for i, (a, b) in enumerate(pairs)]
    for copy in copies:
        copy.start()
    for copy in copies:
        copy.wait()
    g, _ = position()
    odd = g % 2 == 1
    for q in range(SLOTS):
        patch = jnp.full((1, LANES), patch_ref[q].astype(F32), F32)
        wave = jnp.full((1, LANES), table_ref[index_ref[q]], F32)
        for s in range(NS):
            out_ref[s, 10 * q + 8 : 10 * q + 9, :] = patch
            out_ref[s, 10 * q + 9 : 10 * q + 10, :] = wave
    for s in range(NS):
        layer = jnp.where(odd, EDGE - 1 - s, s)
        for q in range(SLOTS):
            for a, ref in enumerate((field_ref, source_ref)):
                for part in range(2):
                    row = 10 * q + 4 * a + 2 * part
                    cells = ref[q, part, pl.ds(layer, 1), :]
                    out_ref[s, row : row + 1, :] = cells[:, :LANES]
                    out_ref[s, row + 1 : row + 2, :] = cells[:, LANES:]


def place_body(raw_ref, plane_ref, field_ref, slot_ref):
    patches = raw_ref[pl.ds(8, LIVE, stride=10), :]
    held = (patches == iota((LIVE, LANES), 1).astype(F32)).astype(F32)
    slot_ref[...] = held
    pick = held.T[:PATCHES]
    order = (0, 1, 2, 3, 4, 5, 6, 7, 9)
    rows = jnp.concatenate([raw_ref[pl.ds(c, LIVE, stride=10), :] for c in order], 1)
    placed = select(pick, rows)
    for c in range(4):
        pair = [placed[:, CELLS * c : CELLS * c + LANES], placed[:, CELLS * c + LANES : CELLS * (c + 1)]]
        put(plane_ref, c, pair)
        if c < 2:
            put(field_ref, c, pair)
    put(plane_ref, 4, [placed[:, 4 * CELLS :]] * 2)


def first_body(own_ref, before_ref, after_ref, far_ref, out_ref):
    _, s = position()
    u = field_of(own_ref, 0)
    v = field_of(far_ref, 0)
    before = choose(s == 0, v, field_of(before_ref, 0))
    after = choose(s == NS - 1, v, field_of(after_ref, 0))
    new = smooth(u, around(u, before, after), field_of(own_ref, 2), own_ref[4, :, :LANES])
    for part in range(2):
        put(out_ref, part, new[part])
        put(out_ref, 2 + part, v[part])


def open_factor():
    g, s = position()
    return jnp.where((s >= NS // 2) | low_side_open(g), 1.0, 0.0)


def window_lane(shape, dim):
    cell = iota(shape, dim)
    part, inside = cell // CELLS, cell % CELLS
    return part * 64 + (inside // (4 * EDGE) + 2) * 8 + (inside % EDGE) // 4 + 2


def second_body(own_ref, far_ref, before_ref, after_ref, mine_ref, field_ref, sums_ref, values_ref):
    _, s = position()
    first, last = s == 0, s == NS - 1
    u = field_of(own_ref, 0)
    v = field_of(far_ref, 0)
    one = field_of(mine_ref, 0)
    rights = field_of(own_ref, 2)
    wave = own_ref[4, :, :LANES]
    v_before = choose(first, u, field_of(before_ref, 2))
    v_after = choose(last, u, field_of(after_ref, 2))
    v_one = smooth(v, around(v, v_before, v_after), field_of(far_ref, 2), far_ref[4, :, :LANES])
    factor = open_factor()
    v_one = [[x * factor for x in pair] for pair in v_one]
    before = choose(first, v_one, field_of(before_ref, 0))
    after = choose(last, v_one, field_of(after_ref, 0))
    two = smooth(one, around(one, before, after), rights, wave)
    for part in range(2):
        put(field_ref, part, two[part])
    r = residual(two, [in_plane(two[0]), in_plane(two[1])], rights, wave)
    rows = jnp.concatenate(
        [jnp.concatenate(r[0] + r[1], 1), jnp.concatenate(two[0] + two[1], 1)], 0
    )
    shape = (2 * CELLS, LANES)
    gather = jnp.where(window_lane(shape, 0) == iota(shape, 1), 1.0, 0.0)
    sums = select_lanes(rows, gather)
    lane = iota((PATCHES, LANES), 1)
    sums_ref[...] = jnp.where(lane == 0, wave, sums[:PATCHES])
    values_ref[...] = sums[PATCHES:]


def join_body(sums_ref, values_ref, before_ref, after_ref, out_ref):
    _, s = position()
    before = jnp.where(s == 0, 0.0, before_ref[...])
    after = jnp.where(s == NS - 1, 0.0, after_ref[...])
    out_ref[0] = sums_ref[...] + (before + after)
    out_ref[1] = values_ref[...]


def sides(x, patch, col):
    return (
        jnp.where(patch >= PZ, row_roll(x, PZ), 0.0),
        jnp.where(patch < PATCHES - PZ, row_roll(x, -PZ), 0.0),
        jnp.where(col > 0, row_roll(x, 1), 0.0),
        jnp.where(col < PZ - 1, row_roll(x, -1), 0.0),
    )


def windows(x):
    patch, lane = iota(x.shape, 0), iota(x.shape, 1)
    col = patch % PZ
    a, b = (lane // 8) % 8, lane % 8
    x = jnp.where((a >= 2) & (a < 6) & (b >= 2) & (b < 6), x, 0.0)
    _, _, low, high = sides(x, patch, col)
    x = x + jnp.where(b < 2, lane_roll(low, -4), 0.0) + jnp.where(b >= 6, lane_roll(high, 4), 0.0)
    low, high, _, _ = sides(x, patch, col)
    return x + jnp.where(a < 2, lane_roll(low, -32), 0.0) + jnp.where(a >= 6, lane_roll(high, 32), 0.0)


def slots_body(field_ref, own_ref, slot_ref, out_ref, wave_ref, patch_ref):
    _, s = position()
    rows = [half for c in range(2) for half in halves(field_ref, c)]
    out_ref[...] = select(slot_ref[:, :PATCHES], jnp.concatenate(rows, 1))
    wave = own_ref[4, :, :LANES]
    patch, lane = iota(wave.shape, 0), iota(wave.shape, 1)
    col = patch % PZ
    a, b = (lane // 8) % 8, lane % 8
    _, _, low, high = sides(wave, patch, col)
    wave = jnp.where(b < 2, low, jnp.where(b >= 6, high, wave))
    low, high, _, _ = sides(wave, patch, col)
    wave = jnp.where(a < 2, low, jnp.where(a >= 6, high, wave))
    mine = slot_ref[pl.ds(SLOTS * s, SLOTS), :]
    wave_ref[...] = select(mine[:, :PATCHES], wave)
    index = iota(mine.shape, 1).astype(F32) + 1.0
    patch_ref[...] = jnp.broadcast_to(jnp.sum(mine * index, 1, keepdims=True) - 1.0, mine.shape)


def bundle_body(sent_ref, block_ref, far_ref, slot_ref, out_ref):
    _, s = position()
    factor = open_factor()
    edge = jnp.where((s == 0) | (s == NS - 1), 1.0, 0.0)
    own = windows(block_ref[0] + edge * far_ref[1])
    far = windows(factor * (far_ref[0] + edge * block_ref[1]))
    patch, lane = iota(far.shape, 0), iota(far.shape, 1)
    wave = jnp.broadcast_to(far_ref[0, :, 0:1], far.shape)
    beside = (wave,) + sides(wave, patch, patch % PZ)
    for i, x in enumerate(beside):
        far = jnp.where(lane == i, x, far)
    placed = select(slot_ref[:, :PATCHES], jnp.concatenate([own, far], 1))
    for c in range(4):
        out_ref[pl.ds(c, LIVE, stride=6), :] = sent_ref[:, LANES * c : LANES * (c + 1)]
    for c in range(2):
        out_ref[pl.ds(4 + c, LIVE, stride=6), :] = placed[:, LANES * c : LANES * (c + 1)]


def coarse_sum(e):
    return (lane_roll(e, -1) + lane_roll(e, 1)) + (lane_roll(e, -8) + lane_roll(e, 8))


def correct_body(raw_ref, wave_ref, patch_ref, out_ref, grown_ref, smooth_ref):
    g, _ = position()
    odd = g % 2 == 1
    rows = 24
    shape = (SLOTS, LANES)

    def slot_rows(s, c):
        return raw_ref[pl.ds(rows * s + c, SLOTS, stride=6), :]

    def total(start, c):
        parts = [slot_rows(start + i, c) for i in range(4)]
        return ((parts[0] + parts[1]) + (parts[2] + parts[3])) * (1.0 / 64.0)

    lane = iota((LANES, LANES), 1)
    a, b = (lane // 8) % 8, lane % 8
    region = jnp.where(a < 2, 1, jnp.where(a >= 6, 2, jnp.where(b < 2, 3, jnp.where(b >= 6, 4, 0))))
    spread = jnp.where(iota((LANES, LANES), 0) == region, 1.0, 0.0)
    ends = jnp.concatenate([slot_rows(0, 5), slot_rows(NS - 1, 5)], 0)
    ends = select_lanes(ends, spread)
    low, high = ends[:SLOTS], ends[SLOTS:]
    own = wave_ref[...]
    wave = jnp.concatenate([low, low, own, own, own, own, high, high], 0)
    rhs = jnp.concatenate(
        [total(4, 5), total(0, 5)] + [total(4 * i, 4) for i in range(4)] + [total(12, 5), total(8, 5)], 0
    )
    lane = iota(shape, 1)
    a, b = (lane // 8) % 8, lane % 8
    patch = patch_ref[...].astype(jnp.int32)
    line, col = patch // PZ, patch % PZ
    y, z = 4 * line + a - 2, 4 * col + b - 2
    inside = jnp.where((y >= 0) & (y < 4 * PY) & (z >= 0) & (z < 4 * PZ), 1.0, 0.0)
    lower = jnp.where(low_side_open(g), inside, 0.0)
    inside = jnp.concatenate([lower, lower] + [inside] * 6, 0) > 0.0
    part_sign = jnp.where(iota(wave.shape, 1) < 64, -1.0, 1.0)
    real, imag = 6.0 / 16.0 - wave, shift_imag * wave
    scale = omega_coarse / (real * real + imag * imag)
    real, imag = real * scale, part_sign * imag * scale

    def divide(x):
        return jnp.where(inside, x * real + lane_roll(x, 64) * imag, 0.0)

    e = divide(rhs)
    for _ in range(2):
        beside = coarse_sum(e) + (row_roll(e, SLOTS) + row_roll(e, -SLOTS))
        e = (1.0 - omega_coarse) * e + divide(rhs + beside * (1.0 / 16.0))
    wide = (LANES, 2 * CELLS)
    widen = jnp.where(window_lane(wide, 1) == iota(wide, 0), 1.0, 0.0)
    grown_ref[...] = select_lanes(e[2 * SLOTS : 6 * SLOTS], widen)
    for i in range(EDGE):
        s = jnp.where(odd, EDGE - 1 - i, i)
        for q in range(SLOTS):
            for part in range(2):
                for h in range(2):
                    row = raw_ref[pl.ds(rows * s + 6 * q + 2 * part + h, 1), :]
                    smooth_ref[2 * q + part, i : i + 1, LANES * h : LANES * (h + 1)] = row
    for q in range(SLOTS):
        held = jnp.broadcast_to(patch_ref[q : q + 1, 0:1] >= 0.0, (4, CELLS))
        for i in range(4):
            plane = jnp.where(odd, 3 - i, i)
            line = grown_ref[pl.ds(SLOTS * plane + q, 1), :]
            for part in range(2):
                extra = jnp.broadcast_to(line[:, CELLS * part : CELLS * (part + 1)], (4, CELLS))
                value = smooth_ref[2 * q + part, 4 * i : 4 * i + 4] + extra
                out_ref[q, part, 4 * i : 4 * i + 4] = jnp.where(held, value, 0.0)


def swap_pairs(groups, subs):
    pairs = []
    for s in subs:
        for g in range(0 if s >= NS // 2 else 1, groups - 1, 2):
            a, b = g * NS + s, (g + 1) * NS + s
            pairs += [(a, b), (b, a)]
    return pairs


def body(field, source, patch_of_slot, neighbour, wave_index, wave_table):
    groups = lax.axis_size("grp")
    both = ("grp", "sub")
    up = [(i, (i + 1) % NS) for i in range(NS)]
    down = [((i + 1) % NS, i) for i in range(NS)]
    ring = lambda x: (lax.ppermute(x, "sub", up), lax.ppermute(x, "sub", down))
    plane = (PATCHES, CELLS)

    hbm = pl.BlockSpec(memory_space=pltpu.HBM)
    (packed,) = call(
        pack_body,
        [(NS, 40, LANES)],
        [field, source, patch_of_slot, wave_index, wave_table],
        [
            field.shape,
            source.shape,
            pltpu.SMEM(patch_of_slot.shape, jnp.int32),
            pltpu.SMEM(wave_index.shape, jnp.int32),
            pltpu.SMEM(wave_table.shape, F32),
            pltpu.SemaphoreType.DMA((5,)),
        ],
        [hbm] * 5,
        60,
    )
    raw = lax.all_to_all(packed, "sub", 0, 0, tiled=True).reshape(NS * 40, LANES)
    own, start, slot = call(place_body, [(5,) + plane, (2,) + plane, (LIVE, LANES)], [raw])
    far = lax.ppermute(own, both, swap_pairs(groups, (0, 1, 14, 15)))
    before, after = ring(start)
    (one,) = call(first_body, [(4,) + plane], [own, before, after, far])
    before, after = ring(one)
    row = (PATCHES, LANES)
    two, sums, values = call(
        second_body, [(2,) + plane, row, row], [own, far, before, after, one]
    )
    before, after = ring(values)
    mine = (SLOTS, LANES)
    sent, wave, patch = call(slots_body, [(LIVE, 2 * CELLS), mine, mine], [two, own, slot])
    (block,) = call(join_body, [(2,) + row], [sums, values, before, after])
    far_block = lax.ppermute(block, both, swap_pairs(groups, range(NS)))
    (bundle,) = call(bundle_body, [(LIVE * 6, LANES)], [sent, block, far_block, slot])
    back = lax.all_to_all(bundle.reshape(NS, 24, LANES), "sub", 0, 0, tiled=True)
    (out,) = call(
        correct_body,
        [(SLOTS, 2, EDGE, CELLS)],
        [back.reshape(NS * 24, LANES), wave, patch],
        [(EDGE, 2 * CELLS), (2 * SLOTS, EDGE, CELLS)],
    )
    return out


def solution(mesh):
    return jax.shard_map(
        body,
        mesh=mesh,
        in_specs=(
            P(("grp", "sub"), None, None, None),
            P(("grp", "sub"), None, None, None),
            P(("grp", "sub")),
            P(("grp", "sub"), None),
            P(("grp", "sub")),
            P(),
        ),
        out_specs=P(("grp", "sub"), None, None, None),
        check_vma=False,
    )
```

```python
import jax
import jax.numpy as jnp
from jax import lax
from jax.experimental import pallas as pl
from jax.experimental.pallas import tpu as pltpu
from jax.sharding import PartitionSpec as P

PZ = 4
PY = 12
PATCHES = PY * PZ
EDGE = 16
CELLS = EDGE * EDGE
SLOTS = 4
NS = 16
LIVE = NS * SLOTS
LANES = 128

omega_fine = 0.7
omega_coarse = 0.6
shift_imag = 0.5

F32 = jnp.float32
VM = pl.BlockSpec(memory_space=pltpu.VMEM)
SM = pl.BlockSpec(memory_space=pltpu.SMEM)


def call(body, outs, ins, scratch=(), specs=None, limit=16):
    return pl.pallas_call(
        body,
        out_shape=[jax.ShapeDtypeStruct(shape, F32) for shape in outs],
        in_specs=specs or [SM if a.dtype == jnp.int32 else VM for a in ins],
        out_specs=[VM] * len(outs),
        scratch_shapes=[pltpu.VMEM(s, F32) if isinstance(s, tuple) else s for s in scratch],
        compiler_params=pltpu.CompilerParams(vmem_limit_bytes=limit << 20),
    )(*ins)


def select(picks, x):
    picks = picks.astype(jnp.bfloat16)
    out = None
    for _ in range(3):
        piece = x.astype(jnp.bfloat16)
        x = x - piece.astype(F32)
        term = jnp.dot(picks, piece, preferred_element_type=F32)
        out = term if out is None else out + term
    return out


def select_lanes(x, picks):
    picks = picks.astype(jnp.bfloat16)
    out = None
    for _ in range(3):
        piece = x.astype(jnp.bfloat16)
        x = x - piece.astype(F32)
        term = jnp.dot(piece, picks, preferred_element_type=F32)
        out = term if out is None else out + term
    return out


def iota(shape, dim):
    return lax.broadcasted_iota(jnp.int32, shape, dim)


def lane_roll(x, shift):
    return pltpu.roll(x, shift % x.shape[1], 1)


def row_roll(x, shift):
    return pltpu.roll(x, shift % x.shape[0], 0)


def in_plane(u):
    shape = u[0].shape
    lane = iota(shape, 1)
    patch = iota(shape, 0)
    k = lane % EDGE
    col = patch % PZ
    not_last, not_first = k < EDGE - 1, k > 0
    has_next, has_prev = col < PZ - 1, col > 0
    out = []
    ahead = [lane_roll(t, -EDGE) for t in u]
    behind = [lane_roll(t, EDGE) for t in u]
    low, high = lane >= EDGE, lane < LANES - EDGE
    y_next = [
        jnp.where(high, ahead[0], ahead[1]),
        jnp.where(high, ahead[1], jnp.where(patch < PATCHES - PZ, row_roll(ahead[0], -PZ), 0.0)),
    ]
    y_prev = [
        jnp.where(low, behind[0], jnp.where(patch >= PZ, row_roll(behind[1], PZ), 0.0)),
        jnp.where(low, behind[1], behind[0]),
    ]
    for h in range(2):
        t = u[h]
        z_next = jnp.where(
            not_last,
            lane_roll(t, -1),
            jnp.where(has_next, row_roll(lane_roll(t, EDGE - 1), -1), 0.0),
        )
        z_prev = jnp.where(
            not_first,
            lane_roll(t, 1),
            jnp.where(has_prev, row_roll(lane_roll(t, 1 - EDGE), 1), 0.0),
        )
        out.append((z_next + z_prev) + (y_next[h] + y_prev[h]))
    return out


def halves(ref, index):
    return [ref[index, :, :LANES], ref[index, :, LANES:]]


def put(ref, index, pair):
    ref[index, :, :LANES] = pair[0]
    ref[index, :, LANES:] = pair[1]


def field_of(ref, first):
    return [halves(ref, first), halves(ref, first + 1)]


def choose(flag, a, b):
    return [[jnp.where(flag, x, y) for x, y in zip(p, q)] for p, q in zip(a, b)]


def around(u, before, after):
    return [
        [n + (x + y) for n, x, y in zip(in_plane(u[part]), before[part], after[part])]
        for part in range(2)
    ]


def diagonal(wave):
    real, imag = 6.0 - wave, shift_imag * wave
    return real, imag


def smooth(u, total, rights, wave):
    real, imag = diagonal(wave)
    scale = omega_fine / (real * real + imag * imag)
    real, imag = real * scale, imag * scale
    keep = 1.0 - omega_fine
    out_re, out_im = [], []
    for h in range(2):
        a = rights[0][h] + total[0][h]
        b = rights[1][h] + total[1][h]
        out_re.append(keep * u[0][h] + (a * real - b * imag))
        out_im.append(keep * u[1][h] + (a * imag + b * real))
    return [out_re, out_im]


def residual(u, total, rights, wave):
    real, imag = diagonal(wave)
    out_re, out_im = [], []
    for h in range(2):
        out_re.append(rights[0][h] + total[0][h] - (real * u[0][h] + imag * u[1][h]))
        out_im.append(rights[1][h] + total[1][h] - (real * u[1][h] - imag * u[0][h]))
    return [out_re, out_im]


def position():
    return lax.axis_index("grp"), (lax.axis_index("sub") + NS - 1) % NS


def device_at(place):
    return (place + 1) % NS


def low_side_open(g):
    last = lax.axis_size("grp") - 1
    beyond = jnp.where(g % 2 == 0, g - 1, g + 1)
    return (beyond >= 0) & (beyond <= last)


def pack_body(
    field_hbm, source_hbm, patch_hbm, index_hbm, table_hbm, out_ref,
    field_ref, source_ref, patch_ref, index_ref, table_ref, sems,
):
    pairs = (
        (field_hbm, field_ref),
        (source_hbm, source_ref),
        (patch_hbm, patch_ref),
        (index_hbm, index_ref),
        (table_hbm, table_ref),
    )
    copies = [pltpu.make_async_copy(a, b, sems.at[i]) for i, (a, b) in enumerate(pairs)]
    for copy in copies:
        copy.start()
    for copy in copies:
        copy.wait()
    g, _ = position()
    odd = g % 2 == 1
    for q in range(SLOTS):
        patch = jnp.full((1, LANES), patch_ref[q].astype(F32), F32)
        wave = jnp.full((1, LANES), table_ref[index_ref[q]], F32)
        for s in range(NS):
            out_ref[s, 10 * q + 8 : 10 * q + 9, :] = patch
            out_ref[s, 10 * q + 9 : 10 * q + 10, :] = wave
    for s in range(NS):
        place = (s + NS - 1) % NS
        layer = jnp.where(odd, EDGE - 1 - place, place)
        for q in range(SLOTS):
            for a, ref in enumerate((field_ref, source_ref)):
                for part in range(2):
                    row = 10 * q + 4 * a + 2 * part
                    cells = ref[q, part, pl.ds(layer, 1), :]
                    out_ref[s, row : row + 1, :] = cells[:, :LANES]
                    out_ref[s, row + 1 : row + 2, :] = cells[:, LANES:]


def place_body(raw_ref, plane_ref, field_ref, slot_ref):
    patches = raw_ref[pl.ds(8, LIVE, stride=10), :]
    held = (patches == iota((LIVE, LANES), 1).astype(F32)).astype(F32)
    slot_ref[...] = held
    pick = held.T[:PATCHES]
    order = (0, 1, 2, 3, 4, 5, 6, 7, 9)
    rows = jnp.concatenate([raw_ref[pl.ds(c, LIVE, stride=10), :] for c in order], 1)
    placed = select(pick, rows)
    for c in range(4):
        pair = [placed[:, CELLS * c : CELLS * c + LANES], placed[:, CELLS * c + LANES : CELLS * (c + 1)]]
        put(plane_ref, c, pair)
        if c < 2:
            put(field_ref, c, pair)
    put(plane_ref, 4, [placed[:, 4 * CELLS :]] * 2)


def first_body(own_ref, before_ref, after_ref, far_ref, out_ref):
    _, s = position()
    u = field_of(own_ref, 0)
    factor = open_factor()
    v = [[x * factor for x in pair] for pair in field_of(far_ref.at[other()], 0)]
    before = choose(s == 0, v, field_of(before_ref, 0))
    after = choose(s == NS - 1, v, field_of(after_ref, 0))
    new = smooth(u, around(u, before, after), field_of(own_ref, 2), own_ref[4, :, :LANES])
    for part in range(2):
        put(out_ref, part, new[part])
        put(out_ref, 2 + part, v[part])


def other():
    g, s = position()
    return jnp.where((g % 2 == 0) == (s >= NS // 2), 1, 0)


def open_factor():
    g, s = position()
    return jnp.where((s >= NS // 2) | low_side_open(g), 1.0, 0.0)


def window_lane(shape, dim):
    cell = iota(shape, dim)
    part, inside = cell // CELLS, cell % CELLS
    return part * 64 + (inside // (4 * EDGE) + 2) * 8 + (inside % EDGE) // 4 + 2


def second_body(own_ref, far_ref, before_ref, after_ref, mine_ref, field_ref, sums_ref, values_ref):
    _, s = position()
    first, last = s == 0, s == NS - 1
    u = field_of(own_ref, 0)
    far_ref = far_ref.at[other()]
    factor = open_factor()
    v = [[x * factor for x in pair] for pair in field_of(far_ref, 0)]
    one = field_of(mine_ref, 0)
    rights = field_of(own_ref, 2)
    wave = own_ref[4, :, :LANES]
    v_before = choose(first, u, field_of(before_ref, 2))
    v_after = choose(last, u, field_of(after_ref, 2))
    v_one = smooth(v, around(v, v_before, v_after), field_of(far_ref, 2), far_ref[4, :, :LANES])
    v_one = [[x * factor for x in pair] for pair in v_one]
    before = choose(first, v_one, field_of(before_ref, 0))
    after = choose(last, v_one, field_of(after_ref, 0))
    two = smooth(one, around(one, before, after), rights, wave)
    for part in range(2):
        put(field_ref, part, two[part])
    r = residual(two, [in_plane(two[0]), in_plane(two[1])], rights, wave)
    rows = jnp.concatenate(
        [jnp.concatenate(r[0] + r[1], 1), jnp.concatenate(two[0] + two[1], 1)], 0
    )
    shape = (2 * CELLS, LANES)
    gather = jnp.where(window_lane(shape, 0) == iota(shape, 1), 1.0, 0.0)
    sums = select_lanes(rows, gather)
    lane = iota((PATCHES, LANES), 1)
    values = sums[PATCHES:]
    beside = jnp.where((s % 4 == 0) | (s % 4 == 3), 1.0, 2.0)
    sums_ref[...] = jnp.where(lane == 0, wave, sums[:PATCHES] + beside * values)
    values_ref[...] = values


def join_body(sums_ref, pair_ref, out_ref):
    _, s = position()
    core = lax.axis_index("sub") % 2
    meets = ((s % 4 == 0) | (s % 4 == 3)) & (s > 0) & (s < NS - 1)
    out_ref[0] = sums_ref[...] + jnp.where(meets, pair_ref[1 - core], 0.0)
    out_ref[1] = pair_ref[core]


def sides(x, patch, col):
    return (
        jnp.where(patch >= PZ, row_roll(x, PZ), 0.0),
        jnp.where(patch < PATCHES - PZ, row_roll(x, -PZ), 0.0),
        jnp.where(col > 0, row_roll(x, 1), 0.0),
        jnp.where(col < PZ - 1, row_roll(x, -1), 0.0),
    )


def windows(x):
    patch, lane = iota(x.shape, 0), iota(x.shape, 1)
    col = patch % PZ
    a, b = (lane // 8) % 8, lane % 8
    x = jnp.where((a >= 2) & (a < 6) & (b >= 2) & (b < 6), x, 0.0)
    _, _, low, high = sides(x, patch, col)
    x = x + jnp.where(b < 2, lane_roll(low, -4), 0.0) + jnp.where(b >= 6, lane_roll(high, 4), 0.0)
    low, high, _, _ = sides(x, patch, col)
    return x + jnp.where(a < 2, lane_roll(low, -32), 0.0) + jnp.where(a >= 6, lane_roll(high, 32), 0.0)


def slots_body(field_ref, own_ref, slot_ref, out_ref, wave_ref, patch_ref):
    _, s = position()
    rows = [half for c in range(2) for half in halves(field_ref, c)]
    out_ref[...] = select(slot_ref[:, :PATCHES], jnp.concatenate(rows, 1))
    wave = own_ref[4, :, :LANES]
    patch, lane = iota(wave.shape, 0), iota(wave.shape, 1)
    col = patch % PZ
    a, b = (lane // 8) % 8, lane % 8
    _, _, low, high = sides(wave, patch, col)
    wave = jnp.where(b < 2, low, jnp.where(b >= 6, high, wave))
    low, high, _, _ = sides(wave, patch, col)
    wave = jnp.where(a < 2, low, jnp.where(a >= 6, high, wave))
    mine = slot_ref[pl.ds(SLOTS * device_at(s), SLOTS), :]
    wave_ref[...] = select(mine[:, :PATCHES], wave)
    index = iota(mine.shape, 1).astype(F32) + 1.0
    patch_ref[...] = jnp.broadcast_to(jnp.sum(mine * index, 1, keepdims=True) - 1.0, mine.shape)


def bundle_body(sent_ref, block_ref, far_ref, slot_ref, out_ref):
    _, s = position()
    factor = open_factor()
    far_ref = far_ref.at[other()]
    edge = jnp.where((s == 0) | (s == NS - 1), 1.0, 0.0)
    own = windows(block_ref[0] + (edge * factor) * far_ref[1])
    far = windows(factor * (far_ref[0] + edge * block_ref[1]))
    patch, lane = iota(far.shape, 0), iota(far.shape, 1)
    wave = jnp.broadcast_to(far_ref[0, :, 0:1], far.shape)
    beside = (wave,) + sides(wave, patch, patch % PZ)
    for i, x in enumerate(beside):
        far = jnp.where(lane == i, x, far)
    placed = select(slot_ref[:, :PATCHES], jnp.concatenate([own, far], 1))
    for c in range(4):
        out_ref[pl.ds(c, LIVE, stride=6), :] = sent_ref[:, LANES * c : LANES * (c + 1)]
    for c in range(2):
        out_ref[pl.ds(4 + c, LIVE, stride=6), :] = placed[:, LANES * c : LANES * (c + 1)]


def coarse_sum(e):
    return (lane_roll(e, -1) + lane_roll(e, 1)) + (lane_roll(e, -8) + lane_roll(e, 8))


def correct_body(raw_ref, wave_ref, patch_ref, out_ref, grown_ref, smooth_ref):
    g, _ = position()
    odd = g % 2 == 1
    rows = 24
    shape = (SLOTS, LANES)

    def slot_rows(s, c):
        return raw_ref[pl.ds(rows * s + c, SLOTS, stride=6), :]

    def total(start, c):
        parts = [slot_rows(device_at(start + i), c) for i in range(4)]
        return ((parts[0] + parts[1]) + (parts[2] + parts[3])) * (1.0 / 64.0)

    lane = iota((LANES, LANES), 1)
    a, b = (lane // 8) % 8, lane % 8
    region = jnp.where(a < 2, 1, jnp.where(a >= 6, 2, jnp.where(b < 2, 3, jnp.where(b >= 6, 4, 0))))
    spread = jnp.where(iota((LANES, LANES), 0) == region, 1.0, 0.0)
    ends = jnp.concatenate([slot_rows(device_at(0), 5), slot_rows(device_at(NS - 1), 5)], 0)
    ends = select_lanes(ends, spread)
    low, high = ends[:SLOTS], ends[SLOTS:]
    own = wave_ref[...]
    wave = jnp.concatenate([low, low, own, own, own, own, high, high], 0)
    rhs = jnp.concatenate(
        [total(4, 5), total(0, 5)] + [total(4 * i, 4) for i in range(4)] + [total(12, 5), total(8, 5)], 0
    )
    lane = iota(shape, 1)
    a, b = (lane // 8) % 8, lane % 8
    patch = patch_ref[...].astype(jnp.int32)
    line, col = patch // PZ, patch % PZ
    y, z = 4 * line + a - 2, 4 * col + b - 2
    inside = jnp.where((y >= 0) & (y < 4 * PY) & (z >= 0) & (z < 4 * PZ), 1.0, 0.0)
    lower = jnp.where(low_side_open(g), inside, 0.0)
    inside = jnp.concatenate([lower, lower] + [inside] * 6, 0) > 0.0
    part_sign = jnp.where(iota(wave.shape, 1) < 64, -1.0, 1.0)
    real, imag = 6.0 / 16.0 - wave, shift_imag * wave
    scale = omega_coarse / (real * real + imag * imag)
    real, imag = real * scale, part_sign * imag * scale

    def divide(x):
        return jnp.where(inside, x * real + lane_roll(x, 64) * imag, 0.0)

    e = divide(rhs)
    for _ in range(2):
        beside = coarse_sum(e) + (row_roll(e, SLOTS) + row_roll(e, -SLOTS))
        e = (1.0 - omega_coarse) * e + divide(rhs + beside * (1.0 / 16.0))
    wide = (LANES, 2 * CELLS)
    widen = jnp.where(window_lane(wide, 1) == iota(wide, 0), 1.0, 0.0)
    grown_ref[...] = select_lanes(e[2 * SLOTS : 6 * SLOTS], widen)
    for i in range(EDGE):
        s = device_at(jnp.where(odd, EDGE - 1 - i, i))
        for q in range(SLOTS):
            for part in range(2):
                for h in range(2):
                    row = raw_ref[pl.ds(rows * s + 6 * q + 2 * part + h, 1), :]
                    smooth_ref[2 * q + part, i : i + 1, LANES * h : LANES * (h + 1)] = row
    for q in range(SLOTS):
        held = jnp.broadcast_to(patch_ref[q : q + 1, 0:1] >= 0.0, (4, CELLS))
        for i in range(4):
            plane = jnp.where(odd, 3 - i, i)
            line = grown_ref[pl.ds(SLOTS * plane + q, 1), :]
            for part in range(2):
                extra = jnp.broadcast_to(line[:, CELLS * part : CELLS * (part + 1)], (4, CELLS))
                value = smooth_ref[2 * q + part, 4 * i : 4 * i + 4] + extra
                out_ref[q, part, 4 * i : 4 * i + 4] = jnp.where(held, value, 0.0)


def facing(groups, reach):
    pairs, met = [], set()
    for place in [i for i in range(NS) if i < reach or i >= NS - reach]:
        s = device_at(place)
        for g in range(0 if place >= NS // 2 else 1, groups - 1, 2):
            pairs.append([g * NS + s, (g + 1) * NS + s])
            met.update(pairs[-1])
    for g in range(groups):
        rest = [g * NS + s for s in range(NS) if g * NS + s not in met]
        whole = [i for i in rest if i ^ 1 in rest]
        rest = [i for i in rest if i ^ 1 not in rest]
        pairs += [whole[i : i + 2] for i in range(0, len(whole), 2)]
        pairs += [rest[i : i + 2] for i in range(0, len(rest), 2)]
    return pairs


def body(field, source, patch_of_slot, neighbour, wave_index, wave_table):
    groups = lax.axis_size("grp")
    both = ("grp", "sub")
    up = [(i, (i + 1) % NS) for i in range(NS)]
    down = [((i + 1) % NS, i) for i in range(NS)]
    ring = lambda x: (lax.ppermute(x, "sub", up), lax.ppermute(x, "sub", down))
    plane = (PATCHES, CELLS)

    hbm = pl.BlockSpec(memory_space=pltpu.HBM)
    (packed,) = call(
        pack_body,
        [(NS, 40, LANES)],
        [field, source, patch_of_slot, wave_index, wave_table],
        [
            field.shape,
            source.shape,
            pltpu.SMEM(patch_of_slot.shape, jnp.int32),
            pltpu.SMEM(wave_index.shape, jnp.int32),
            pltpu.SMEM(wave_table.shape, F32),
            pltpu.SemaphoreType.DMA((5,)),
        ],
        [hbm] * 5,
        60,
    )
    raw = lax.all_to_all(packed, "sub", 0, 0, tiled=True).reshape(NS * 40, LANES)
    own, start, slot = call(place_body, [(5,) + plane, (2,) + plane, (LIVE, LANES)], [raw])
    far = lax.all_gather(own, both, axis_index_groups=facing(groups, 2))
    before, after = ring(start)
    (one,) = call(first_body, [(4,) + plane], [own, before, after, far])
    before, after = ring(one)
    row = (PATCHES, LANES)
    two, sums, values = call(
        second_body, [(2,) + plane, row, row], [own, far, before, after, one]
    )
    chips = [[i, i + 1] for i in range(0, NS, 2)]
    pair = lax.all_gather(values, "sub", axis_index_groups=chips)
    mine = (SLOTS, LANES)
    sent, wave, patch = call(slots_body, [(LIVE, 2 * CELLS), mine, mine], [two, own, slot])
    (block,) = call(join_body, [(2,) + row], [sums, pair])
    far_block = lax.all_gather(block, both, axis_index_groups=facing(groups, NS // 2))
    (bundle,) = call(bundle_body, [(LIVE * 6, LANES)], [sent, block, far_block, slot])
    back = lax.all_to_all(bundle.reshape(NS, 24, LANES), "sub", 0, 0, tiled=True)
    (out,) = call(
        correct_body,
        [(SLOTS, 2, EDGE, CELLS)],
        [back.reshape(NS * 24, LANES), wave, patch],
        [(EDGE, 2 * CELLS), (2 * SLOTS, EDGE, CELLS)],
    )
    return out


def solution(mesh):
    return jax.shard_map(
        body,
        mesh=mesh,
        in_specs=(
            P(("grp", "sub"), None, None, None),
            P(("grp", "sub"), None, None, None),
            P(("grp", "sub")),
            P(("grp", "sub"), None),
            P(("grp", "sub")),
            P(),
        ),
        out_specs=P(("grp", "sub"), None, None, None),
        check_vma=False,
    )
```

```python
import jax
import jax.numpy as jnp
from jax import lax
from jax.experimental import pallas as pl
from jax.experimental.pallas import tpu as pltpu
from jax.sharding import PartitionSpec as P

PZ = 4
PY = 12
PATCHES = PY * PZ
EDGE = 16
CELLS = EDGE * EDGE
SLOTS = 4
NS = 16
LIVE = NS * SLOTS
LANES = 128

omega_fine = 0.7
omega_coarse = 0.6
shift_imag = 0.5

F32 = jnp.float32
VM = pl.BlockSpec(memory_space=pltpu.VMEM)
SM = pl.BlockSpec(memory_space=pltpu.SMEM)


def call(body, outs, ins, scratch=(), specs=None, limit=16):
    return pl.pallas_call(
        body,
        out_shape=[jax.ShapeDtypeStruct(shape, F32) for shape in outs],
        in_specs=specs or [SM if a.dtype == jnp.int32 else VM for a in ins],
        out_specs=[VM] * len(outs),
        scratch_shapes=[pltpu.VMEM(s, F32) if isinstance(s, tuple) else s for s in scratch],
        compiler_params=pltpu.CompilerParams(vmem_limit_bytes=limit << 20),
    )(*ins)


def select(picks, x):
    picks = picks.astype(jnp.bfloat16)
    out = None
    for _ in range(3):
        piece = x.astype(jnp.bfloat16)
        x = x - piece.astype(F32)
        term = jnp.dot(picks, piece, preferred_element_type=F32)
        out = term if out is None else out + term
    return out


def select_lanes(x, picks):
    picks = picks.astype(jnp.bfloat16)
    out = None
    for _ in range(3):
        piece = x.astype(jnp.bfloat16)
        x = x - piece.astype(F32)
        term = jnp.dot(piece, picks, preferred_element_type=F32)
        out = term if out is None else out + term
    return out


def iota(shape, dim):
    return lax.broadcasted_iota(jnp.int32, shape, dim)


def lane_roll(x, shift):
    return pltpu.roll(x, shift % x.shape[1], 1)


def row_roll(x, shift):
    return pltpu.roll(x, shift % x.shape[0], 0)


def in_plane(u):
    shape = u[0].shape
    lane = iota(shape, 1)
    patch = iota(shape, 0)
    k = lane % EDGE
    col = patch % PZ
    not_last, not_first = k < EDGE - 1, k > 0
    has_next, has_prev = col < PZ - 1, col > 0
    out = []
    ahead = [lane_roll(t, -EDGE) for t in u]
    behind = [lane_roll(t, EDGE) for t in u]
    low, high = lane >= EDGE, lane < LANES - EDGE
    y_next = [
        jnp.where(high, ahead[0], ahead[1]),
        jnp.where(high, ahead[1], jnp.where(patch < PATCHES - PZ, row_roll(ahead[0], -PZ), 0.0)),
    ]
    y_prev = [
        jnp.where(low, behind[0], jnp.where(patch >= PZ, row_roll(behind[1], PZ), 0.0)),
        jnp.where(low, behind[1], behind[0]),
    ]
    for h in range(2):
        t = u[h]
        z_next = jnp.where(
            not_last,
            lane_roll(t, -1),
            jnp.where(has_next, row_roll(lane_roll(t, EDGE - 1), -1), 0.0),
        )
        z_prev = jnp.where(
            not_first,
            lane_roll(t, 1),
            jnp.where(has_prev, row_roll(lane_roll(t, 1 - EDGE), 1), 0.0),
        )
        out.append((z_next + z_prev) + (y_next[h] + y_prev[h]))
    return out


def halves(ref, index):
    return [ref[index, :, :LANES], ref[index, :, LANES:]]


def put(ref, index, pair):
    ref[index, :, :LANES] = pair[0]
    ref[index, :, LANES:] = pair[1]


def field_of(ref, first):
    return [halves(ref, first), halves(ref, first + 1)]


def rows_of(ref, first):
    return [
        [ref[PATCHES * c : PATCHES * (c + 1), :LANES], ref[PATCHES * c : PATCHES * (c + 1), LANES:]]
        for c in (first, first + 1)
    ]


def wave_row(wave):
    return jnp.sum(jnp.where(iota(wave.shape, 0) == iota(wave.shape, 1), wave, 0.0), 0, keepdims=True)


def wave_rows(row):
    shape = (PATCHES, LANES)
    own = jnp.where(iota(shape, 0) == iota(shape, 1), jnp.broadcast_to(row, shape), 0.0)
    return jnp.broadcast_to(jnp.sum(own, 1, keepdims=True), shape)


def choose(flag, a, b):
    return [[jnp.where(flag, x, y) for x, y in zip(p, q)] for p, q in zip(a, b)]


def around(u, before, after):
    return [
        [n + (x + y) for n, x, y in zip(in_plane(u[part]), before[part], after[part])]
        for part in range(2)
    ]


def diagonal(wave):
    real, imag = 6.0 - wave, shift_imag * wave
    return real, imag


def smooth(u, total, rights, wave):
    real, imag = diagonal(wave)
    scale = omega_fine / (real * real + imag * imag)
    real, imag = real * scale, imag * scale
    keep = 1.0 - omega_fine
    out_re, out_im = [], []
    for h in range(2):
        a = rights[0][h] + total[0][h]
        b = rights[1][h] + total[1][h]
        out_re.append(keep * u[0][h] + (a * real - b * imag))
        out_im.append(keep * u[1][h] + (a * imag + b * real))
    return [out_re, out_im]


def residual(u, total, rights, wave):
    real, imag = diagonal(wave)
    out_re, out_im = [], []
    for h in range(2):
        out_re.append(rights[0][h] + total[0][h] - (real * u[0][h] + imag * u[1][h]))
        out_im.append(rights[1][h] + total[1][h] - (real * u[1][h] - imag * u[0][h]))
    return [out_re, out_im]


def position():
    return lax.axis_index("grp"), (lax.axis_index("sub") + NS - 1) % NS


def device_at(place):
    return (place + 1) % NS


def low_side_open(g):
    last = lax.axis_size("grp") - 1
    beyond = jnp.where(g % 2 == 0, g - 1, g + 1)
    return (beyond >= 0) & (beyond <= last)


def pack_body(
    field_hbm, source_hbm, patch_hbm, index_hbm, table_hbm, out_ref,
    field_ref, source_ref, patch_ref, index_ref, table_ref, sems,
):
    pairs = (
        (field_hbm, field_ref),
        (source_hbm, source_ref),
        (patch_hbm, patch_ref),
        (index_hbm, index_ref),
        (table_hbm, table_ref),
    )
    copies = [pltpu.make_async_copy(a, b, sems.at[i]) for i, (a, b) in enumerate(pairs)]
    for copy in copies:
        copy.start()
    for copy in copies:
        copy.wait()
    g, _ = position()
    odd = g % 2 == 1
    for q in range(SLOTS):
        patch = jnp.full((1, LANES), patch_ref[q].astype(F32), F32)
        wave = jnp.full((1, LANES), table_ref[index_ref[q]], F32)
        for s in range(NS):
            out_ref[s, 10 * q + 8 : 10 * q + 9, :] = patch
            out_ref[s, 10 * q + 9 : 10 * q + 10, :] = wave
    for s in range(NS):
        place = (s + NS - 1) % NS
        layer = jnp.where(odd, EDGE - 1 - place, place)
        for q in range(SLOTS):
            for a, ref in enumerate((field_ref, source_ref)):
                for part in range(2):
                    row = 10 * q + 4 * a + 2 * part
                    cells = ref[q, part, pl.ds(layer, 1), :]
                    out_ref[s, row : row + 1, :] = cells[:, :LANES]
                    out_ref[s, row + 1 : row + 2, :] = cells[:, LANES:]


def place_body(raw_ref, plane_ref, field_ref, slot_ref, wave_ref):
    patches = raw_ref[pl.ds(8, LIVE, stride=10), :]
    held = (patches == iota((LIVE, LANES), 1).astype(F32)).astype(F32)
    slot_ref[...] = held
    pick = held.T[:PATCHES]
    order = (0, 1, 2, 3, 4, 5, 6, 7, 9)
    rows = jnp.concatenate([raw_ref[pl.ds(c, LIVE, stride=10), :] for c in order], 1)
    placed = select(pick, rows)
    for c in range(4):
        pair = [placed[:, CELLS * c : CELLS * c + LANES], placed[:, CELLS * c + LANES : CELLS * (c + 1)]]
        plane_ref[PATCHES * c : PATCHES * (c + 1), :LANES] = pair[0]
        plane_ref[PATCHES * c : PATCHES * (c + 1), LANES:] = pair[1]
        if c < 2:
            put(field_ref, c, pair)
    wave = placed[:, 4 * CELLS :]
    wave_ref[...] = wave
    row = jnp.broadcast_to(wave_row(wave), (8, LANES))
    plane_ref[4 * PATCHES :, :LANES] = row
    plane_ref[4 * PATCHES :, LANES:] = row


def first_body(own_ref, wave_ref, before_ref, after_ref, far_ref, out_ref):
    _, s = position()
    u = rows_of(own_ref, 0)
    factor = open_factor()
    v = [[x * factor for x in pair] for pair in rows_of(far_ref.at[other()], 0)]
    before = choose(s == 0, v, field_of(before_ref, 0))
    after = choose(s == NS - 1, v, field_of(after_ref, 0))
    new = smooth(u, around(u, before, after), rows_of(own_ref, 2), wave_ref[...])
    for part in range(2):
        put(out_ref, part, new[part])
        put(out_ref, 2 + part, v[part])


def other():
    g, s = position()
    return jnp.where((g % 2 == 0) == (s >= NS // 2), 1, 0)


def open_factor():
    g, s = position()
    return jnp.where((s >= NS // 2) | low_side_open(g), 1.0, 0.0)


def window_lane(shape, dim):
    cell = iota(shape, dim)
    part, inside = cell // CELLS, cell % CELLS
    return part * 64 + (inside // (4 * EDGE) + 2) * 8 + (inside % EDGE) // 4 + 2


def second_body(own_ref, wave_ref, far_ref, before_ref, after_ref, mine_ref, field_ref, sums_ref, values_ref):
    _, s = position()
    first, last = s == 0, s == NS - 1
    u = rows_of(own_ref, 0)
    far_ref = far_ref.at[other()]
    factor = open_factor()
    v = [[x * factor for x in pair] for pair in rows_of(far_ref, 0)]
    one = field_of(mine_ref, 0)
    rights = rows_of(own_ref, 2)
    wave = wave_ref[...]
    far_wave = wave_rows(far_ref[4 * PATCHES : 4 * PATCHES + 1, :LANES])
    v_before = choose(first, u, field_of(before_ref, 2))
    v_after = choose(last, u, field_of(after_ref, 2))
    v_one = smooth(v, around(v, v_before, v_after), rows_of(far_ref, 2), far_wave)
    v_one = [[x * factor for x in pair] for pair in v_one]
    before = choose(first, v_one, field_of(before_ref, 0))
    after = choose(last, v_one, field_of(after_ref, 0))
    two = smooth(one, around(one, before, after), rights, wave)
    for part in range(2):
        put(field_ref, part, two[part])
    r = residual(two, [in_plane(two[0]), in_plane(two[1])], rights, wave)
    rows = jnp.concatenate(
        [jnp.concatenate(r[0] + r[1], 1), jnp.concatenate(two[0] + two[1], 1)], 0
    )
    shape = (2 * CELLS, LANES)
    gather = jnp.where(window_lane(shape, 0) == iota(shape, 1), 1.0, 0.0)
    sums = select_lanes(rows, gather)
    lane = iota((PATCHES, LANES), 1)
    values = sums[PATCHES:]
    beside = jnp.where((s % 4 == 0) | (s % 4 == 3), 1.0, 2.0)
    sums_ref[...] = jnp.where(lane == 0, wave, sums[:PATCHES] + beside * values)
    values_ref[...] = values


def join_body(sums_ref, pair_ref, out_ref):
    _, s = position()
    core = lax.axis_index("sub") % 2
    meets = ((s % 4 == 0) | (s % 4 == 3)) & (s > 0) & (s < NS - 1)
    out_ref[...] = sums_ref[...] + (
        jnp.where(meets, pair_ref[1 - core], 0.0) + lane_roll(pair_ref[core], 4)
    )


def sides(x, patch, col):
    return (
        jnp.where(patch >= PZ, row_roll(x, PZ), 0.0),
        jnp.where(patch < PATCHES - PZ, row_roll(x, -PZ), 0.0),
        jnp.where(col > 0, row_roll(x, 1), 0.0),
        jnp.where(col < PZ - 1, row_roll(x, -1), 0.0),
    )


def windows(x):
    patch, lane = iota(x.shape, 0), iota(x.shape, 1)
    col = patch % PZ
    a, b = (lane // 8) % 8, lane % 8
    x = jnp.where((a >= 2) & (a < 6) & (b >= 2) & (b < 6), x, 0.0)
    _, _, low, high = sides(x, patch, col)
    x = x + jnp.where(b < 2, lane_roll(low, -4), 0.0) + jnp.where(b >= 6, lane_roll(high, 4), 0.0)
    low, high, _, _ = sides(x, patch, col)
    return x + jnp.where(a < 2, lane_roll(low, -32), 0.0) + jnp.where(a >= 6, lane_roll(high, 32), 0.0)


def slots_body(field_ref, own_wave_ref, slot_ref, out_ref, wave_ref, patch_ref):
    _, s = position()
    rows = [half for c in range(2) for half in halves(field_ref, c)]
    out_ref[...] = select(slot_ref[:, :PATCHES], jnp.concatenate(rows, 1))
    wave = own_wave_ref[...]
    patch, lane = iota(wave.shape, 0), iota(wave.shape, 1)
    col = patch % PZ
    a, b = (lane // 8) % 8, lane % 8
    _, _, low, high = sides(wave, patch, col)
    wave = jnp.where(b < 2, low, jnp.where(b >= 6, high, wave))
    low, high, _, _ = sides(wave, patch, col)
    wave = jnp.where(a < 2, low, jnp.where(a >= 6, high, wave))
    mine = slot_ref[pl.ds(SLOTS * device_at(s), SLOTS), :]
    wave_ref[...] = select(mine[:, :PATCHES], wave)
    index = iota(mine.shape, 1).astype(F32) + 1.0
    patch_ref[...] = jnp.broadcast_to(jnp.sum(mine * index, 1, keepdims=True) - 1.0, mine.shape)


def bundle_body(sent_ref, block_ref, far_ref, slot_ref, out_ref):
    _, s = position()
    factor = open_factor()
    far_ref = far_ref.at[other()]
    edge = jnp.where((s == 0) | (s == NS - 1), 1.0, 0.0)
    block, far_block = block_ref[...], far_ref[...]
    own = windows(block + (edge * factor) * lane_roll(far_block, -4))
    far = windows(factor * (far_block + edge * lane_roll(block, -4)))
    patch, lane = iota(far.shape, 0), iota(far.shape, 1)
    wave = jnp.broadcast_to(far_block[:, 0:1], far.shape)
    beside = (wave,) + sides(wave, patch, patch % PZ)
    for i, x in enumerate(beside):
        far = jnp.where(lane == i, x, far)
    placed = select(slot_ref[:, :PATCHES], jnp.concatenate([own, far], 1))
    for c in range(4):
        out_ref[pl.ds(c, LIVE, stride=6), :] = sent_ref[:, LANES * c : LANES * (c + 1)]
    for c in range(2):
        out_ref[pl.ds(4 + c, LIVE, stride=6), :] = placed[:, LANES * c : LANES * (c + 1)]


def coarse_sum(e):
    return (lane_roll(e, -1) + lane_roll(e, 1)) + (lane_roll(e, -8) + lane_roll(e, 8))


def correct_body(raw_ref, wave_ref, patch_ref, out_ref, grown_ref, smooth_ref):
    g, _ = position()
    odd = g % 2 == 1
    rows = 24
    shape = (SLOTS, LANES)

    def slot_rows(s, c):
        return raw_ref[pl.ds(rows * s + c, SLOTS, stride=6), :]

    def total(start, c):
        parts = [slot_rows(device_at(start + i), c) for i in range(4)]
        return ((parts[0] + parts[1]) + (parts[2] + parts[3])) * (1.0 / 64.0)

    lane = iota((LANES, LANES), 1)
    a, b = (lane // 8) % 8, lane % 8
    region = jnp.where(a < 2, 1, jnp.where(a >= 6, 2, jnp.where(b < 2, 3, jnp.where(b >= 6, 4, 0))))
    spread = jnp.where(iota((LANES, LANES), 0) == region, 1.0, 0.0)
    ends = jnp.concatenate([slot_rows(device_at(0), 5), slot_rows(device_at(NS - 1), 5)], 0)
    ends = select_lanes(ends, spread)
    low, high = ends[:SLOTS], ends[SLOTS:]
    own = wave_ref[...]
    wave = jnp.concatenate([low, low, own, own, own, own, high, high], 0)
    rhs = jnp.concatenate(
        [total(4, 5), total(0, 5)] + [total(4 * i, 4) for i in range(4)] + [total(12, 5), total(8, 5)], 0
    )
    lane = iota(shape, 1)
    a, b = (lane // 8) % 8, lane % 8
    patch = patch_ref[...].astype(jnp.int32)
    line, col = patch // PZ, patch % PZ
    y, z = 4 * line + a - 2, 4 * col + b - 2
    inside = jnp.where((y >= 0) & (y < 4 * PY) & (z >= 0) & (z < 4 * PZ), 1.0, 0.0)
    lower = jnp.where(low_side_open(g), inside, 0.0)
    inside = jnp.concatenate([lower, lower] + [inside] * 6, 0) > 0.0
    part_sign = jnp.where(iota(wave.shape, 1) < 64, -1.0, 1.0)
    real, imag = 6.0 / 16.0 - wave, shift_imag * wave
    scale = omega_coarse / (real * real + imag * imag)
    real, imag = real * scale, part_sign * imag * scale

    def divide(x):
        return jnp.where(inside, x * real + lane_roll(x, 64) * imag, 0.0)

    e = divide(rhs)
    for _ in range(2):
        beside = coarse_sum(e) + (row_roll(e, SLOTS) + row_roll(e, -SLOTS))
        e = (1.0 - omega_coarse) * e + divide(rhs + beside * (1.0 / 16.0))
    wide = (LANES, 2 * CELLS)
    widen = jnp.where(window_lane(wide, 1) == iota(wide, 0), 1.0, 0.0)
    grown_ref[...] = select_lanes(e[2 * SLOTS : 6 * SLOTS], widen)
    for i in range(EDGE):
        s = device_at(jnp.where(odd, EDGE - 1 - i, i))
        for q in range(SLOTS):
            for part in range(2):
                for h in range(2):
                    row = raw_ref[pl.ds(rows * s + 6 * q + 2 * part + h, 1), :]
                    smooth_ref[2 * q + part, i : i + 1, LANES * h : LANES * (h + 1)] = row
    for q in range(SLOTS):
        held = jnp.broadcast_to(patch_ref[q : q + 1, 0:1] >= 0.0, (4, CELLS))
        for i in range(4):
            plane = jnp.where(odd, 3 - i, i)
            line = grown_ref[pl.ds(SLOTS * plane + q, 1), :]
            for part in range(2):
                extra = jnp.broadcast_to(line[:, CELLS * part : CELLS * (part + 1)], (4, CELLS))
                value = smooth_ref[2 * q + part, 4 * i : 4 * i + 4] + extra
                out_ref[q, part, 4 * i : 4 * i + 4] = jnp.where(held, value, 0.0)


def facing(groups, reach):
    pairs, met = [], set()
    for place in [i for i in range(NS) if i < reach or i >= NS - reach]:
        s = device_at(place)
        for g in range(0 if place >= NS // 2 else 1, groups - 1, 2):
            pairs.append([g * NS + s, (g + 1) * NS + s])
            met.update(pairs[-1])
    for g in range(groups):
        rest = [g * NS + s for s in range(NS) if g * NS + s not in met]
        whole = [i for i in rest if i ^ 1 in rest]
        rest = [i for i in rest if i ^ 1 not in rest]
        pairs += [whole[i : i + 2] for i in range(0, len(whole), 2)]
        pairs += [rest[i : i + 2] for i in range(0, len(rest), 2)]
    return pairs


def body(field, source, patch_of_slot, neighbour, wave_index, wave_table):
    groups = lax.axis_size("grp")
    both = ("grp", "sub")
    up = [(i, (i + 1) % NS) for i in range(NS)]
    down = [((i + 1) % NS, i) for i in range(NS)]
    ring = lambda x: (lax.ppermute(x, "sub", up), lax.ppermute(x, "sub", down))
    plane = (PATCHES, CELLS)

    hbm = pl.BlockSpec(memory_space=pltpu.HBM)
    (packed,) = call(
        pack_body,
        [(NS, 40, LANES)],
        [
            pltpu.with_memory_space_constraint(x, pltpu.HBM)
            for x in (field, source, patch_of_slot, wave_index, wave_table)
        ],
        [
            field.shape,
            source.shape,
            pltpu.SMEM(patch_of_slot.shape, jnp.int32),
            pltpu.SMEM(wave_index.shape, jnp.int32),
            pltpu.SMEM(wave_table.shape, F32),
            pltpu.SemaphoreType.DMA((5,)),
        ],
        [hbm] * 5,
        16,
    )
    raw = lax.all_to_all(packed, "sub", 0, 0, tiled=True).reshape(NS * 40, LANES)
    row = (PATCHES, LANES)
    stacked = (4 * PATCHES + 8, CELLS)
    own, start, slot, own_wave = call(place_body, [stacked, (2,) + plane, (LIVE, LANES), row], [raw])
    far = lax.all_gather(own, both, axis_index_groups=facing(groups, 2))
    before, after = ring(start)
    (one,) = call(first_body, [(4,) + plane], [own, own_wave, before, after, far])
    before, after = ring(one)
    two, sums, values = call(
        second_body, [(2,) + plane, row, row], [own, own_wave, far, before, after, one]
    )
    chips = [[i, i + 1] for i in range(0, NS, 2)]
    pair = lax.all_gather(values, "sub", axis_index_groups=chips)
    mine = (SLOTS, LANES)
    sent, wave, patch = call(slots_body, [(LIVE, 2 * CELLS), mine, mine], [two, own_wave, slot])
    (block,) = call(join_body, [row], [sums, pair])
    far_block = lax.all_gather(block, both, axis_index_groups=facing(groups, NS // 2))
    (bundle,) = call(bundle_body, [(LIVE * 6, LANES)], [sent, block, far_block, slot])
    back = lax.all_to_all(bundle.reshape(NS, 24, LANES), "sub", 0, 0, tiled=True)
    (out,) = call(
        correct_body,
        [(SLOTS, 2, EDGE, CELLS)],
        [back.reshape(NS * 24, LANES), wave, patch],
        [(EDGE, 2 * CELLS), (2 * SLOTS, EDGE, CELLS)],
    )
    return out


def solution(mesh):
    return jax.shard_map(
        body,
        mesh=mesh,
        in_specs=(
            P(("grp", "sub"), None, None, None),
            P(("grp", "sub"), None, None, None),
            P(("grp", "sub")),
            P(("grp", "sub"), None),
            P(("grp", "sub")),
            P(),
        ),
        out_specs=P(("grp", "sub"), None, None, None),
        check_vma=False,
    )
```

```python
import jax
import jax.numpy as jnp
from jax import lax
from jax.experimental import pallas as pl
from jax.experimental.pallas import tpu as pltpu
from jax.sharding import PartitionSpec as P

PZ = 4
PY = 12
PATCHES = PY * PZ
EDGE = 16
CELLS = EDGE * EDGE
SLOTS = 4
NS = 16
LIVE = NS * SLOTS
LANES = 128

omega_fine = 0.7
omega_coarse = 0.6
shift_imag = 0.5

F32 = jnp.float32
VM = pl.BlockSpec(memory_space=pltpu.VMEM)
SM = pl.BlockSpec(memory_space=pltpu.SMEM)


def call(body, outs, ins, scratch=(), specs=None, limit=16):
    return pl.pallas_call(
        body,
        out_shape=[jax.ShapeDtypeStruct(shape, F32) for shape in outs],
        in_specs=specs or [SM if a.dtype == jnp.int32 else VM for a in ins],
        out_specs=[VM] * len(outs),
        scratch_shapes=[pltpu.VMEM(s, F32) if isinstance(s, tuple) else s for s in scratch],
        compiler_params=pltpu.CompilerParams(vmem_limit_bytes=limit << 20),
    )(*ins)


def select(picks, x):
    picks = picks.astype(jnp.bfloat16)
    out = None
    for _ in range(3):
        piece = x.astype(jnp.bfloat16)
        x = x - piece.astype(F32)
        term = jnp.dot(picks, piece, preferred_element_type=F32)
        out = term if out is None else out + term
    return out


def select_lanes(x, picks):
    picks = picks.astype(jnp.bfloat16)
    out = None
    for _ in range(3):
        piece = x.astype(jnp.bfloat16)
        x = x - piece.astype(F32)
        term = jnp.dot(piece, picks, preferred_element_type=F32)
        out = term if out is None else out + term
    return out


def iota(shape, dim):
    return lax.broadcasted_iota(jnp.int32, shape, dim)


def lane_roll(x, shift):
    return pltpu.roll(x, shift % x.shape[1], 1)


def row_roll(x, shift):
    return pltpu.roll(x, shift % x.shape[0], 0)


def in_plane(u):
    shape = u[0].shape
    lane = iota(shape, 1)
    patch = iota(shape, 0)
    k = lane % EDGE
    col = patch % PZ
    not_last, not_first = k < EDGE - 1, k > 0
    has_next, has_prev = col < PZ - 1, col > 0
    out = []
    ahead = [lane_roll(t, -EDGE) for t in u]
    behind = [lane_roll(t, EDGE) for t in u]
    low, high = lane >= EDGE, lane < LANES - EDGE
    y_next = [
        jnp.where(high, ahead[0], ahead[1]),
        jnp.where(high, ahead[1], jnp.where(patch < PATCHES - PZ, row_roll(ahead[0], -PZ), 0.0)),
    ]
    y_prev = [
        jnp.where(low, behind[0], jnp.where(patch >= PZ, row_roll(behind[1], PZ), 0.0)),
        jnp.where(low, behind[1], behind[0]),
    ]
    for h in range(2):
        t = u[h]
        z_next = jnp.where(
            not_last,
            lane_roll(t, -1),
            jnp.where(has_next, row_roll(lane_roll(t, EDGE - 1), -1), 0.0),
        )
        z_prev = jnp.where(
            not_first,
            lane_roll(t, 1),
            jnp.where(has_prev, row_roll(lane_roll(t, 1 - EDGE), 1), 0.0),
        )
        out.append((z_next + z_prev) + (y_next[h] + y_prev[h]))
    return out


def halves(ref, index):
    return [ref[index, :, :LANES], ref[index, :, LANES:]]


def put(ref, index, pair):
    ref[index, :, :LANES] = pair[0]
    ref[index, :, LANES:] = pair[1]


def field_of(ref, first):
    return [halves(ref, first), halves(ref, first + 1)]


def rows_of(ref, first):
    return [
        [ref[PATCHES * c : PATCHES * (c + 1), :LANES], ref[PATCHES * c : PATCHES * (c + 1), LANES:]]
        for c in (first, first + 1)
    ]


def wave_row(wave):
    return jnp.sum(jnp.where(iota(wave.shape, 0) == iota(wave.shape, 1), wave, 0.0), 0, keepdims=True)


def wave_rows(row):
    shape = (PATCHES, LANES)
    own = jnp.where(iota(shape, 0) == iota(shape, 1), jnp.broadcast_to(row, shape), 0.0)
    return jnp.broadcast_to(jnp.sum(own, 1, keepdims=True), shape)


def choose(flag, a, b):
    return [[jnp.where(flag, x, y) for x, y in zip(p, q)] for p, q in zip(a, b)]


def around(u, before, after):
    return [
        [n + (x + y) for n, x, y in zip(in_plane(u[part]), before[part], after[part])]
        for part in range(2)
    ]


def diagonal(wave):
    real, imag = 6.0 - wave, shift_imag * wave
    return real, imag


def smooth(u, total, rights, wave):
    real, imag = diagonal(wave)
    scale = omega_fine / (real * real + imag * imag)
    real, imag = real * scale, imag * scale
    keep = 1.0 - omega_fine
    out_re, out_im = [], []
    for h in range(2):
        a = rights[0][h] + total[0][h]
        b = rights[1][h] + total[1][h]
        out_re.append(keep * u[0][h] + (a * real - b * imag))
        out_im.append(keep * u[1][h] + (a * imag + b * real))
    return [out_re, out_im]


def residual(u, total, rights, wave):
    real, imag = diagonal(wave)
    out_re, out_im = [], []
    for h in range(2):
        out_re.append(rights[0][h] + total[0][h] - (real * u[0][h] + imag * u[1][h]))
        out_im.append(rights[1][h] + total[1][h] - (real * u[1][h] - imag * u[0][h]))
    return [out_re, out_im]


def position():
    return lax.axis_index("grp"), (lax.axis_index("sub") + NS - 1) % NS


def device_at(place):
    return (place + 1) % NS


def low_side_open(g):
    last = lax.axis_size("grp") - 1
    beyond = jnp.where(g % 2 == 0, g - 1, g + 1)
    return (beyond >= 0) & (beyond <= last)


def pack_body(
    field_hbm, source_hbm, patch_hbm, index_hbm, table_hbm, out_ref,
    field_ref, source_ref, patch_ref, index_ref, table_ref, sems,
):
    pairs = (
        (field_hbm, field_ref),
        (source_hbm, source_ref),
        (patch_hbm, patch_ref),
        (index_hbm, index_ref),
        (table_hbm, table_ref),
    )
    copies = [pltpu.make_async_copy(a, b, sems.at[i]) for i, (a, b) in enumerate(pairs)]
    for copy in copies:
        copy.start()
    for copy in copies:
        copy.wait()
    g, _ = position()
    odd = g % 2 == 1
    for q in range(SLOTS):
        patch = jnp.full((1, LANES), patch_ref[q].astype(F32), F32)
        wave = jnp.full((1, LANES), table_ref[index_ref[q]], F32)
        for s in range(NS):
            out_ref[s, 10 * q + 8 : 10 * q + 9, :] = patch
            out_ref[s, 10 * q + 9 : 10 * q + 10, :] = wave
    for s in range(NS):
        place = (s + NS - 1) % NS
        layer = jnp.where(odd, EDGE - 1 - place, place)
        for q in range(SLOTS):
            for a, ref in enumerate((field_ref, source_ref)):
                for part in range(2):
                    row = 10 * q + 4 * a + 2 * part
                    cells = ref[q, part, pl.ds(layer, 1), :]
                    out_ref[s, row : row + 1, :] = cells[:, :LANES]
                    out_ref[s, row + 1 : row + 2, :] = cells[:, LANES:]


def place_body(raw_ref, plane_ref, field_ref, slot_ref, wave_ref):
    patches = raw_ref[pl.ds(8, LIVE, stride=10), :]
    held = (patches == iota((LIVE, LANES), 1).astype(F32)).astype(F32)
    slot_ref[...] = held
    pick = held.T[:PATCHES]
    order = (0, 1, 2, 3, 4, 5, 6, 7, 9)
    rows = jnp.concatenate([raw_ref[pl.ds(c, LIVE, stride=10), :] for c in order], 1)
    placed = select(pick, rows)
    for c in range(4):
        pair = [placed[:, CELLS * c : CELLS * c + LANES], placed[:, CELLS * c + LANES : CELLS * (c + 1)]]
        plane_ref[PATCHES * c : PATCHES * (c + 1), :LANES] = pair[0]
        plane_ref[PATCHES * c : PATCHES * (c + 1), LANES:] = pair[1]
        if c < 2:
            put(field_ref, c, pair)
    wave = placed[:, 4 * CELLS :]
    wave_ref[...] = wave
    row = jnp.broadcast_to(wave_row(wave), (8, LANES))
    plane_ref[4 * PATCHES :, :LANES] = row
    plane_ref[4 * PATCHES :, LANES:] = row


def first_body(own_ref, wave_ref, before_ref, after_ref, far_ref, out_ref, up_ref, down_ref):
    _, s = position()
    u = rows_of(own_ref, 0)
    factor = open_factor()
    v = [[x * factor for x in pair] for pair in rows_of(far_ref.at[other()], 0)]
    before = choose(s == 0, v, field_of(before_ref, 0))
    after = choose(s == NS - 1, v, field_of(after_ref, 0))
    new = smooth(u, around(u, before, after), rows_of(own_ref, 2), wave_ref[...])
    real, imag = diagonal(wave_rows(far_ref[other(), 4 * PATCHES : 4 * PATCHES + 1, :LANES]))
    scale = omega_fine / (real * real + imag * imag)
    real, imag = real * scale, imag * scale
    more = [
        [a * real - b * imag for a, b in zip(v[0], v[1])],
        [a * imag + b * real for a, b in zip(v[0], v[1])],
    ]
    for part in range(2):
        put(out_ref, part, new[part])
        put(up_ref, part, [x + jnp.where(s == NS - 2, y, 0.0) for x, y in zip(new[part], more[part])])
        put(down_ref, part, [x + jnp.where(s == 1, y, 0.0) for x, y in zip(new[part], more[part])])


def other():
    g, s = position()
    return jnp.where((g % 2 == 0) == (s >= NS // 2), 1, 0)


def open_factor():
    g, s = position()
    return jnp.where((s >= NS // 2) | low_side_open(g), 1.0, 0.0)


def window_lane(shape, dim):
    cell = iota(shape, dim)
    part, inside = cell // CELLS, cell % CELLS
    return part * 64 + (inside // (4 * EDGE) + 2) * 8 + (inside % EDGE) // 4 + 2


def second_body(own_ref, wave_ref, far_ref, before_ref, after_ref, mine_ref, field_ref, sums_ref, values_ref):
    _, s = position()
    first, last = s == 0, s == NS - 1
    u = rows_of(own_ref, 0)
    far_ref = far_ref.at[other()]
    factor = open_factor()
    v = [[x * factor for x in pair] for pair in rows_of(far_ref, 0)]
    one = field_of(mine_ref, 0)
    rights = rows_of(own_ref, 2)
    wave = wave_ref[...]
    far_wave = wave_rows(far_ref[4 * PATCHES : 4 * PATCHES + 1, :LANES])
    v_one = smooth(v, [[x + y for x, y in zip(in_plane(p), q)] for p, q in zip(v, u)], rows_of(far_ref, 2), far_wave)
    v_one = [[x * factor for x in pair] for pair in v_one]
    before = choose(first, v_one, field_of(before_ref, 0))
    after = choose(last, v_one, field_of(after_ref, 0))
    two = smooth(one, around(one, before, after), rights, wave)
    for part in range(2):
        put(field_ref, part, two[part])
    r = residual(two, [in_plane(two[0]), in_plane(two[1])], rights, wave)
    rows = jnp.concatenate(
        [jnp.concatenate(r[0] + r[1], 1), jnp.concatenate(two[0] + two[1], 1)], 0
    )
    shape = (2 * CELLS, LANES)
    gather = jnp.where(window_lane(shape, 0) == iota(shape, 1), 1.0, 0.0)
    sums = select_lanes(rows, gather)
    lane = iota((PATCHES, LANES), 1)
    values = sums[PATCHES:]
    beside = jnp.where((s % 4 == 0) | (s % 4 == 3), 1.0, 2.0)
    sums_ref[...] = jnp.where(lane == 0, wave, sums[:PATCHES] + beside * values)
    values_ref[...] = values


def join_body(sums_ref, pair_ref, out_ref):
    _, s = position()
    core = lax.axis_index("sub") % 2
    meets = ((s % 4 == 0) | (s % 4 == 3)) & (s > 0) & (s < NS - 1)
    out_ref[...] = sums_ref[...] + (
        jnp.where(meets, pair_ref[1 - core], 0.0) + lane_roll(pair_ref[core], 4)
    )


def sides(x, patch, col):
    return (
        jnp.where(patch >= PZ, row_roll(x, PZ), 0.0),
        jnp.where(patch < PATCHES - PZ, row_roll(x, -PZ), 0.0),
        jnp.where(col > 0, row_roll(x, 1), 0.0),
        jnp.where(col < PZ - 1, row_roll(x, -1), 0.0),
    )


def windows(x):
    patch, lane = iota(x.shape, 0), iota(x.shape, 1)
    col = patch % PZ
    a, b = (lane // 8) % 8, lane % 8
    x = jnp.where((a >= 2) & (a < 6) & (b >= 2) & (b < 6), x, 0.0)
    _, _, low, high = sides(x, patch, col)
    x = x + jnp.where(b < 2, lane_roll(low, -4), 0.0) + jnp.where(b >= 6, lane_roll(high, 4), 0.0)
    low, high, _, _ = sides(x, patch, col)
    return x + jnp.where(a < 2, lane_roll(low, -32), 0.0) + jnp.where(a >= 6, lane_roll(high, 32), 0.0)


def slots_body(field_ref, own_wave_ref, slot_ref, out_ref, wave_ref, patch_ref):
    _, s = position()
    rows = [half for c in range(2) for half in halves(field_ref, c)]
    out_ref[...] = select(slot_ref[:, :PATCHES], jnp.concatenate(rows, 1))
    wave = own_wave_ref[...]
    patch, lane = iota(wave.shape, 0), iota(wave.shape, 1)
    col = patch % PZ
    a, b = (lane // 8) % 8, lane % 8
    _, _, low, high = sides(wave, patch, col)
    wave = jnp.where(b < 2, low, jnp.where(b >= 6, high, wave))
    low, high, _, _ = sides(wave, patch, col)
    wave = jnp.where(a < 2, low, jnp.where(a >= 6, high, wave))
    mine = slot_ref[pl.ds(SLOTS * device_at(s), SLOTS), :]
    wave_ref[...] = select(mine[:, :PATCHES], wave)
    index = iota(mine.shape, 1).astype(F32) + 1.0
    patch_ref[...] = jnp.broadcast_to(jnp.sum(mine * index, 1, keepdims=True) - 1.0, mine.shape)


def bundle_body(sent_ref, block_ref, far_ref, slot_ref, out_ref):
    _, s = position()
    factor = open_factor()
    far_ref = far_ref.at[other()]
    edge = jnp.where((s == 0) | (s == NS - 1), 1.0, 0.0)
    block, far_block = block_ref[...], far_ref[...]
    own = windows(block + (edge * factor) * lane_roll(far_block, -4))
    far = windows(factor * (far_block + edge * lane_roll(block, -4)))
    patch, lane = iota(far.shape, 0), iota(far.shape, 1)
    wave = jnp.broadcast_to(far_block[:, 0:1], far.shape)
    beside = (wave,) + sides(wave, patch, patch % PZ)
    for i, x in enumerate(beside):
        far = jnp.where(lane == i, x, far)
    placed = select(slot_ref[:, :PATCHES], jnp.concatenate([own, far], 1))
    for c in range(4):
        out_ref[pl.ds(c, LIVE, stride=6), :] = sent_ref[:, LANES * c : LANES * (c + 1)]
    for c in range(2):
        out_ref[pl.ds(4 + c, LIVE, stride=6), :] = placed[:, LANES * c : LANES * (c + 1)]


def coarse_sum(e):
    return (lane_roll(e, -1) + lane_roll(e, 1)) + (lane_roll(e, -8) + lane_roll(e, 8))


def correct_body(raw_ref, wave_ref, patch_ref, out_ref, grown_ref, smooth_ref):
    g, _ = position()
    odd = g % 2 == 1
    rows = 24
    shape = (SLOTS, LANES)

    def slot_rows(s, c):
        return raw_ref[pl.ds(rows * s + c, SLOTS, stride=6), :]

    def total(start, c):
        parts = [slot_rows(device_at(start + i), c) for i in range(4)]
        return ((parts[0] + parts[1]) + (parts[2] + parts[3])) * (1.0 / 64.0)

    lane = iota((LANES, LANES), 1)
    a, b = (lane // 8) % 8, lane % 8
    region = jnp.where(a < 2, 1, jnp.where(a >= 6, 2, jnp.where(b < 2, 3, jnp.where(b >= 6, 4, 0))))
    spread = jnp.where(iota((LANES, LANES), 0) == region, 1.0, 0.0)
    ends = jnp.concatenate([slot_rows(device_at(0), 5), slot_rows(device_at(NS - 1), 5)], 0)
    ends = select_lanes(ends, spread)
    low, high = ends[:SLOTS], ends[SLOTS:]
    own = wave_ref[...]
    wave = jnp.concatenate([low, low, own, own, own, own, high, high], 0)
    rhs = jnp.concatenate(
        [total(4, 5), total(0, 5)] + [total(4 * i, 4) for i in range(4)] + [total(12, 5), total(8, 5)], 0
    )
    lane = iota(shape, 1)
    a, b = (lane // 8) % 8, lane % 8
    patch = patch_ref[...].astype(jnp.int32)
    line, col = patch // PZ, patch % PZ
    y, z = 4 * line + a - 2, 4 * col + b - 2
    inside = jnp.where((y >= 0) & (y < 4 * PY) & (z >= 0) & (z < 4 * PZ), 1.0, 0.0)
    lower = jnp.where(low_side_open(g), inside, 0.0)
    inside = jnp.concatenate([lower, lower] + [inside] * 6, 0) > 0.0
    part_sign = jnp.where(iota(wave.shape, 1) < 64, -1.0, 1.0)
    real, imag = 6.0 / 16.0 - wave, shift_imag * wave
    scale = omega_coarse / (real * real + imag * imag)
    real, imag = real * scale, part_sign * imag * scale

    def divide(x):
        return jnp.where(inside, x * real + lane_roll(x, 64) * imag, 0.0)

    e = divide(rhs)
    for _ in range(2):
        beside = coarse_sum(e) + (row_roll(e, SLOTS) + row_roll(e, -SLOTS))
        e = (1.0 - omega_coarse) * e + divide(rhs + beside * (1.0 / 16.0))
    wide = (LANES, 2 * CELLS)
    widen = jnp.where(window_lane(wide, 1) == iota(wide, 0), 1.0, 0.0)
    grown_ref[...] = select_lanes(e[2 * SLOTS : 6 * SLOTS], widen)
    for i in range(EDGE):
        s = device_at(jnp.where(odd, EDGE - 1 - i, i))
        for q in range(SLOTS):
            for part in range(2):
                for h in range(2):
                    row = raw_ref[pl.ds(rows * s + 6 * q + 2 * part + h, 1), :]
                    smooth_ref[2 * q + part, i : i + 1, LANES * h : LANES * (h + 1)] = row
    for q in range(SLOTS):
        held = jnp.broadcast_to(patch_ref[q : q + 1, 0:1] >= 0.0, (4, CELLS))
        for i in range(4):
            plane = jnp.where(odd, 3 - i, i)
            line = grown_ref[pl.ds(SLOTS * plane + q, 1), :]
            for part in range(2):
                extra = jnp.broadcast_to(line[:, CELLS * part : CELLS * (part + 1)], (4, CELLS))
                value = smooth_ref[2 * q + part, 4 * i : 4 * i + 4] + extra
                out_ref[q, part, 4 * i : 4 * i + 4] = jnp.where(held, value, 0.0)


def facing(groups, reach):
    pairs, met = [], set()
    for place in [i for i in range(NS) if i < reach or i >= NS - reach]:
        s = device_at(place)
        for g in range(0 if place >= NS // 2 else 1, groups - 1, 2):
            pairs.append([g * NS + s, (g + 1) * NS + s])
            met.update(pairs[-1])
    for g in range(groups):
        rest = [g * NS + s for s in range(NS) if g * NS + s not in met]
        whole = [i for i in rest if i ^ 1 in rest]
        rest = [i for i in rest if i ^ 1 not in rest]
        pairs += [whole[i : i + 2] for i in range(0, len(whole), 2)]
        pairs += [rest[i : i + 2] for i in range(0, len(rest), 2)]
    return pairs


def body(field, source, patch_of_slot, neighbour, wave_index, wave_table):
    groups = lax.axis_size("grp")
    both = ("grp", "sub")
    up = [(i, (i + 1) % NS) for i in range(NS)]
    down = [((i + 1) % NS, i) for i in range(NS)]
    ring = lambda x: (lax.ppermute(x, "sub", up), lax.ppermute(x, "sub", down))
    plane = (PATCHES, CELLS)

    hbm = pl.BlockSpec(memory_space=pltpu.HBM)
    (packed,) = call(
        pack_body,
        [(NS, 40, LANES)],
        [
            pltpu.with_memory_space_constraint(x, pltpu.HBM)
            for x in (field, source, patch_of_slot, wave_index, wave_table)
        ],
        [
            field.shape,
            source.shape,
            pltpu.SMEM(patch_of_slot.shape, jnp.int32),
            pltpu.SMEM(wave_index.shape, jnp.int32),
            pltpu.SMEM(wave_table.shape, F32),
            pltpu.SemaphoreType.DMA((5,)),
        ],
        [hbm] * 5,
        16,
    )
    raw = lax.all_to_all(packed, "sub", 0, 0, tiled=True).reshape(NS * 40, LANES)
    row = (PATCHES, LANES)
    stacked = (4 * PATCHES + 8, CELLS)
    own, start, slot, own_wave = call(place_body, [stacked, (2,) + plane, (LIVE, LANES), row], [raw])
    far = lax.all_gather(own, both, axis_index_groups=facing(groups, 2))
    before, after = ring(start)
    one, rising, falling = call(
        first_body, [(2,) + plane] * 3, [own, own_wave, before, after, far]
    )
    before = lax.ppermute(rising, "sub", up)
    after = lax.ppermute(falling, "sub", down)
    two, sums, values = call(
        second_body, [(2,) + plane, row, row], [own, own_wave, far, before, after, one]
    )
    chips = [[i, i + 1] for i in range(0, NS, 2)]
    pair = lax.all_gather(values, "sub", axis_index_groups=chips)
    mine = (SLOTS, LANES)
    sent, wave, patch = call(slots_body, [(LIVE, 2 * CELLS), mine, mine], [two, own_wave, slot])
    (block,) = call(join_body, [row], [sums, pair])
    far_block = lax.all_gather(block, both, axis_index_groups=facing(groups, NS // 2))
    (bundle,) = call(bundle_body, [(LIVE * 6, LANES)], [sent, block, far_block, slot])
    back = lax.all_to_all(bundle.reshape(NS, 24, LANES), "sub", 0, 0, tiled=True)
    (out,) = call(
        correct_body,
        [(SLOTS, 2, EDGE, CELLS)],
        [back.reshape(NS * 24, LANES), wave, patch],
        [(EDGE, 2 * CELLS), (2 * SLOTS, EDGE, CELLS)],
    )
    return out


def solution(mesh):
    return jax.shard_map(
        body,
        mesh=mesh,
        in_specs=(
            P(("grp", "sub"), None, None, None),
            P(("grp", "sub"), None, None, None),
            P(("grp", "sub")),
            P(("grp", "sub"), None),
            P(("grp", "sub")),
            P(),
        ),
        out_specs=P(("grp", "sub"), None, None, None),
        check_vma=False,
    )
```

```python
import jax
import jax.numpy as jnp
from jax import lax
from jax.experimental import pallas as pl
from jax.experimental.pallas import tpu as pltpu
from jax.sharding import PartitionSpec as P

PZ = 4
PY = 12
PATCHES = PY * PZ
EDGE = 16
CELLS = EDGE * EDGE
SLOTS = 4
NS = 16
LIVE = NS * SLOTS
LANES = 128

omega_fine = 0.7
omega_coarse = 0.6
shift_imag = 0.5

F32 = jnp.float32
VM = pl.BlockSpec(memory_space=pltpu.VMEM)
SM = pl.BlockSpec(memory_space=pltpu.SMEM)


def call(body, outs, ins, scratch=(), specs=None, limit=16):
    return pl.pallas_call(
        body,
        out_shape=[jax.ShapeDtypeStruct(shape, F32) for shape in outs],
        in_specs=specs or [SM if a.dtype == jnp.int32 else VM for a in ins],
        out_specs=[VM] * len(outs),
        scratch_shapes=[pltpu.VMEM(s, F32) if isinstance(s, tuple) else s for s in scratch],
        compiler_params=pltpu.CompilerParams(vmem_limit_bytes=limit << 20),
    )(*ins)


def select(picks, x):
    picks = picks.astype(jnp.bfloat16)
    out = None
    for _ in range(3):
        piece = x.astype(jnp.bfloat16)
        x = x - piece.astype(F32)
        term = jnp.dot(picks, piece, preferred_element_type=F32)
        out = term if out is None else out + term
    return out


def select_lanes(x, picks):
    picks = picks.astype(jnp.bfloat16)
    out = None
    for _ in range(3):
        piece = x.astype(jnp.bfloat16)
        x = x - piece.astype(F32)
        term = jnp.dot(piece, picks, preferred_element_type=F32)
        out = term if out is None else out + term
    return out


def iota(shape, dim):
    return lax.broadcasted_iota(jnp.int32, shape, dim)


def lane_roll(x, shift):
    return pltpu.roll(x, shift % x.shape[1], 1)


def row_roll(x, shift):
    return pltpu.roll(x, shift % x.shape[0], 0)


def in_plane(u):
    shape = u[0].shape
    lane = iota(shape, 1)
    patch = iota(shape, 0)
    k = lane % EDGE
    col = patch % PZ
    not_last, not_first = k < EDGE - 1, k > 0
    has_next, has_prev = col < PZ - 1, col > 0
    out = []
    ahead = [lane_roll(t, -EDGE) for t in u]
    behind = [lane_roll(t, EDGE) for t in u]
    low, high = lane >= EDGE, lane < LANES - EDGE
    y_next = [
        jnp.where(high, ahead[0], ahead[1]),
        jnp.where(high, ahead[1], jnp.where(patch < PATCHES - PZ, row_roll(ahead[0], -PZ), 0.0)),
    ]
    y_prev = [
        jnp.where(low, behind[0], jnp.where(patch >= PZ, row_roll(behind[1], PZ), 0.0)),
        jnp.where(low, behind[1], behind[0]),
    ]
    for h in range(2):
        t = u[h]
        z_next = jnp.where(
            not_last,
            lane_roll(t, -1),
            jnp.where(has_next, row_roll(lane_roll(t, EDGE - 1), -1), 0.0),
        )
        z_prev = jnp.where(
            not_first,
            lane_roll(t, 1),
            jnp.where(has_prev, row_roll(lane_roll(t, 1 - EDGE), 1), 0.0),
        )
        out.append((z_next + z_prev) + (y_next[h] + y_prev[h]))
    return out


def halves(ref, index):
    return [ref[index, :, :LANES], ref[index, :, LANES:]]


def put(ref, index, pair):
    ref[index, :, :LANES] = pair[0]
    ref[index, :, LANES:] = pair[1]


def field_of(ref, first):
    return [halves(ref, first), halves(ref, first + 1)]


def rows_of(ref, first):
    return [
        [ref[PATCHES * c : PATCHES * (c + 1), :LANES], ref[PATCHES * c : PATCHES * (c + 1), LANES:]]
        for c in (first, first + 1)
    ]


def wave_row(wave):
    return jnp.sum(jnp.where(iota(wave.shape, 0) == iota(wave.shape, 1), wave, 0.0), 0, keepdims=True)


def wave_rows(row):
    shape = (PATCHES, LANES)
    own = jnp.where(iota(shape, 0) == iota(shape, 1), jnp.broadcast_to(row, shape), 0.0)
    return jnp.broadcast_to(jnp.sum(own, 1, keepdims=True), shape)


def choose(flag, a, b):
    return [[jnp.where(flag, x, y) for x, y in zip(p, q)] for p, q in zip(a, b)]


def around(u, before, after):
    return [
        [n + (x + y) for n, x, y in zip(in_plane(u[part]), before[part], after[part])]
        for part in range(2)
    ]


def diagonal(wave):
    real, imag = 6.0 - wave, shift_imag * wave
    return real, imag


def smooth(u, total, rights, wave):
    real, imag = diagonal(wave)
    scale = omega_fine / (real * real + imag * imag)
    real, imag = real * scale, imag * scale
    keep = 1.0 - omega_fine
    out_re, out_im = [], []
    for h in range(2):
        a = rights[0][h] + total[0][h]
        b = rights[1][h] + total[1][h]
        out_re.append(keep * u[0][h] + (a * real - b * imag))
        out_im.append(keep * u[1][h] + (a * imag + b * real))
    return [out_re, out_im]


def residual(u, total, rights, wave):
    real, imag = diagonal(wave)
    out_re, out_im = [], []
    for h in range(2):
        out_re.append(rights[0][h] + total[0][h] - (real * u[0][h] + imag * u[1][h]))
        out_im.append(rights[1][h] + total[1][h] - (real * u[1][h] - imag * u[0][h]))
    return [out_re, out_im]


def position():
    return lax.axis_index("grp"), (lax.axis_index("sub") + NS - 1) % NS


def device_at(place):
    return (place + 1) % NS


def low_side_open(g):
    last = lax.axis_size("grp") - 1
    beyond = jnp.where(g % 2 == 0, g - 1, g + 1)
    return (beyond >= 0) & (beyond <= last)


def pack_body(
    field_hbm, source_hbm, patch_hbm, index_hbm, table_hbm, out_ref,
    field_ref, source_ref, patch_ref, index_ref, table_ref, sems,
):
    pairs = (
        (field_hbm, field_ref),
        (source_hbm, source_ref),
        (patch_hbm, patch_ref),
        (index_hbm, index_ref),
        (table_hbm, table_ref),
    )
    copies = [pltpu.make_async_copy(a, b, sems.at[i]) for i, (a, b) in enumerate(pairs)]
    for copy in copies:
        copy.start()
    for copy in copies:
        copy.wait()
    g, _ = position()
    odd = g % 2 == 1
    for q in range(SLOTS):
        patch = jnp.full((1, LANES), patch_ref[q].astype(F32), F32)
        wave = jnp.full((1, LANES), table_ref[index_ref[q]], F32)
        for s in range(NS):
            out_ref[s, 10 * q + 8 : 10 * q + 9, :] = patch
            out_ref[s, 10 * q + 9 : 10 * q + 10, :] = wave
    for s in range(NS):
        place = (s + NS - 1) % NS
        layer = jnp.where(odd, EDGE - 1 - place, place)
        for q in range(SLOTS):
            for a, ref in enumerate((field_ref, source_ref)):
                for part in range(2):
                    row = 10 * q + 4 * a + 2 * part
                    cells = ref[q, part, pl.ds(layer, 1), :]
                    out_ref[s, row : row + 1, :] = cells[:, :LANES]
                    out_ref[s, row + 1 : row + 2, :] = cells[:, LANES:]


def place_body(raw_ref, plane_ref, field_ref, slot_ref, wave_ref):
    patches = raw_ref[pl.ds(8, LIVE, stride=10), :]
    held = (patches == iota((LIVE, LANES), 1).astype(F32)).astype(F32)
    slot_ref[...] = held
    pick = held.T[:PATCHES]
    order = (0, 1, 2, 3, 4, 5, 6, 7, 9)
    rows = jnp.concatenate([raw_ref[pl.ds(c, LIVE, stride=10), :] for c in order], 1)
    placed = select(pick, rows)
    for c in range(4):
        pair = [placed[:, CELLS * c : CELLS * c + LANES], placed[:, CELLS * c + LANES : CELLS * (c + 1)]]
        plane_ref[PATCHES * c : PATCHES * (c + 1), :LANES] = pair[0]
        plane_ref[PATCHES * c : PATCHES * (c + 1), LANES:] = pair[1]
        if c < 2:
            put(field_ref, c, pair)
    wave = placed[:, 4 * CELLS :]
    wave_ref[...] = wave
    row = jnp.broadcast_to(wave_row(wave), (8, LANES))
    plane_ref[4 * PATCHES :, :LANES] = row
    plane_ref[4 * PATCHES :, LANES:] = row


def first_body(own_ref, wave_ref, before_ref, after_ref, far_ref, out_ref, up_ref, down_ref):
    _, s = position()
    u = rows_of(own_ref, 0)
    factor = open_factor()
    v = [[x * factor for x in pair] for pair in rows_of(far_ref.at[other()], 0)]
    before = choose(s == 0, v, field_of(before_ref, 0))
    after = choose(s == NS - 1, v, field_of(after_ref, 0))
    new = smooth(u, around(u, before, after), rows_of(own_ref, 2), wave_ref[...])
    real, imag = diagonal(wave_rows(far_ref[other(), 4 * PATCHES : 4 * PATCHES + 1, :LANES]))
    scale = omega_fine / (real * real + imag * imag)
    real, imag = real * scale, imag * scale
    more = [
        [a * real - b * imag for a, b in zip(v[0], v[1])],
        [a * imag + b * real for a, b in zip(v[0], v[1])],
    ]
    for part in range(2):
        put(out_ref, part, new[part])
        put(up_ref, part, [x + jnp.where(s == NS - 2, y, 0.0) for x, y in zip(new[part], more[part])])
        put(down_ref, part, [x + jnp.where(s == 1, y, 0.0) for x, y in zip(new[part], more[part])])


def other():
    g, s = position()
    return jnp.where((g % 2 == 0) == (s >= NS // 2), 1, 0)


def open_factor():
    g, s = position()
    return jnp.where((s >= NS // 2) | low_side_open(g), 1.0, 0.0)


def window_lane(shape, dim):
    cell = iota(shape, dim)
    part, inside = cell // CELLS, cell % CELLS
    return part * 64 + (inside // (4 * EDGE) + 2) * 8 + (inside % EDGE) // 4 + 2


def second_body(own_ref, wave_ref, far_ref, before_ref, after_ref, mine_ref, field_ref, sums_ref, values_ref):
    _, s = position()
    first, last = s == 0, s == NS - 1
    u = rows_of(own_ref, 0)
    far_ref = far_ref.at[other()]
    factor = open_factor()
    v = [[x * factor for x in pair] for pair in rows_of(far_ref, 0)]
    one = field_of(mine_ref, 0)
    rights = rows_of(own_ref, 2)
    wave = wave_ref[...]
    far_wave = wave_rows(far_ref[4 * PATCHES : 4 * PATCHES + 1, :LANES])
    v_one = smooth(v, [[x + y for x, y in zip(in_plane(p), q)] for p, q in zip(v, u)], rows_of(far_ref, 2), far_wave)
    v_one = [[x * factor for x in pair] for pair in v_one]
    before = choose(first, v_one, field_of(before_ref, 0))
    after = choose(last, v_one, field_of(after_ref, 0))
    two = smooth(one, around(one, before, after), rights, wave)
    for part in range(2):
        put(field_ref, part, two[part])
    r = residual(two, [in_plane(two[0]), in_plane(two[1])], rights, wave)
    rows = jnp.concatenate(
        [jnp.concatenate(r[0] + r[1], 1), jnp.concatenate(two[0] + two[1], 1)], 0
    )
    shape = (2 * CELLS, LANES)
    gather = jnp.where(window_lane(shape, 0) == iota(shape, 1), 1.0, 0.0)
    sums = select_lanes(rows, gather)
    lane = iota((PATCHES, LANES), 1)
    values = sums[PATCHES:]
    beside = jnp.where((s % 4 == 0) | (s % 4 == 3), 1.0, 2.0)
    sums_ref[...] = jnp.where(lane == 0, wave, sums[:PATCHES] + beside * values)
    values_ref[...] = values


def join_body(sums_ref, values_ref, pair_ref, out_ref):
    out_ref[...] = sums_ref[...] + (pair_ref[...] + lane_roll(values_ref[...], 4))


def sides(x, patch, col):
    return (
        jnp.where(patch >= PZ, row_roll(x, PZ), 0.0),
        jnp.where(patch < PATCHES - PZ, row_roll(x, -PZ), 0.0),
        jnp.where(col > 0, row_roll(x, 1), 0.0),
        jnp.where(col < PZ - 1, row_roll(x, -1), 0.0),
    )


def windows(x):
    patch, lane = iota(x.shape, 0), iota(x.shape, 1)
    col = patch % PZ
    a, b = (lane // 8) % 8, lane % 8
    x = jnp.where((a >= 2) & (a < 6) & (b >= 2) & (b < 6), x, 0.0)
    _, _, low, high = sides(x, patch, col)
    x = x + jnp.where(b < 2, lane_roll(low, -4), 0.0) + jnp.where(b >= 6, lane_roll(high, 4), 0.0)
    low, high, _, _ = sides(x, patch, col)
    return x + jnp.where(a < 2, lane_roll(low, -32), 0.0) + jnp.where(a >= 6, lane_roll(high, 32), 0.0)


def slots_body(field_ref, own_wave_ref, slot_ref, out_ref, wave_ref, patch_ref):
    _, s = position()
    rows = [half for c in range(2) for half in halves(field_ref, c)]
    out_ref[...] = select(slot_ref[:, :PATCHES], jnp.concatenate(rows, 1))
    wave = own_wave_ref[...]
    patch, lane = iota(wave.shape, 0), iota(wave.shape, 1)
    col = patch % PZ
    a, b = (lane // 8) % 8, lane % 8
    _, _, low, high = sides(wave, patch, col)
    wave = jnp.where(b < 2, low, jnp.where(b >= 6, high, wave))
    low, high, _, _ = sides(wave, patch, col)
    wave = jnp.where(a < 2, low, jnp.where(a >= 6, high, wave))
    mine = slot_ref[pl.ds(SLOTS * device_at(s), SLOTS), :]
    wave_ref[...] = select(mine[:, :PATCHES], wave)
    index = iota(mine.shape, 1).astype(F32) + 1.0
    patch_ref[...] = jnp.broadcast_to(jnp.sum(mine * index, 1, keepdims=True) - 1.0, mine.shape)


def bundle_body(sent_ref, block_ref, far_ref, slot_ref, out_ref):
    _, s = position()
    factor = open_factor()
    far_ref = far_ref.at[other()]
    edge = jnp.where((s == 0) | (s == NS - 1), 1.0, 0.0)
    block, far_block = block_ref[...], far_ref[...]
    own = windows(block + (edge * factor) * lane_roll(far_block, -4))
    far = windows(factor * (far_block + edge * lane_roll(block, -4)))
    patch, lane = iota(far.shape, 0), iota(far.shape, 1)
    wave = jnp.broadcast_to(far_block[:, 0:1], far.shape)
    beside = (wave,) + sides(wave, patch, patch % PZ)
    for i, x in enumerate(beside):
        far = jnp.where(lane == i, x, far)
    placed = select(slot_ref[:, :PATCHES], jnp.concatenate([own, far], 1))
    for c in range(4):
        out_ref[pl.ds(c, LIVE, stride=6), :] = sent_ref[:, LANES * c : LANES * (c + 1)]
    for c in range(2):
        out_ref[pl.ds(4 + c, LIVE, stride=6), :] = placed[:, LANES * c : LANES * (c + 1)]


def coarse_sum(e):
    return (lane_roll(e, -1) + lane_roll(e, 1)) + (lane_roll(e, -8) + lane_roll(e, 8))


def correct_body(raw_ref, wave_ref, patch_ref, out_ref, grown_ref, smooth_ref):
    g, _ = position()
    odd = g % 2 == 1
    rows = 24
    shape = (SLOTS, LANES)

    def slot_rows(s, c):
        return raw_ref[pl.ds(rows * s + c, SLOTS, stride=6), :]

    def total(start, c):
        parts = [slot_rows(device_at(start + i), c) for i in range(4)]
        return ((parts[0] + parts[1]) + (parts[2] + parts[3])) * (1.0 / 64.0)

    lane = iota((LANES, LANES), 1)
    a, b = (lane // 8) % 8, lane % 8
    region = jnp.where(a < 2, 1, jnp.where(a >= 6, 2, jnp.where(b < 2, 3, jnp.where(b >= 6, 4, 0))))
    spread = jnp.where(iota((LANES, LANES), 0) == region, 1.0, 0.0)
    ends = jnp.concatenate([slot_rows(device_at(0), 5), slot_rows(device_at(NS - 1), 5)], 0)
    ends = select_lanes(ends, spread)
    low, high = ends[:SLOTS], ends[SLOTS:]
    own = wave_ref[...]
    wave = jnp.concatenate([low, low, own, own, own, own, high, high], 0)
    rhs = jnp.concatenate(
        [total(4, 5), total(0, 5)] + [total(4 * i, 4) for i in range(4)] + [total(12, 5), total(8, 5)], 0
    )
    lane = iota(shape, 1)
    a, b = (lane // 8) % 8, lane % 8
    patch = patch_ref[...].astype(jnp.int32)
    line, col = patch // PZ, patch % PZ
    y, z = 4 * line + a - 2, 4 * col + b - 2
    inside = jnp.where((y >= 0) & (y < 4 * PY) & (z >= 0) & (z < 4 * PZ), 1.0, 0.0)
    lower = jnp.where(low_side_open(g), inside, 0.0)
    inside = jnp.concatenate([lower, lower] + [inside] * 6, 0) > 0.0
    part_sign = jnp.where(iota(wave.shape, 1) < 64, -1.0, 1.0)
    real, imag = 6.0 / 16.0 - wave, shift_imag * wave
    scale = omega_coarse / (real * real + imag * imag)
    real, imag = real * scale, part_sign * imag * scale

    def divide(x):
        return jnp.where(inside, x * real + lane_roll(x, 64) * imag, 0.0)

    e = divide(rhs)
    for _ in range(2):
        beside = coarse_sum(e) + (row_roll(e, SLOTS) + row_roll(e, -SLOTS))
        e = (1.0 - omega_coarse) * e + divide(rhs + beside * (1.0 / 16.0))
    wide = (LANES, 2 * CELLS)
    widen = jnp.where(window_lane(wide, 1) == iota(wide, 0), 1.0, 0.0)
    grown_ref[...] = select_lanes(e[2 * SLOTS : 6 * SLOTS], widen)
    for i in range(EDGE):
        s = device_at(jnp.where(odd, EDGE - 1 - i, i))
        for q in range(SLOTS):
            for part in range(2):
                for h in range(2):
                    row = raw_ref[pl.ds(rows * s + 6 * q + 2 * part + h, 1), :]
                    smooth_ref[2 * q + part, i : i + 1, LANES * h : LANES * (h + 1)] = row
    for q in range(SLOTS):
        held = jnp.broadcast_to(patch_ref[q : q + 1, 0:1] >= 0.0, (4, CELLS))
        for i in range(4):
            plane = jnp.where(odd, 3 - i, i)
            line = grown_ref[pl.ds(SLOTS * plane + q, 1), :]
            for part in range(2):
                extra = jnp.broadcast_to(line[:, CELLS * part : CELLS * (part + 1)], (4, CELLS))
                value = smooth_ref[2 * q + part, 4 * i : 4 * i + 4] + extra
                out_ref[q, part, 4 * i : 4 * i + 4] = jnp.where(held, value, 0.0)


def facing(groups, reach):
    pairs, met = [], set()
    for place in [i for i in range(NS) if i < reach or i >= NS - reach]:
        s = device_at(place)
        for g in range(0 if place >= NS // 2 else 1, groups - 1, 2):
            pairs.append([g * NS + s, (g + 1) * NS + s])
            met.update(pairs[-1])
    for g in range(groups):
        rest = [g * NS + s for s in range(NS) if g * NS + s not in met]
        whole = [i for i in rest if i ^ 1 in rest and 2 * reach < NS]
        rest = [i for i in rest if i not in whole]
        pairs += [whole[i : i + 2] for i in range(0, len(whole), 2)]
        pairs += [rest[i : i + 2] for i in range(0, len(rest), 2)]
    return pairs


def body(field, source, patch_of_slot, neighbour, wave_index, wave_table):
    groups = lax.axis_size("grp")
    both = ("grp", "sub")
    up = [(i, (i + 1) % NS) for i in range(NS)]
    down = [((i + 1) % NS, i) for i in range(NS)]
    ring = lambda x: (lax.ppermute(x, "sub", up), lax.ppermute(x, "sub", down))
    plane = (PATCHES, CELLS)

    hbm = pl.BlockSpec(memory_space=pltpu.HBM)
    (packed,) = call(
        pack_body,
        [(NS, 40, LANES)],
        [
            pltpu.with_memory_space_constraint(x, pltpu.HBM)
            for x in (field, source, patch_of_slot, wave_index, wave_table)
        ],
        [
            field.shape,
            source.shape,
            pltpu.SMEM(patch_of_slot.shape, jnp.int32),
            pltpu.SMEM(wave_index.shape, jnp.int32),
            pltpu.SMEM(wave_table.shape, F32),
            pltpu.SemaphoreType.DMA((5,)),
        ],
        [hbm] * 5,
        16,
    )
    raw = lax.all_to_all(packed, "sub", 0, 0, tiled=True).reshape(NS * 40, LANES)
    row = (PATCHES, LANES)
    stacked = (4 * PATCHES + 8, CELLS)
    own, start, slot, own_wave = call(place_body, [stacked, (2,) + plane, (LIVE, LANES), row], [raw])
    far = lax.all_gather(own, both, axis_index_groups=facing(groups, 2))
    before, after = ring(start)
    one, rising, falling = call(
        first_body, [(2,) + plane] * 3, [own, own_wave, before, after, far]
    )
    before = lax.ppermute(rising, "sub", up)
    after = lax.ppermute(falling, "sub", down)
    two, sums, values = call(
        second_body, [(2,) + plane, row, row], [own, own_wave, far, before, after, one]
    )
    edges = [device_at(4 * i + 3) for i in range(NS // 4 - 1)]
    pair = lax.ppermute(values, "sub", [(i, i + 1) for i in edges] + [(i + 1, i) for i in edges])
    mine = (SLOTS, LANES)
    sent, wave, patch = call(slots_body, [(LIVE, 2 * CELLS), mine, mine], [two, own_wave, slot])
    (block,) = call(join_body, [row], [sums, values, pair])
    far_block = lax.all_gather(block, both, axis_index_groups=facing(groups, NS // 2))
    (bundle,) = call(bundle_body, [(LIVE * 6, LANES)], [sent, block, far_block, slot])
    back = lax.all_to_all(bundle.reshape(NS, 24, LANES), "sub", 0, 0, tiled=True)
    (out,) = call(
        correct_body,
        [(SLOTS, 2, EDGE, CELLS)],
        [back.reshape(NS * 24, LANES), wave, patch],
        [(EDGE, 2 * CELLS), (2 * SLOTS, EDGE, CELLS)],
    )
    return out


def solution(mesh):
    return jax.shard_map(
        body,
        mesh=mesh,
        in_specs=(
            P(("grp", "sub"), None, None, None),
            P(("grp", "sub"), None, None, None),
            P(("grp", "sub")),
            P(("grp", "sub"), None),
            P(("grp", "sub")),
            P(),
        ),
        out_specs=P(("grp", "sub"), None, None, None),
        check_vma=False,
    )
```

```python
import jax
import jax.numpy as jnp
from jax import lax
from jax.experimental import pallas as pl
from jax.experimental.pallas import tpu as pltpu
from jax.sharding import PartitionSpec as P

PZ = 4
PY = 12
PATCHES = PY * PZ
EDGE = 16
CELLS = EDGE * EDGE
SLOTS = 4
NS = 16
LIVE = NS * SLOTS
LANES = 128

omega_fine = 0.7
omega_coarse = 0.6
shift_imag = 0.5

F32 = jnp.float32
VM = pl.BlockSpec(memory_space=pltpu.VMEM)
SM = pl.BlockSpec(memory_space=pltpu.SMEM)


def call(body, outs, ins, scratch=(), specs=None, limit=16, to=VM):
    return pl.pallas_call(
        body,
        out_shape=[jax.ShapeDtypeStruct(shape, F32) for shape in outs],
        in_specs=specs or [SM if a.dtype == jnp.int32 else VM for a in ins],
        out_specs=[to] * len(outs),
        scratch_shapes=[pltpu.VMEM(s, F32) if isinstance(s, tuple) else s for s in scratch],
        compiler_params=pltpu.CompilerParams(vmem_limit_bytes=limit << 20),
    )(*ins)


def select(picks, x):
    picks = picks.astype(jnp.bfloat16)
    out = None
    for _ in range(3):
        piece = x.astype(jnp.bfloat16)
        x = x - piece.astype(F32)
        term = jnp.dot(picks, piece, preferred_element_type=F32)
        out = term if out is None else out + term
    return out


def select_lanes(x, picks):
    pieces = []
    for _ in range(3):
        piece = x.astype(jnp.bfloat16).astype(F32)
        x = x - piece
        pieces.append(piece)
    n = x.shape[0]
    stacked = jnp.concatenate(pieces, 0).astype(jnp.bfloat16)
    out = jnp.dot(stacked, picks.astype(jnp.bfloat16), preferred_element_type=F32)
    return (out[:n] + out[n : 2 * n]) + out[2 * n :]


def iota(shape, dim):
    return lax.broadcasted_iota(jnp.int32, shape, dim)


def lane_roll(x, shift):
    return pltpu.roll(x, shift % x.shape[1], 1)


def row_roll(x, shift):
    return pltpu.roll(x, shift % x.shape[0], 0)


def in_plane(u):
    shape = u[0].shape
    lane = iota(shape, 1)
    patch = iota(shape, 0)
    k = lane % EDGE
    col = patch % PZ
    not_last, not_first = k < EDGE - 1, k > 0
    has_next, has_prev = col < PZ - 1, col > 0
    out = []
    ahead = [lane_roll(t, -EDGE) for t in u]
    behind = [lane_roll(t, EDGE) for t in u]
    low, high = lane >= EDGE, lane < LANES - EDGE
    y_next = [
        jnp.where(high, ahead[0], ahead[1]),
        jnp.where(high, ahead[1], jnp.where(patch < PATCHES - PZ, row_roll(ahead[0], -PZ), 0.0)),
    ]
    y_prev = [
        jnp.where(low, behind[0], jnp.where(patch >= PZ, row_roll(behind[1], PZ), 0.0)),
        jnp.where(low, behind[1], behind[0]),
    ]
    for h in range(2):
        t = u[h]
        z_next = jnp.where(
            not_last,
            lane_roll(t, -1),
            jnp.where(has_next, row_roll(lane_roll(t, EDGE - 1), -1), 0.0),
        )
        z_prev = jnp.where(
            not_first,
            lane_roll(t, 1),
            jnp.where(has_prev, row_roll(lane_roll(t, 1 - EDGE), 1), 0.0),
        )
        out.append((z_next + z_prev) + (y_next[h] + y_prev[h]))
    return out


def halves(ref, index):
    return [ref[index, :, :LANES], ref[index, :, LANES:]]


def put(ref, index, pair):
    ref[index, :, :LANES] = pair[0]
    ref[index, :, LANES:] = pair[1]


def field_of(ref, first):
    return [halves(ref, first), halves(ref, first + 1)]


def rows_of(ref, first):
    return [
        [ref[PATCHES * c : PATCHES * (c + 1), :LANES], ref[PATCHES * c : PATCHES * (c + 1), LANES:]]
        for c in (first, first + 1)
    ]


def wave_row(wave):
    return jnp.sum(jnp.where(iota(wave.shape, 0) == iota(wave.shape, 1), wave, 0.0), 0, keepdims=True)


def wave_rows(row):
    shape = (PATCHES, LANES)
    own = jnp.where(iota(shape, 0) == iota(shape, 1), jnp.broadcast_to(row, shape), 0.0)
    return jnp.broadcast_to(jnp.sum(own, 1, keepdims=True), shape)


def choose(flag, a, b):
    return [[jnp.where(flag, x, y) for x, y in zip(p, q)] for p, q in zip(a, b)]


def around(u, before, after):
    return [
        [n + (x + y) for n, x, y in zip(in_plane(u[part]), before[part], after[part])]
        for part in range(2)
    ]


def diagonal(wave):
    real, imag = 6.0 - wave, shift_imag * wave
    return real, imag


def smooth(u, total, rights, wave):
    real, imag = diagonal(wave)
    scale = omega_fine / (real * real + imag * imag)
    real, imag = real * scale, imag * scale
    keep = 1.0 - omega_fine
    out_re, out_im = [], []
    for h in range(2):
        a = rights[0][h] + total[0][h]
        b = rights[1][h] + total[1][h]
        out_re.append(keep * u[0][h] + (a * real - b * imag))
        out_im.append(keep * u[1][h] + (a * imag + b * real))
    return [out_re, out_im]


def residual(u, total, rights, wave):
    real, imag = diagonal(wave)
    out_re, out_im = [], []
    for h in range(2):
        out_re.append(rights[0][h] + total[0][h] - (real * u[0][h] + imag * u[1][h]))
        out_im.append(rights[1][h] + total[1][h] - (real * u[1][h] - imag * u[0][h]))
    return [out_re, out_im]


def position():
    return lax.axis_index("grp"), (lax.axis_index("sub") + NS - 1) % NS


def device_at(place):
    return (place + 1) % NS


def low_side_open(g):
    last = lax.axis_size("grp") - 1
    beyond = jnp.where(g % 2 == 0, g - 1, g + 1)
    return (beyond >= 0) & (beyond <= last)


def pack_body(
    field_hbm, source_hbm, patch_hbm, index_hbm, table_hbm, out_ref,
    field_ref, source_ref, patch_ref, index_ref, table_ref, sems,
):
    pairs = (
        (field_hbm, field_ref),
        (source_hbm, source_ref),
        (patch_hbm, patch_ref),
        (index_hbm, index_ref),
        (table_hbm, table_ref),
    )
    copies = [pltpu.make_async_copy(a, b, sems.at[i]) for i, (a, b) in enumerate(pairs)]
    for copy in copies:
        copy.start()
    for i in (2, 3, 4):
        copies[i].wait()
    g, _ = position()
    odd = g % 2 == 1
    for q in range(SLOTS):
        patch = jnp.full((1, LANES), patch_ref[q].astype(F32), F32)
        wave = jnp.full((1, LANES), table_ref[index_ref[q]], F32)
        for s in range(NS):
            out_ref[s, 10 * q + 8 : 10 * q + 9, :] = patch
            out_ref[s, 10 * q + 9 : 10 * q + 10, :] = wave
    for a, ref in enumerate((field_ref, source_ref)):
        copies[a].wait()
        for s in range(NS):
            place = (s + NS - 1) % NS
            layer = jnp.where(odd, EDGE - 1 - place, place)
            for q in range(SLOTS):
                for part in range(2):
                    row = 10 * q + 4 * a + 2 * part
                    cells = ref[q, part, pl.ds(layer, 1), :]
                    out_ref[s, row : row + 1, :] = cells[:, :LANES]
                    out_ref[s, row + 1 : row + 2, :] = cells[:, LANES:]


def place_body(raw_ref, plane_ref, field_ref, slot_ref, wave_ref):
    patches = raw_ref[pl.ds(8, LIVE, stride=10), :]
    held = (patches == iota((LIVE, LANES), 1).astype(F32)).astype(F32)
    slot_ref[...] = held
    pick = held.T[:PATCHES]
    order = (0, 1, 2, 3, 4, 5, 6, 7, 9)
    rows = jnp.concatenate([raw_ref[pl.ds(c, LIVE, stride=10), :] for c in order], 1)
    placed = select(pick, rows)
    for c in range(4):
        pair = [placed[:, CELLS * c : CELLS * c + LANES], placed[:, CELLS * c + LANES : CELLS * (c + 1)]]
        plane_ref[PATCHES * c : PATCHES * (c + 1), :LANES] = pair[0]
        plane_ref[PATCHES * c : PATCHES * (c + 1), LANES:] = pair[1]
        if c < 2:
            put(field_ref, c, pair)
    wave = placed[:, 4 * CELLS :]
    wave_ref[...] = wave
    row = jnp.broadcast_to(wave_row(wave), (8, LANES))
    plane_ref[4 * PATCHES :, :LANES] = row
    plane_ref[4 * PATCHES :, LANES:] = row


def first_body(own_ref, wave_ref, before_ref, after_ref, far_ref, out_ref, up_ref, down_ref):
    _, s = position()
    u = rows_of(own_ref, 0)
    factor = open_factor()
    v = [[x * factor for x in pair] for pair in rows_of(far_ref.at[other()], 0)]
    before = choose(s == 0, v, field_of(before_ref, 0))
    after = choose(s == NS - 1, v, field_of(after_ref, 0))
    new = smooth(u, around(u, before, after), rows_of(own_ref, 2), wave_ref[...])
    real, imag = diagonal(wave_rows(far_ref[other(), 4 * PATCHES : 4 * PATCHES + 1, :LANES]))
    scale = omega_fine / (real * real + imag * imag)
    real, imag = real * scale, imag * scale
    more = [
        [a * real - b * imag for a, b in zip(v[0], v[1])],
        [a * imag + b * real for a, b in zip(v[0], v[1])],
    ]
    for part in range(2):
        put(out_ref, part, new[part])
        put(up_ref, part, [x + jnp.where(s == NS - 2, y, 0.0) for x, y in zip(new[part], more[part])])
        put(down_ref, part, [x + jnp.where(s == 1, y, 0.0) for x, y in zip(new[part], more[part])])


def other():
    g, s = position()
    return jnp.where((g % 2 == 0) == (s >= NS // 2), 1, 0)


def open_factor():
    g, s = position()
    return jnp.where((s >= NS // 2) | low_side_open(g), 1.0, 0.0)


def window_lane(shape, dim):
    cell = iota(shape, dim)
    part, inside = cell // CELLS, cell % CELLS
    return part * 64 + (inside // (4 * EDGE) + 2) * 8 + (inside % EDGE) // 4 + 2


def second_body(own_ref, wave_ref, far_ref, before_ref, after_ref, mine_ref, field_ref, sums_ref, values_ref):
    _, s = position()
    first, last = s == 0, s == NS - 1
    u = rows_of(own_ref, 0)
    far_ref = far_ref.at[other()]
    factor = open_factor()
    v = [[x * factor for x in pair] for pair in rows_of(far_ref, 0)]
    one = field_of(mine_ref, 0)
    rights = rows_of(own_ref, 2)
    wave = wave_ref[...]
    far_wave = wave_rows(far_ref[4 * PATCHES : 4 * PATCHES + 1, :LANES])
    v_one = smooth(v, [[x + y for x, y in zip(in_plane(p), q)] for p, q in zip(v, u)], rows_of(far_ref, 2), far_wave)
    v_one = [[x * factor for x in pair] for pair in v_one]
    before = choose(first, v_one, field_of(before_ref, 0))
    after = choose(last, v_one, field_of(after_ref, 0))
    two = smooth(one, around(one, before, after), rights, wave)
    for part in range(2):
        put(field_ref, part, two[part])
    r = residual(two, [in_plane(two[0]), in_plane(two[1])], rights, wave)
    rows = jnp.concatenate(
        [jnp.concatenate(r[0] + r[1], 1), jnp.concatenate(two[0] + two[1], 1)], 0
    )
    shape = (2 * CELLS, LANES)
    gather = jnp.where(window_lane(shape, 0) == iota(shape, 1), 1.0, 0.0)
    sums = select_lanes(rows, gather)
    lane = iota((PATCHES, LANES), 1)
    values = sums[PATCHES:]
    beside = jnp.where((s % 4 == 0) | (s % 4 == 3), 1.0, 2.0)
    sums_ref[...] = jnp.where(lane == 0, wave, sums[:PATCHES] + beside * values)
    values_ref[...] = values


def join_body(sums_ref, values_ref, pair_ref, out_ref):
    out_ref[...] = sums_ref[...] + (pair_ref[...] + lane_roll(values_ref[...], 4))


def sides(x, patch, col):
    return (
        jnp.where(patch >= PZ, row_roll(x, PZ), 0.0),
        jnp.where(patch < PATCHES - PZ, row_roll(x, -PZ), 0.0),
        jnp.where(col > 0, row_roll(x, 1), 0.0),
        jnp.where(col < PZ - 1, row_roll(x, -1), 0.0),
    )


def windows(x):
    patch, lane = iota(x.shape, 0), iota(x.shape, 1)
    col = patch % PZ
    a, b = (lane // 8) % 8, lane % 8
    x = jnp.where((a >= 2) & (a < 6) & (b >= 2) & (b < 6), x, 0.0)
    _, _, low, high = sides(x, patch, col)
    x = x + jnp.where(b < 2, lane_roll(low, -4), 0.0) + jnp.where(b >= 6, lane_roll(high, 4), 0.0)
    low, high, _, _ = sides(x, patch, col)
    return x + jnp.where(a < 2, lane_roll(low, -32), 0.0) + jnp.where(a >= 6, lane_roll(high, 32), 0.0)


def slots_body(field_ref, own_wave_ref, slot_ref, out_ref, wave_ref, patch_ref):
    _, s = position()
    rows = [half for c in range(2) for half in halves(field_ref, c)]
    out_ref[...] = select(slot_ref[:, :PATCHES], jnp.concatenate(rows, 1))
    wave = own_wave_ref[...]
    patch, lane = iota(wave.shape, 0), iota(wave.shape, 1)
    col = patch % PZ
    a, b = (lane // 8) % 8, lane % 8
    _, _, low, high = sides(wave, patch, col)
    wave = jnp.where(b < 2, low, jnp.where(b >= 6, high, wave))
    low, high, _, _ = sides(wave, patch, col)
    wave = jnp.where(a < 2, low, jnp.where(a >= 6, high, wave))
    mine = slot_ref[pl.ds(SLOTS * device_at(s), SLOTS), :]
    wave_ref[...] = select(mine[:, :PATCHES], wave)
    index = iota(mine.shape, 1).astype(F32) + 1.0
    patch_ref[...] = jnp.broadcast_to(jnp.sum(mine * index, 1, keepdims=True) - 1.0, mine.shape)


def bundle_body(sent_ref, block_ref, far_ref, slot_ref, out_ref):
    _, s = position()
    factor = open_factor()
    far_ref = far_ref.at[other()]
    edge = jnp.where((s == 0) | (s == NS - 1), 1.0, 0.0)
    block, far_block = block_ref[...], far_ref[...]
    own = windows(block + (edge * factor) * lane_roll(far_block, -4))
    far = windows(factor * (far_block + edge * lane_roll(block, -4)))
    patch, lane = iota(far.shape, 0), iota(far.shape, 1)
    wave = jnp.broadcast_to(far_block[:, 0:1], far.shape)
    beside = (wave,) + sides(wave, patch, patch % PZ)
    for i, x in enumerate(beside):
        far = jnp.where(lane == i, x, far)
    placed = select(slot_ref[:, :PATCHES], jnp.concatenate([own, far], 1))
    for c in range(4):
        out_ref[pl.ds(c, LIVE, stride=6), :] = sent_ref[:, LANES * c : LANES * (c + 1)]
    for c in range(2):
        out_ref[pl.ds(4 + c, LIVE, stride=6), :] = placed[:, LANES * c : LANES * (c + 1)]


def coarse_sum(e):
    return (lane_roll(e, -1) + lane_roll(e, 1)) + (lane_roll(e, -8) + lane_roll(e, 8))


def correct_body(raw_ref, wave_ref, patch_ref, out_hbm, grown_ref, smooth_ref, sems):
    g, _ = position()
    odd = g % 2 == 1
    rows = 24
    shape = (SLOTS, LANES)

    def slot_rows(s, c):
        return raw_ref[pl.ds(rows * s + c, SLOTS, stride=6), :]

    def total(start, c):
        parts = [slot_rows(device_at(start + i), c) for i in range(4)]
        return ((parts[0] + parts[1]) + (parts[2] + parts[3])) * (1.0 / 64.0)

    lane = iota((LANES, LANES), 1)
    a, b = (lane // 8) % 8, lane % 8
    region = jnp.where(a < 2, 1, jnp.where(a >= 6, 2, jnp.where(b < 2, 3, jnp.where(b >= 6, 4, 0))))
    spread = jnp.where(iota((LANES, LANES), 0) == region, 1.0, 0.0)
    ends = jnp.concatenate([slot_rows(device_at(0), 5), slot_rows(device_at(NS - 1), 5)], 0)
    ends = select_lanes(ends, spread)
    low, high = ends[:SLOTS], ends[SLOTS:]
    own = wave_ref[...]
    wave = jnp.concatenate([low, low, own, own, own, own, high, high], 0)
    rhs = jnp.concatenate(
        [total(4, 5), total(0, 5)] + [total(4 * i, 4) for i in range(4)] + [total(12, 5), total(8, 5)], 0
    )
    lane = iota(shape, 1)
    a, b = (lane // 8) % 8, lane % 8
    patch = patch_ref[...].astype(jnp.int32)
    line, col = patch // PZ, patch % PZ
    y, z = 4 * line + a - 2, 4 * col + b - 2
    inside = jnp.where((y >= 0) & (y < 4 * PY) & (z >= 0) & (z < 4 * PZ), 1.0, 0.0)
    lower = jnp.where(low_side_open(g), inside, 0.0)
    inside = jnp.concatenate([lower, lower] + [inside] * 6, 0) > 0.0
    part_sign = jnp.where(iota(wave.shape, 1) < 64, -1.0, 1.0)
    real, imag = 6.0 / 16.0 - wave, shift_imag * wave
    scale = omega_coarse / (real * real + imag * imag)
    real, imag = real * scale, part_sign * imag * scale

    def divide(x):
        return jnp.where(inside, x * real + lane_roll(x, 64) * imag, 0.0)

    e = divide(rhs)
    for _ in range(2):
        beside = coarse_sum(e) + (row_roll(e, SLOTS) + row_roll(e, -SLOTS))
        e = (1.0 - omega_coarse) * e + divide(rhs + beside * (1.0 / 16.0))
    wide = (LANES, 2 * CELLS)
    widen = jnp.where(window_lane(wide, 1) == iota(wide, 0), 1.0, 0.0)
    grown_ref[...] = select_lanes(e[2 * SLOTS : 6 * SLOTS], widen)
    copies = []
    for q in range(SLOTS):
        held = jnp.broadcast_to(patch_ref[q : q + 1, 0:1] >= 0.0, (4, CELLS))
        for i in range(EDGE):
            s = device_at(jnp.where(odd, EDGE - 1 - i, i))
            for part in range(2):
                for h in range(2):
                    row = raw_ref[pl.ds(rows * s + 6 * q + 2 * part + h, 1), :]
                    smooth_ref[q, part, i : i + 1, LANES * h : LANES * (h + 1)] = row
        for i in range(4):
            plane = jnp.where(odd, 3 - i, i)
            line = grown_ref[pl.ds(SLOTS * plane + q, 1), :]
            for part in range(2):
                extra = jnp.broadcast_to(line[:, CELLS * part : CELLS * (part + 1)], (4, CELLS))
                value = smooth_ref[q, part, 4 * i : 4 * i + 4] + extra
                smooth_ref[q, part, 4 * i : 4 * i + 4] = jnp.where(held, value, 0.0)
        copies.append(pltpu.make_async_copy(smooth_ref.at[q], out_hbm.at[q], sems.at[q]))
        copies[q].start()
    for copy in copies:
        copy.wait()


def facing(groups, reach):
    pairs, met = [], set()
    for place in [i for i in range(NS) if i < reach or i >= NS - reach]:
        s = device_at(place)
        for g in range(0 if place >= NS // 2 else 1, groups - 1, 2):
            pairs.append([g * NS + s, (g + 1) * NS + s])
            met.update(pairs[-1])
    for g in range(groups):
        rest = [g * NS + s for s in range(NS) if g * NS + s not in met]
        whole = [i for i in rest if i ^ 1 in rest and 2 * reach < NS]
        rest = [i for i in rest if i not in whole]
        pairs += [whole[i : i + 2] for i in range(0, len(whole), 2)]
        pairs += [rest[i : i + 2] for i in range(0, len(rest), 2)]
    return pairs


def body(field, source, patch_of_slot, neighbour, wave_index, wave_table):
    groups = lax.axis_size("grp")
    both = ("grp", "sub")
    up = [(i, (i + 1) % NS) for i in range(NS)]
    down = [((i + 1) % NS, i) for i in range(NS)]
    ring = lambda x: (lax.ppermute(x, "sub", up), lax.ppermute(x, "sub", down))
    plane = (PATCHES, CELLS)

    hbm = pl.BlockSpec(memory_space=pltpu.HBM)
    (packed,) = call(
        pack_body,
        [(NS, 40, LANES)],
        [
            pltpu.with_memory_space_constraint(x, pltpu.HBM)
            for x in (field, source, patch_of_slot, wave_index, wave_table)
        ],
        [
            field.shape,
            source.shape,
            pltpu.SMEM(patch_of_slot.shape, jnp.int32),
            pltpu.SMEM(wave_index.shape, jnp.int32),
            pltpu.SMEM(wave_table.shape, F32),
            pltpu.SemaphoreType.DMA((5,)),
        ],
        [hbm] * 5,
        16,
    )
    raw = lax.all_to_all(packed, "sub", 0, 0, tiled=True).reshape(NS * 40, LANES)
    row = (PATCHES, LANES)
    stacked = (4 * PATCHES + 8, CELLS)
    own, start, slot, own_wave = call(place_body, [stacked, (2,) + plane, (LIVE, LANES), row], [raw])
    far = lax.all_gather(own, both, axis_index_groups=facing(groups, 2))
    before, after = ring(start)
    one, rising, falling = call(
        first_body, [(2,) + plane] * 3, [own, own_wave, before, after, far]
    )
    before = lax.ppermute(rising, "sub", up)
    after = lax.ppermute(falling, "sub", down)
    two, sums, values = call(
        second_body, [(2,) + plane, row, row], [own, own_wave, far, before, after, one]
    )
    edges = [device_at(4 * i + 3) for i in range(NS // 4 - 1)]
    pair = lax.ppermute(values, "sub", [(i, i + 1) for i in edges] + [(i + 1, i) for i in edges])
    mine = (SLOTS, LANES)
    sent, wave, patch = call(slots_body, [(LIVE, 2 * CELLS), mine, mine], [two, own_wave, slot])
    (block,) = call(join_body, [row], [sums, values, pair])
    far_block = lax.all_gather(block, both, axis_index_groups=facing(groups, NS // 2))
    (bundle,) = call(bundle_body, [(LIVE * 6, LANES)], [sent, block, far_block, slot])
    back = lax.all_to_all(bundle.reshape(NS, 24, LANES), "sub", 0, 0, tiled=True)
    (out,) = call(
        correct_body,
        [(SLOTS, 2, EDGE, CELLS)],
        [back.reshape(NS * 24, LANES), wave, patch],
        [(EDGE, 2 * CELLS), (SLOTS, 2, EDGE, CELLS), pltpu.SemaphoreType.DMA((SLOTS,))],
        to=hbm,
    )
    return out


def solution(mesh):
    return jax.shard_map(
        body,
        mesh=mesh,
        in_specs=(
            P(("grp", "sub"), None, None, None),
            P(("grp", "sub"), None, None, None),
            P(("grp", "sub")),
            P(("grp", "sub"), None),
            P(("grp", "sub")),
            P(),
        ),
        out_specs=P(("grp", "sub"), None, None, None),
        check_vma=False,
    )
```

```python
import jax
import jax.numpy as jnp
from jax import lax
from jax.experimental import pallas as pl
from jax.experimental.pallas import tpu as pltpu
from jax.sharding import PartitionSpec as P

PZ = 4
PY = 12
PATCHES = PY * PZ
EDGE = 16
CELLS = EDGE * EDGE
SLOTS = 4
NS = 16
LIVE = NS * SLOTS
LANES = 128

omega_fine = 0.7
omega_coarse = 0.6
shift_imag = 0.5

F32 = jnp.float32
VM = pl.BlockSpec(memory_space=pltpu.VMEM)
SM = pl.BlockSpec(memory_space=pltpu.SMEM)


def call(body, outs, ins, scratch=(), specs=None, limit=16, to=VM):
    return pl.pallas_call(
        body,
        out_shape=[jax.ShapeDtypeStruct(shape, F32) for shape in outs],
        in_specs=specs or [SM if a.dtype == jnp.int32 else VM for a in ins],
        out_specs=[to] * len(outs),
        scratch_shapes=[pltpu.VMEM(s, F32) if isinstance(s, tuple) else s for s in scratch],
        compiler_params=pltpu.CompilerParams(vmem_limit_bytes=limit << 20),
    )(*ins)


def select(picks, x):
    pieces = []
    for _ in range(3):
        piece = x.astype(jnp.bfloat16).astype(F32)
        x = x - piece
        pieces.append(piece)
    stacked = jnp.concatenate(pieces, 0).astype(jnp.bfloat16)
    thrice = jnp.concatenate([picks] * 3, 1).astype(jnp.bfloat16)
    return jnp.dot(thrice, stacked, preferred_element_type=F32)


def select_lanes(x, picks):
    pieces = []
    for _ in range(3):
        piece = x.astype(jnp.bfloat16).astype(F32)
        x = x - piece
        pieces.append(piece)
    n = x.shape[0]
    stacked = jnp.concatenate(pieces, 0).astype(jnp.bfloat16)
    out = jnp.dot(stacked, picks.astype(jnp.bfloat16), preferred_element_type=F32)
    return (out[:n] + out[n : 2 * n]) + out[2 * n :]


def iota(shape, dim):
    return lax.broadcasted_iota(jnp.int32, shape, dim)


def lane_roll(x, shift):
    return pltpu.roll(x, shift % x.shape[1], 1)


def row_roll(x, shift):
    return pltpu.roll(x, shift % x.shape[0], 0)


def in_plane(u):
    shape = u[0].shape
    lane = iota(shape, 1)
    patch = iota(shape, 0)
    k = lane % EDGE
    col = patch % PZ
    not_last, not_first = k < EDGE - 1, k > 0
    has_next, has_prev = col < PZ - 1, col > 0
    out = []
    ahead = [lane_roll(t, -EDGE) for t in u]
    behind = [lane_roll(t, EDGE) for t in u]
    low, high = lane >= EDGE, lane < LANES - EDGE
    y_next = [
        jnp.where(high, ahead[0], ahead[1]),
        jnp.where(high, ahead[1], jnp.where(patch < PATCHES - PZ, row_roll(ahead[0], -PZ), 0.0)),
    ]
    y_prev = [
        jnp.where(low, behind[0], jnp.where(patch >= PZ, row_roll(behind[1], PZ), 0.0)),
        jnp.where(low, behind[1], behind[0]),
    ]
    for h in range(2):
        t = u[h]
        z_next = jnp.where(
            not_last,
            lane_roll(t, -1),
            jnp.where(has_next, row_roll(lane_roll(t, EDGE - 1), -1), 0.0),
        )
        z_prev = jnp.where(
            not_first,
            lane_roll(t, 1),
            jnp.where(has_prev, row_roll(lane_roll(t, 1 - EDGE), 1), 0.0),
        )
        out.append((z_next + z_prev) + (y_next[h] + y_prev[h]))
    return out


def halves(ref, index):
    return [ref[index, :, :LANES], ref[index, :, LANES:]]


def put(ref, index, pair):
    ref[index, :, :LANES] = pair[0]
    ref[index, :, LANES:] = pair[1]


def field_of(ref, first):
    return [halves(ref, first), halves(ref, first + 1)]


def rows_of(ref, first):
    return [
        [ref[PATCHES * c : PATCHES * (c + 1), :LANES], ref[PATCHES * c : PATCHES * (c + 1), LANES:]]
        for c in (first, first + 1)
    ]


def wave_row(wave):
    return jnp.sum(jnp.where(iota(wave.shape, 0) == iota(wave.shape, 1), wave, 0.0), 0, keepdims=True)


def wave_rows(row):
    shape = (PATCHES, LANES)
    own = jnp.where(iota(shape, 0) == iota(shape, 1), jnp.broadcast_to(row, shape), 0.0)
    return jnp.broadcast_to(jnp.sum(own, 1, keepdims=True), shape)


def choose(flag, a, b):
    return [[jnp.where(flag, x, y) for x, y in zip(p, q)] for p, q in zip(a, b)]


def around(u, before, after):
    return [
        [n + (x + y) for n, x, y in zip(in_plane(u[part]), before[part], after[part])]
        for part in range(2)
    ]


def diagonal(wave):
    real, imag = 6.0 - wave, shift_imag * wave
    return real, imag


def smooth(u, total, rights, wave):
    real, imag = diagonal(wave)
    scale = omega_fine / (real * real + imag * imag)
    real, imag = real * scale, imag * scale
    keep = 1.0 - omega_fine
    out_re, out_im = [], []
    for h in range(2):
        a = rights[0][h] + total[0][h]
        b = rights[1][h] + total[1][h]
        out_re.append(keep * u[0][h] + (a * real - b * imag))
        out_im.append(keep * u[1][h] + (a * imag + b * real))
    return [out_re, out_im]


def residual(u, total, rights, wave):
    real, imag = diagonal(wave)
    out_re, out_im = [], []
    for h in range(2):
        out_re.append(rights[0][h] + total[0][h] - (real * u[0][h] + imag * u[1][h]))
        out_im.append(rights[1][h] + total[1][h] - (real * u[1][h] - imag * u[0][h]))
    return [out_re, out_im]


def position():
    return lax.axis_index("grp"), (lax.axis_index("sub") + NS - 1) % NS


def device_at(place):
    return (place + 1) % NS


def low_side_open(g):
    last = lax.axis_size("grp") - 1
    beyond = jnp.where(g % 2 == 0, g - 1, g + 1)
    return (beyond >= 0) & (beyond <= last)


def pack_body(
    field_hbm, source_hbm, patch_hbm, index_hbm, table_hbm, out_ref,
    field_ref, source_ref, patch_ref, index_ref, table_ref, sems,
):
    pairs = (
        (field_hbm, field_ref),
        (source_hbm, source_ref),
        (patch_hbm, patch_ref),
        (index_hbm, index_ref),
        (table_hbm, table_ref),
    )
    copies = [pltpu.make_async_copy(a, b, sems.at[i]) for i, (a, b) in enumerate(pairs)]
    for copy in copies:
        copy.start()
    for i in (2, 3, 4):
        copies[i].wait()
    g, _ = position()
    odd = g % 2 == 1
    for q in range(SLOTS):
        patch = jnp.full((1, LANES), patch_ref[q].astype(F32), F32)
        wave = jnp.full((1, LANES), table_ref[index_ref[q]], F32)
        for s in range(NS):
            out_ref[s, 10 * q + 8 : 10 * q + 9, :] = patch
            out_ref[s, 10 * q + 9 : 10 * q + 10, :] = wave
    for a, ref in enumerate((field_ref, source_ref)):
        copies[a].wait()
        for s in range(NS):
            place = (s + NS - 1) % NS
            layer = jnp.where(odd, EDGE - 1 - place, place)
            for q in range(SLOTS):
                for part in range(2):
                    row = 10 * q + 4 * a + 2 * part
                    cells = ref[q, part, pl.ds(layer, 1), :]
                    out_ref[s, row : row + 1, :] = cells[:, :LANES]
                    out_ref[s, row + 1 : row + 2, :] = cells[:, LANES:]


def place_body(raw_ref, plane_ref, field_ref, slot_ref, wave_ref):
    patches = raw_ref[pl.ds(8, LIVE, stride=10), :]
    held = (patches == iota((LIVE, LANES), 1).astype(F32)).astype(F32)
    slot_ref[...] = held
    pick = held.T[:PATCHES]
    order = (0, 1, 2, 3, 4, 5, 6, 7, 9)
    rows = jnp.concatenate([raw_ref[pl.ds(c, LIVE, stride=10), :] for c in order], 1)
    placed = select(pick, rows)
    for c in range(4):
        pair = [placed[:, CELLS * c : CELLS * c + LANES], placed[:, CELLS * c + LANES : CELLS * (c + 1)]]
        plane_ref[PATCHES * c : PATCHES * (c + 1), :LANES] = pair[0]
        plane_ref[PATCHES * c : PATCHES * (c + 1), LANES:] = pair[1]
        if c < 2:
            put(field_ref, c, pair)
    wave = placed[:, 4 * CELLS :]
    wave_ref[...] = wave
    row = jnp.broadcast_to(wave_row(wave), (8, LANES))
    plane_ref[4 * PATCHES :, :LANES] = row
    plane_ref[4 * PATCHES :, LANES:] = row


def first_body(own_ref, wave_ref, before_ref, after_ref, far_ref, out_ref, up_ref, down_ref):
    _, s = position()
    u = rows_of(own_ref, 0)
    factor = open_factor()
    v = [[x * factor for x in pair] for pair in rows_of(far_ref.at[other()], 0)]
    before = choose(s == 0, v, field_of(before_ref, 0))
    after = choose(s == NS - 1, v, field_of(after_ref, 0))
    new = smooth(u, around(u, before, after), rows_of(own_ref, 2), wave_ref[...])
    real, imag = diagonal(wave_rows(far_ref[other(), 4 * PATCHES : 4 * PATCHES + 1, :LANES]))
    scale = omega_fine / (real * real + imag * imag)
    real, imag = real * scale, imag * scale
    more = [
        [a * real - b * imag for a, b in zip(v[0], v[1])],
        [a * imag + b * real for a, b in zip(v[0], v[1])],
    ]
    for part in range(2):
        put(out_ref, part, new[part])
        put(up_ref, part, [x + jnp.where(s == NS - 2, y, 0.0) for x, y in zip(new[part], more[part])])
        put(down_ref, part, [x + jnp.where(s == 1, y, 0.0) for x, y in zip(new[part], more[part])])


def other():
    g, s = position()
    return jnp.where((g % 2 == 0) == (s >= NS // 2), 1, 0)


def open_factor():
    g, s = position()
    return jnp.where((s >= NS // 2) | low_side_open(g), 1.0, 0.0)


def window_lane(shape, dim):
    cell = iota(shape, dim)
    part, inside = cell // CELLS, cell % CELLS
    return part * 64 + (inside // (4 * EDGE) + 2) * 8 + (inside % EDGE) // 4 + 2


def second_body(own_ref, wave_ref, far_ref, before_ref, after_ref, mine_ref, field_ref, sums_ref, values_ref):
    _, s = position()
    first, last = s == 0, s == NS - 1
    u = rows_of(own_ref, 0)
    far_ref = far_ref.at[other()]
    factor = open_factor()
    v = [[x * factor for x in pair] for pair in rows_of(far_ref, 0)]
    one = field_of(mine_ref, 0)
    rights = rows_of(own_ref, 2)
    wave = wave_ref[...]
    far_wave = wave_rows(far_ref[4 * PATCHES : 4 * PATCHES + 1, :LANES])
    v_one = smooth(v, [[x + y for x, y in zip(in_plane(p), q)] for p, q in zip(v, u)], rows_of(far_ref, 2), far_wave)
    v_one = [[x * factor for x in pair] for pair in v_one]
    before = choose(first, v_one, field_of(before_ref, 0))
    after = choose(last, v_one, field_of(after_ref, 0))
    two = smooth(one, around(one, before, after), rights, wave)
    for part in range(2):
        put(field_ref, part, two[part])
    r = residual(two, [in_plane(two[0]), in_plane(two[1])], rights, wave)
    rows = jnp.concatenate(
        [jnp.concatenate(r[0] + r[1], 1), jnp.concatenate(two[0] + two[1], 1)], 0
    )
    shape = (2 * CELLS, LANES)
    gather = jnp.where(window_lane(shape, 0) == iota(shape, 1), 1.0, 0.0)
    sums = select_lanes(rows, gather)
    lane = iota((PATCHES, LANES), 1)
    values = sums[PATCHES:]
    beside = jnp.where((s % 4 == 0) | (s % 4 == 3), 1.0, 2.0)
    sums_ref[...] = jnp.where(lane == 0, wave, sums[:PATCHES] + beside * values)
    values_ref[...] = values


def join_body(sums_ref, values_ref, pair_ref, out_ref):
    out_ref[...] = sums_ref[...] + (pair_ref[...] + lane_roll(values_ref[...], 4))


def sides(x, patch, col):
    return (
        jnp.where(patch >= PZ, row_roll(x, PZ), 0.0),
        jnp.where(patch < PATCHES - PZ, row_roll(x, -PZ), 0.0),
        jnp.where(col > 0, row_roll(x, 1), 0.0),
        jnp.where(col < PZ - 1, row_roll(x, -1), 0.0),
    )


def windows(x):
    patch, lane = iota(x.shape, 0), iota(x.shape, 1)
    col = patch % PZ
    a, b = (lane // 8) % 8, lane % 8
    x = jnp.where((a >= 2) & (a < 6) & (b >= 2) & (b < 6), x, 0.0)
    _, _, low, high = sides(x, patch, col)
    x = x + jnp.where(b < 2, lane_roll(low, -4), 0.0) + jnp.where(b >= 6, lane_roll(high, 4), 0.0)
    low, high, _, _ = sides(x, patch, col)
    return x + jnp.where(a < 2, lane_roll(low, -32), 0.0) + jnp.where(a >= 6, lane_roll(high, 32), 0.0)


def slots_body(field_ref, own_wave_ref, slot_ref, out_ref, wave_ref, patch_ref):
    _, s = position()
    rows = [half for c in range(2) for half in halves(field_ref, c)]
    out_ref[...] = select(slot_ref[:, :PATCHES], jnp.concatenate(rows, 1))
    wave = own_wave_ref[...]
    patch, lane = iota(wave.shape, 0), iota(wave.shape, 1)
    col = patch % PZ
    a, b = (lane // 8) % 8, lane % 8
    _, _, low, high = sides(wave, patch, col)
    wave = jnp.where(b < 2, low, jnp.where(b >= 6, high, wave))
    low, high, _, _ = sides(wave, patch, col)
    wave = jnp.where(a < 2, low, jnp.where(a >= 6, high, wave))
    mine = slot_ref[pl.ds(SLOTS * device_at(s), SLOTS), :]
    wave_ref[...] = select(mine[:, :PATCHES], wave)
    index = iota(mine.shape, 1).astype(F32) + 1.0
    patch_ref[...] = jnp.broadcast_to(jnp.sum(mine * index, 1, keepdims=True) - 1.0, mine.shape)


def bundle_body(sent_ref, block_ref, far_ref, slot_ref, out_ref):
    _, s = position()
    factor = open_factor()
    far_ref = far_ref.at[other()]
    edge = jnp.where((s == 0) | (s == NS - 1), 1.0, 0.0)
    block, far_block = block_ref[...], far_ref[...]
    own = windows(block + (edge * factor) * lane_roll(far_block, -4))
    far = windows(factor * (far_block + edge * lane_roll(block, -4)))
    patch, lane = iota(far.shape, 0), iota(far.shape, 1)
    wave = jnp.broadcast_to(far_block[:, 0:1], far.shape)
    beside = (wave,) + sides(wave, patch, patch % PZ)
    for i, x in enumerate(beside):
        far = jnp.where(lane == i, x, far)
    placed = select(slot_ref[:, :PATCHES], jnp.concatenate([own, far], 1))
    for c in range(4):
        out_ref[pl.ds(c, LIVE, stride=6), :] = sent_ref[:, LANES * c : LANES * (c + 1)]
    for c in range(2):
        out_ref[pl.ds(4 + c, LIVE, stride=6), :] = placed[:, LANES * c : LANES * (c + 1)]


def coarse_sum(e):
    return (lane_roll(e, -1) + lane_roll(e, 1)) + (lane_roll(e, -8) + lane_roll(e, 8))


def correct_body(raw_ref, wave_ref, patch_ref, out_hbm, grown_ref, smooth_ref, sems):
    g, _ = position()
    odd = g % 2 == 1
    rows = 24
    shape = (SLOTS, LANES)

    def slot_rows(s, c):
        return raw_ref[pl.ds(rows * s + c, SLOTS, stride=6), :]

    def total(start, c):
        parts = [slot_rows(device_at(start + i), c) for i in range(4)]
        return ((parts[0] + parts[1]) + (parts[2] + parts[3])) * (1.0 / 64.0)

    lane = iota((LANES, LANES), 1)
    a, b = (lane // 8) % 8, lane % 8
    region = jnp.where(a < 2, 1, jnp.where(a >= 6, 2, jnp.where(b < 2, 3, jnp.where(b >= 6, 4, 0))))
    spread = jnp.where(iota((LANES, LANES), 0) == region, 1.0, 0.0)
    ends = jnp.concatenate([slot_rows(device_at(0), 5), slot_rows(device_at(NS - 1), 5)], 0)
    ends = select_lanes(ends, spread)
    low, high = ends[:SLOTS], ends[SLOTS:]
    own = wave_ref[...]
    wave = jnp.concatenate([low, low, own, own, own, own, high, high], 0)
    rhs = jnp.concatenate(
        [total(4, 5), total(0, 5)] + [total(4 * i, 4) for i in range(4)] + [total(12, 5), total(8, 5)], 0
    )
    lane = iota(shape, 1)
    a, b = (lane // 8) % 8, lane % 8
    patch = patch_ref[...].astype(jnp.int32)
    line, col = patch // PZ, patch % PZ
    y, z = 4 * line + a - 2, 4 * col + b - 2
    inside = jnp.where((y >= 0) & (y < 4 * PY) & (z >= 0) & (z < 4 * PZ), 1.0, 0.0)
    lower = jnp.where(low_side_open(g), inside, 0.0)
    inside = jnp.concatenate([lower, lower] + [inside] * 6, 0) > 0.0
    part_sign = jnp.where(iota(wave.shape, 1) < 64, -1.0, 1.0)
    real, imag = 6.0 / 16.0 - wave, shift_imag * wave
    scale = omega_coarse / (real * real + imag * imag)
    real, imag = real * scale, part_sign * imag * scale

    def divide(x):
        return jnp.where(inside, x * real + lane_roll(x, 64) * imag, 0.0)

    e = divide(rhs)
    for _ in range(2):
        beside = coarse_sum(e) + (row_roll(e, SLOTS) + row_roll(e, -SLOTS))
        e = (1.0 - omega_coarse) * e + divide(rhs + beside * (1.0 / 16.0))
    wide = (LANES, 2 * CELLS)
    widen = jnp.where(window_lane(wide, 1) == iota(wide, 0), 1.0, 0.0)
    grown_ref[...] = select_lanes(e[2 * SLOTS : 6 * SLOTS], widen)
    copies = []
    for q in range(SLOTS):
        held = jnp.broadcast_to(patch_ref[q : q + 1, 0:1] >= 0.0, (4, CELLS))
        for i in range(EDGE):
            s = device_at(jnp.where(odd, EDGE - 1 - i, i))
            for part in range(2):
                for h in range(2):
                    row = raw_ref[pl.ds(rows * s + 6 * q + 2 * part + h, 1), :]
                    smooth_ref[q, part, i : i + 1, LANES * h : LANES * (h + 1)] = row
        for i in range(4):
            plane = jnp.where(odd, 3 - i, i)
            line = grown_ref[pl.ds(SLOTS * plane + q, 1), :]
            for part in range(2):
                extra = jnp.broadcast_to(line[:, CELLS * part : CELLS * (part + 1)], (4, CELLS))
                value = smooth_ref[q, part, 4 * i : 4 * i + 4] + extra
                smooth_ref[q, part, 4 * i : 4 * i + 4] = jnp.where(held, value, 0.0)
        copies.append(pltpu.make_async_copy(smooth_ref.at[q], out_hbm.at[q], sems.at[q]))
        copies[q].start()
    for copy in copies:
        copy.wait()


def facing(groups, reach):
    pairs, met = [], set()
    for place in [i for i in range(NS) if i < reach or i >= NS - reach]:
        s = device_at(place)
        for g in range(0 if place >= NS // 2 else 1, groups - 1, 2):
            pairs.append([g * NS + s, (g + 1) * NS + s])
            met.update(pairs[-1])
    for g in range(groups):
        rest = [g * NS + s for s in range(NS) if g * NS + s not in met]
        whole = [i for i in rest if i ^ 1 in rest and 2 * reach < NS]
        rest = [i for i in rest if i not in whole]
        pairs += [whole[i : i + 2] for i in range(0, len(whole), 2)]
        pairs += [rest[i : i + 2] for i in range(0, len(rest), 2)]
    return pairs


def body(field, source, patch_of_slot, neighbour, wave_index, wave_table):
    groups = lax.axis_size("grp")
    both = ("grp", "sub")
    up = [(i, (i + 1) % NS) for i in range(NS)]
    down = [((i + 1) % NS, i) for i in range(NS)]
    ring = lambda x: (lax.ppermute(x, "sub", up), lax.ppermute(x, "sub", down))
    plane = (PATCHES, CELLS)

    hbm = pl.BlockSpec(memory_space=pltpu.HBM)
    (packed,) = call(
        pack_body,
        [(NS, 40, LANES)],
        [
            pltpu.with_memory_space_constraint(x, pltpu.HBM)
            for x in (field, source, patch_of_slot, wave_index, wave_table)
        ],
        [
            field.shape,
            source.shape,
            pltpu.SMEM(patch_of_slot.shape, jnp.int32),
            pltpu.SMEM(wave_index.shape, jnp.int32),
            pltpu.SMEM(wave_table.shape, F32),
            pltpu.SemaphoreType.DMA((5,)),
        ],
        [hbm] * 5,
        16,
    )
    raw = lax.all_to_all(packed, "sub", 0, 0, tiled=True).reshape(NS * 40, LANES)
    row = (PATCHES, LANES)
    stacked = (4 * PATCHES + 8, CELLS)
    own, start, slot, own_wave = call(place_body, [stacked, (2,) + plane, (LIVE, LANES), row], [raw])
    far = lax.all_gather(own, both, axis_index_groups=facing(groups, 2))
    before, after = ring(start)
    one, rising, falling = call(
        first_body, [(2,) + plane] * 3, [own, own_wave, before, after, far]
    )
    before = lax.ppermute(rising, "sub", up)
    after = lax.ppermute(falling, "sub", down)
    two, sums, values = call(
        second_body, [(2,) + plane, row, row], [own, own_wave, far, before, after, one]
    )
    edges = [device_at(4 * i + 3) for i in range(NS // 4 - 1)]
    pair = lax.ppermute(values, "sub", [(i, i + 1) for i in edges] + [(i + 1, i) for i in edges])
    mine = (SLOTS, LANES)
    sent, wave, patch = call(slots_body, [(LIVE, 2 * CELLS), mine, mine], [two, own_wave, slot])
    (block,) = call(join_body, [row], [sums, values, pair])
    far_block = lax.all_gather(block, both, axis_index_groups=facing(groups, NS // 2))
    (bundle,) = call(bundle_body, [(LIVE * 6, LANES)], [sent, block, far_block, slot])
    back = lax.all_to_all(bundle.reshape(NS, 24, LANES), "sub", 0, 0, tiled=True)
    (out,) = call(
        correct_body,
        [(SLOTS, 2, EDGE, CELLS)],
        [back.reshape(NS * 24, LANES), wave, patch],
        [(EDGE, 2 * CELLS), (SLOTS, 2, EDGE, CELLS), pltpu.SemaphoreType.DMA((SLOTS,))],
        to=hbm,
    )
    return out


def solution(mesh):
    return jax.shard_map(
        body,
        mesh=mesh,
        in_specs=(
            P(("grp", "sub"), None, None, None),
            P(("grp", "sub"), None, None, None),
            P(("grp", "sub")),
            P(("grp", "sub"), None),
            P(("grp", "sub")),
            P(),
        ),
        out_specs=P(("grp", "sub"), None, None, None),
        check_vma=False,
    )
```

```python
import jax
import jax.numpy as jnp
from jax import lax
from jax.experimental import pallas as pl
from jax.experimental.pallas import tpu as pltpu
from jax.sharding import PartitionSpec as P

PZ = 4
PY = 12
PATCHES = PY * PZ
EDGE = 16
CELLS = EDGE * EDGE
SLOTS = 4
NS = 16
LIVE = NS * SLOTS
LANES = 128

omega_fine = 0.7
omega_coarse = 0.6
shift_imag = 0.5

F32 = jnp.float32
VM = pl.BlockSpec(memory_space=pltpu.VMEM)
SM = pl.BlockSpec(memory_space=pltpu.SMEM)


def call(body, outs, ins, scratch=(), specs=None, limit=16, to=VM):
    return pl.pallas_call(
        body,
        out_shape=[jax.ShapeDtypeStruct(shape, F32) for shape in outs],
        in_specs=specs or [SM if a.dtype == jnp.int32 else VM for a in ins],
        out_specs=[to] * len(outs),
        scratch_shapes=[pltpu.VMEM(s, F32) if isinstance(s, tuple) else s for s in scratch],
        compiler_params=pltpu.CompilerParams(vmem_limit_bytes=limit << 20),
    )(*ins)


def select(picks, x):
    pieces = []
    for _ in range(3):
        piece = x.astype(jnp.bfloat16).astype(F32)
        x = x - piece
        pieces.append(piece)
    stacked = jnp.concatenate(pieces, 0).astype(jnp.bfloat16)
    thrice = jnp.concatenate([picks] * 3, 1).astype(jnp.bfloat16)
    return jnp.dot(thrice, stacked, preferred_element_type=F32)


def select_lanes(x, picks):
    pieces = []
    for _ in range(3):
        piece = x.astype(jnp.bfloat16).astype(F32)
        x = x - piece
        pieces.append(piece)
    n = x.shape[0]
    stacked = jnp.concatenate(pieces, 0).astype(jnp.bfloat16)
    out = jnp.dot(stacked, picks.astype(jnp.bfloat16), preferred_element_type=F32)
    return (out[:n] + out[n : 2 * n]) + out[2 * n :]


def iota(shape, dim):
    return lax.broadcasted_iota(jnp.int32, shape, dim)


def lane_roll(x, shift):
    return pltpu.roll(x, shift % x.shape[1], 1)


def row_roll(x, shift):
    return pltpu.roll(x, shift % x.shape[0], 0)


def in_plane(u):
    shape = u[0].shape
    lane = iota(shape, 1)
    patch = iota(shape, 0)
    k = lane % EDGE
    col = patch % PZ
    not_last, not_first = k < EDGE - 1, k > 0
    has_next, has_prev = col < PZ - 1, col > 0
    out = []
    ahead = [lane_roll(t, -EDGE) for t in u]
    behind = [lane_roll(t, EDGE) for t in u]
    low, high = lane >= EDGE, lane < LANES - EDGE
    y_next = [
        jnp.where(high, ahead[0], ahead[1]),
        jnp.where(high, ahead[1], jnp.where(patch < PATCHES - PZ, row_roll(ahead[0], -PZ), 0.0)),
    ]
    y_prev = [
        jnp.where(low, behind[0], jnp.where(patch >= PZ, row_roll(behind[1], PZ), 0.0)),
        jnp.where(low, behind[1], behind[0]),
    ]
    for h in range(2):
        t = u[h]
        z_next = jnp.where(
            not_last,
            lane_roll(t, -1),
            jnp.where(has_next, row_roll(lane_roll(t, EDGE - 1), -1), 0.0),
        )
        z_prev = jnp.where(
            not_first,
            lane_roll(t, 1),
            jnp.where(has_prev, row_roll(lane_roll(t, 1 - EDGE), 1), 0.0),
        )
        out.append((z_next + z_prev) + (y_next[h] + y_prev[h]))
    return out


def halves(ref, index):
    return [ref[index, :, :LANES], ref[index, :, LANES:]]


def put(ref, index, pair):
    ref[index, :, :LANES] = pair[0]
    ref[index, :, LANES:] = pair[1]


def field_of(ref, first):
    return [halves(ref, first), halves(ref, first + 1)]


def rows_of(ref, first):
    return [
        [ref[PATCHES * c : PATCHES * (c + 1), :LANES], ref[PATCHES * c : PATCHES * (c + 1), LANES:]]
        for c in (first, first + 1)
    ]


def wave_row(wave):
    return jnp.sum(jnp.where(iota(wave.shape, 0) == iota(wave.shape, 1), wave, 0.0), 0, keepdims=True)


def wave_rows(row):
    shape = (PATCHES, LANES)
    own = jnp.where(iota(shape, 0) == iota(shape, 1), jnp.broadcast_to(row, shape), 0.0)
    return jnp.broadcast_to(jnp.sum(own, 1, keepdims=True), shape)


def choose(flag, a, b):
    return [[jnp.where(flag, x, y) for x, y in zip(p, q)] for p, q in zip(a, b)]


def around(u, before, after):
    return [
        [n + (x + y) for n, x, y in zip(in_plane(u[part]), before[part], after[part])]
        for part in range(2)
    ]


def diagonal(wave):
    real, imag = 6.0 - wave, shift_imag * wave
    return real, imag


def smooth(u, total, rights, wave):
    real, imag = diagonal(wave)
    scale = omega_fine / (real * real + imag * imag)
    real, imag = real * scale, imag * scale
    keep = 1.0 - omega_fine
    out_re, out_im = [], []
    for h in range(2):
        a = rights[0][h] + total[0][h]
        b = rights[1][h] + total[1][h]
        out_re.append(keep * u[0][h] + (a * real - b * imag))
        out_im.append(keep * u[1][h] + (a * imag + b * real))
    return [out_re, out_im]


def residual(u, total, rights, wave):
    real, imag = diagonal(wave)
    out_re, out_im = [], []
    for h in range(2):
        out_re.append(rights[0][h] + total[0][h] - (real * u[0][h] + imag * u[1][h]))
        out_im.append(rights[1][h] + total[1][h] - (real * u[1][h] - imag * u[0][h]))
    return [out_re, out_im]


def position():
    return lax.axis_index("grp"), (lax.axis_index("sub") + NS - 1) % NS


def device_at(place):
    return (place + 1) % NS


def low_side_open(g):
    last = lax.axis_size("grp") - 1
    beyond = jnp.where(g % 2 == 0, g - 1, g + 1)
    return (beyond >= 0) & (beyond <= last)


def pack_body(
    field_hbm, source_hbm, patch_hbm, index_hbm, table_hbm, out_ref,
    field_ref, source_ref, patch_ref, index_ref, table_ref, sems,
):
    pairs = (
        (field_hbm, field_ref),
        (source_hbm, source_ref),
        (patch_hbm, patch_ref),
        (index_hbm, index_ref),
        (table_hbm, table_ref),
    )
    copies = [pltpu.make_async_copy(a, b, sems.at[i]) for i, (a, b) in enumerate(pairs)]
    for copy in copies:
        copy.start()
    for i in (2, 3, 4):
        copies[i].wait()
    g, _ = position()
    odd = g % 2 == 1
    for q in range(SLOTS):
        patch = jnp.full((1, LANES), patch_ref[q].astype(F32), F32)
        wave = jnp.full((1, LANES), table_ref[index_ref[q]], F32)
        for s in range(NS):
            out_ref[s, 10 * q + 8 : 10 * q + 9, :] = patch
            out_ref[s, 10 * q + 9 : 10 * q + 10, :] = wave
    for a, ref in enumerate((field_ref, source_ref)):
        copies[a].wait()
        for s in range(NS):
            place = (s + NS - 1) % NS
            layer = jnp.where(odd, EDGE - 1 - place, place)
            for q in range(SLOTS):
                for part in range(2):
                    row = 10 * q + 4 * a + 2 * part
                    cells = ref[q, part, pl.ds(layer, 1), :]
                    out_ref[s, row : row + 1, :] = cells[:, :LANES]
                    out_ref[s, row + 1 : row + 2, :] = cells[:, LANES:]


def place_body(raw_ref, plane_ref, field_ref, slot_ref, wave_ref):
    patches = raw_ref[pl.ds(8, LIVE, stride=10), :]
    held = (patches == iota((LIVE, LANES), 1).astype(F32)).astype(F32)
    slot_ref[...] = held
    pick = held.T[:PATCHES]
    order = (0, 1, 2, 3, 4, 5, 6, 7, 9)
    rows = jnp.concatenate([raw_ref[pl.ds(c, LIVE, stride=10), :] for c in order], 1)
    placed = select(pick, rows)
    for c in range(4):
        pair = [placed[:, CELLS * c : CELLS * c + LANES], placed[:, CELLS * c + LANES : CELLS * (c + 1)]]
        plane_ref[PATCHES * c : PATCHES * (c + 1), :LANES] = pair[0]
        plane_ref[PATCHES * c : PATCHES * (c + 1), LANES:] = pair[1]
        if c < 2:
            put(field_ref, c, pair)
    wave = placed[:, 4 * CELLS :]
    wave_ref[...] = wave
    row = jnp.broadcast_to(wave_row(wave), (8, LANES))
    plane_ref[4 * PATCHES :, :LANES] = row
    plane_ref[4 * PATCHES :, LANES:] = row


def first_body(own_ref, wave_ref, before_ref, after_ref, far_ref, out_ref, up_ref, down_ref):
    _, s = position()
    u = rows_of(own_ref, 0)
    factor = open_factor()
    v = [[x * factor for x in pair] for pair in rows_of(far_ref.at[other()], 0)]
    before = choose(s == 0, v, field_of(before_ref, 0))
    after = choose(s == NS - 1, v, field_of(after_ref, 0))
    new = smooth(u, around(u, before, after), rows_of(own_ref, 2), wave_ref[...])
    real, imag = diagonal(wave_rows(far_ref[other(), 4 * PATCHES : 4 * PATCHES + 1, :LANES]))
    scale = omega_fine / (real * real + imag * imag)
    real, imag = real * scale, imag * scale
    more = [
        [a * real - b * imag for a, b in zip(v[0], v[1])],
        [a * imag + b * real for a, b in zip(v[0], v[1])],
    ]
    for part in range(2):
        put(out_ref, part, new[part])
        put(up_ref, part, [x + jnp.where(s == NS - 2, y, 0.0) for x, y in zip(new[part], more[part])])
        put(down_ref, part, [x + jnp.where(s == 1, y, 0.0) for x, y in zip(new[part], more[part])])


def other():
    g, s = position()
    return jnp.where((g % 2 == 0) == (s >= NS // 2), 1, 0)


def open_factor():
    g, s = position()
    return jnp.where((s >= NS // 2) | low_side_open(g), 1.0, 0.0)


def window_lane(shape, dim):
    cell = iota(shape, dim)
    part, inside = cell // CELLS, cell % CELLS
    return part * 64 + (inside // (4 * EDGE) + 2) * 8 + (inside % EDGE) // 4 + 2


def block_sums(u):
    lane = iota(u[0][0].shape, 1)
    kept = (lane // EDGE % 4 == 0) & (lane % 4 == 0)
    out = None
    for part in range(2):
        for h in range(2):
            t = u[part][h]
            for step in (1, 2, EDGE, 2 * EDGE):
                t = t + lane_roll(t, -step)
            t = lane_roll(jnp.where(kept, t, 0.0), 2 * part + h)
            out = t if out is None else out + t
    return out


def second_body(own_ref, wave_ref, far_ref, before_ref, after_ref, mine_ref, field_ref, sums_ref, values_ref):
    _, s = position()
    first, last = s == 0, s == NS - 1
    u = rows_of(own_ref, 0)
    far_ref = far_ref.at[other()]
    factor = open_factor()
    v = [[x * factor for x in pair] for pair in rows_of(far_ref, 0)]
    one = field_of(mine_ref, 0)
    rights = rows_of(own_ref, 2)
    wave = wave_ref[...]
    far_wave = wave_rows(far_ref[4 * PATCHES : 4 * PATCHES + 1, :LANES])
    v_one = smooth(v, [[x + y for x, y in zip(in_plane(p), q)] for p, q in zip(v, u)], rows_of(far_ref, 2), far_wave)
    v_one = [[x * factor for x in pair] for pair in v_one]
    before = choose(first, v_one, field_of(before_ref, 0))
    after = choose(last, v_one, field_of(after_ref, 0))
    two = smooth(one, around(one, before, after), rights, wave)
    for part in range(2):
        put(field_ref, part, two[part])
    r = residual(two, [in_plane(two[0]), in_plane(two[1])], rights, wave)
    rows = jnp.concatenate([block_sums(r), block_sums(two)], 0)
    shape = (LANES, LANES)
    source = iota(shape, 0)
    half, base = source % 4, source - source % 4
    target = half // 2 * 64 + (half % 2 * 2 + base // 64 + 2) * 8 + base % EDGE // 4 + 2
    gather = jnp.where((base // EDGE % 4 == 0) & (target == iota(shape, 1)), 1.0, 0.0)
    sums = select_lanes(rows, gather)
    lane = iota((PATCHES, LANES), 1)
    values = sums[PATCHES:]
    beside = jnp.where((s % 4 == 0) | (s % 4 == 3), 1.0, 2.0)
    sums_ref[...] = jnp.where(lane == 0, wave, sums[:PATCHES] + beside * values)
    values_ref[...] = values


def join_body(sums_ref, values_ref, pair_ref, out_ref):
    out_ref[...] = sums_ref[...] + (pair_ref[...] + lane_roll(values_ref[...], 4))


def sides(x, patch, col):
    return (
        jnp.where(patch >= PZ, row_roll(x, PZ), 0.0),
        jnp.where(patch < PATCHES - PZ, row_roll(x, -PZ), 0.0),
        jnp.where(col > 0, row_roll(x, 1), 0.0),
        jnp.where(col < PZ - 1, row_roll(x, -1), 0.0),
    )


def windows(x):
    patch, lane = iota(x.shape, 0), iota(x.shape, 1)
    col = patch % PZ
    a, b = (lane // 8) % 8, lane % 8
    x = jnp.where((a >= 2) & (a < 6) & (b >= 2) & (b < 6), x, 0.0)
    _, _, low, high = sides(x, patch, col)
    x = x + jnp.where(b < 2, lane_roll(low, -4), 0.0) + jnp.where(b >= 6, lane_roll(high, 4), 0.0)
    low, high, _, _ = sides(x, patch, col)
    return x + jnp.where(a < 2, lane_roll(low, -32), 0.0) + jnp.where(a >= 6, lane_roll(high, 32), 0.0)


def slots_body(field_ref, own_wave_ref, slot_ref, out_ref, wave_ref, patch_ref):
    _, s = position()
    rows = [half for c in range(2) for half in halves(field_ref, c)]
    out_ref[...] = select(slot_ref[:, :PATCHES], jnp.concatenate(rows, 1))
    wave = own_wave_ref[...]
    patch, lane = iota(wave.shape, 0), iota(wave.shape, 1)
    col = patch % PZ
    a, b = (lane // 8) % 8, lane % 8
    _, _, low, high = sides(wave, patch, col)
    wave = jnp.where(b < 2, low, jnp.where(b >= 6, high, wave))
    low, high, _, _ = sides(wave, patch, col)
    wave = jnp.where(a < 2, low, jnp.where(a >= 6, high, wave))
    mine = slot_ref[pl.ds(SLOTS * device_at(s), SLOTS), :]
    wave_ref[...] = select(mine[:, :PATCHES], wave)
    index = iota(mine.shape, 1).astype(F32) + 1.0
    patch_ref[...] = jnp.broadcast_to(jnp.sum(mine * index, 1, keepdims=True) - 1.0, mine.shape)


def bundle_body(sent_ref, block_ref, far_ref, slot_ref, out_ref):
    _, s = position()
    factor = open_factor()
    far_ref = far_ref.at[other()]
    edge = jnp.where((s == 0) | (s == NS - 1), 1.0, 0.0)
    block, far_block = block_ref[...], far_ref[...]
    own = windows(block + (edge * factor) * lane_roll(far_block, -4))
    far = windows(factor * (far_block + edge * lane_roll(block, -4)))
    patch, lane = iota(far.shape, 0), iota(far.shape, 1)
    wave = jnp.broadcast_to(far_block[:, 0:1], far.shape)
    beside = (wave,) + sides(wave, patch, patch % PZ)
    for i, x in enumerate(beside):
        far = jnp.where(lane == i, x, far)
    placed = select(slot_ref[:, :PATCHES], jnp.concatenate([own, far], 1))
    for c in range(4):
        out_ref[pl.ds(c, LIVE, stride=6), :] = sent_ref[:, LANES * c : LANES * (c + 1)]
    for c in range(2):
        out_ref[pl.ds(4 + c, LIVE, stride=6), :] = placed[:, LANES * c : LANES * (c + 1)]


def coarse_sum(e):
    return (lane_roll(e, -1) + lane_roll(e, 1)) + (lane_roll(e, -8) + lane_roll(e, 8))


def correct_body(raw_ref, wave_ref, patch_ref, out_hbm, grown_ref, smooth_ref, sems):
    g, _ = position()
    odd = g % 2 == 1
    rows = 24
    shape = (SLOTS, LANES)

    def slot_rows(s, c):
        return raw_ref[pl.ds(rows * s + c, SLOTS, stride=6), :]

    def total(start, c):
        parts = [slot_rows(device_at(start + i), c) for i in range(4)]
        return ((parts[0] + parts[1]) + (parts[2] + parts[3])) * (1.0 / 64.0)

    lane = iota((LANES, LANES), 1)
    a, b = (lane // 8) % 8, lane % 8
    region = jnp.where(a < 2, 1, jnp.where(a >= 6, 2, jnp.where(b < 2, 3, jnp.where(b >= 6, 4, 0))))
    spread = jnp.where(iota((LANES, LANES), 0) == region, 1.0, 0.0)
    ends = jnp.concatenate([slot_rows(device_at(0), 5), slot_rows(device_at(NS - 1), 5)], 0)
    ends = select_lanes(ends, spread)
    low, high = ends[:SLOTS], ends[SLOTS:]
    own = wave_ref[...]
    wave = jnp.concatenate([low, low, own, own, own, own, high, high], 0)
    rhs = jnp.concatenate(
        [total(4, 5), total(0, 5)] + [total(4 * i, 4) for i in range(4)] + [total(12, 5), total(8, 5)], 0
    )
    lane = iota(shape, 1)
    a, b = (lane // 8) % 8, lane % 8
    patch = patch_ref[...].astype(jnp.int32)
    line, col = patch // PZ, patch % PZ
    y, z = 4 * line + a - 2, 4 * col + b - 2
    inside = jnp.where((y >= 0) & (y < 4 * PY) & (z >= 0) & (z < 4 * PZ), 1.0, 0.0)
    lower = jnp.where(low_side_open(g), inside, 0.0)
    inside = jnp.concatenate([lower, lower] + [inside] * 6, 0) > 0.0
    part_sign = jnp.where(iota(wave.shape, 1) < 64, -1.0, 1.0)
    real, imag = 6.0 / 16.0 - wave, shift_imag * wave
    scale = omega_coarse / (real * real + imag * imag)
    real, imag = real * scale, part_sign * imag * scale

    def divide(x):
        return jnp.where(inside, x * real + lane_roll(x, 64) * imag, 0.0)

    e = divide(rhs)
    for _ in range(2):
        beside = coarse_sum(e) + (row_roll(e, SLOTS) + row_roll(e, -SLOTS))
        e = (1.0 - omega_coarse) * e + divide(rhs + beside * (1.0 / 16.0))
    wide = (LANES, 2 * CELLS)
    widen = jnp.where(window_lane(wide, 1) == iota(wide, 0), 1.0, 0.0)
    grown_ref[...] = select_lanes(e[2 * SLOTS : 6 * SLOTS], widen)
    copies = []
    for q in range(SLOTS):
        held = jnp.broadcast_to(patch_ref[q : q + 1, 0:1] >= 0.0, (4, CELLS))
        for i in range(EDGE):
            s = device_at(jnp.where(odd, EDGE - 1 - i, i))
            for part in range(2):
                for h in range(2):
                    row = raw_ref[pl.ds(rows * s + 6 * q + 2 * part + h, 1), :]
                    smooth_ref[q, part, i : i + 1, LANES * h : LANES * (h + 1)] = row
        for i in range(4):
            plane = jnp.where(odd, 3 - i, i)
            line = grown_ref[pl.ds(SLOTS * plane + q, 1), :]
            for part in range(2):
                extra = jnp.broadcast_to(line[:, CELLS * part : CELLS * (part + 1)], (4, CELLS))
                value = smooth_ref[q, part, 4 * i : 4 * i + 4] + extra
                smooth_ref[q, part, 4 * i : 4 * i + 4] = jnp.where(held, value, 0.0)
        copies.append(pltpu.make_async_copy(smooth_ref.at[q], out_hbm.at[q], sems.at[q]))
        copies[q].start()
    for copy in copies:
        copy.wait()


def facing(groups, reach):
    pairs, met = [], set()
    for place in [i for i in range(NS) if i < reach or i >= NS - reach]:
        s = device_at(place)
        for g in range(0 if place >= NS // 2 else 1, groups - 1, 2):
            pairs.append([g * NS + s, (g + 1) * NS + s])
            met.update(pairs[-1])
    for g in range(groups):
        rest = [g * NS + s for s in range(NS) if g * NS + s not in met]
        whole = [i for i in rest if i ^ 1 in rest and 2 * reach < NS]
        rest = [i for i in rest if i not in whole]
        pairs += [whole[i : i + 2] for i in range(0, len(whole), 2)]
        pairs += [rest[i : i + 2] for i in range(0, len(rest), 2)]
    return pairs


def body(field, source, patch_of_slot, neighbour, wave_index, wave_table):
    groups = lax.axis_size("grp")
    both = ("grp", "sub")
    up = [(i, (i + 1) % NS) for i in range(NS)]
    down = [((i + 1) % NS, i) for i in range(NS)]
    ring = lambda x: (lax.ppermute(x, "sub", up), lax.ppermute(x, "sub", down))
    plane = (PATCHES, CELLS)

    hbm = pl.BlockSpec(memory_space=pltpu.HBM)
    (packed,) = call(
        pack_body,
        [(NS, 40, LANES)],
        [
            pltpu.with_memory_space_constraint(x, pltpu.HBM)
            for x in (field, source, patch_of_slot, wave_index, wave_table)
        ],
        [
            field.shape,
            source.shape,
            pltpu.SMEM(patch_of_slot.shape, jnp.int32),
            pltpu.SMEM(wave_index.shape, jnp.int32),
            pltpu.SMEM(wave_table.shape, F32),
            pltpu.SemaphoreType.DMA((5,)),
        ],
        [hbm] * 5,
        16,
    )
    raw = lax.all_to_all(packed, "sub", 0, 0, tiled=True).reshape(NS * 40, LANES)
    row = (PATCHES, LANES)
    stacked = (4 * PATCHES + 8, CELLS)
    own, start, slot, own_wave = call(place_body, [stacked, (2,) + plane, (LIVE, LANES), row], [raw])
    far = lax.all_gather(own, both, axis_index_groups=facing(groups, 2))
    before, after = ring(start)
    one, rising, falling = call(
        first_body, [(2,) + plane] * 3, [own, own_wave, before, after, far]
    )
    before = lax.ppermute(rising, "sub", up)
    after = lax.ppermute(falling, "sub", down)
    two, sums, values = call(
        second_body, [(2,) + plane, row, row], [own, own_wave, far, before, after, one]
    )
    edges = [device_at(4 * i + 3) for i in range(NS // 4 - 1)]
    pair = lax.ppermute(values, "sub", [(i, i + 1) for i in edges] + [(i + 1, i) for i in edges])
    mine = (SLOTS, LANES)
    sent, wave, patch = call(slots_body, [(LIVE, 2 * CELLS), mine, mine], [two, own_wave, slot])
    (block,) = call(join_body, [row], [sums, values, pair])
    far_block = lax.all_gather(block, both, axis_index_groups=facing(groups, NS // 2))
    (bundle,) = call(bundle_body, [(LIVE * 6, LANES)], [sent, block, far_block, slot])
    back = lax.all_to_all(bundle.reshape(NS, 24, LANES), "sub", 0, 0, tiled=True)
    (out,) = call(
        correct_body,
        [(SLOTS, 2, EDGE, CELLS)],
        [back.reshape(NS * 24, LANES), wave, patch],
        [(EDGE, 2 * CELLS), (SLOTS, 2, EDGE, CELLS), pltpu.SemaphoreType.DMA((SLOTS,))],
        to=hbm,
    )
    return out


def solution(mesh):
    return jax.shard_map(
        body,
        mesh=mesh,
        in_specs=(
            P(("grp", "sub"), None, None, None),
            P(("grp", "sub"), None, None, None),
            P(("grp", "sub")),
            P(("grp", "sub"), None),
            P(("grp", "sub")),
            P(),
        ),
        out_specs=P(("grp", "sub"), None, None, None),
        check_vma=False,
    )
```
